512 devices in a mesh: doc: 16 (over y_hi, x, core), seq: 32 (over z, y_lo).
Axes of the slice: x: 4, y: 4 (y_hi: 2, y_lo: 2; y = y_hi * 2 + y_lo), z: 16, core: 2. Of those that a mesh axis runs over, the one named last changes fastest.
Arguments:
- queries: bfloat16 [16, 4096, 1024], P('doc', 'seq'), may hold values from -7 to 7
- key_rows: bfloat16 [16, 4096, 1024], P('doc', 'seq'), may hold values from -7 to 7
- value_rows: bfloat16 [16, 4096, 1024], P('doc', 'seq'), may hold values from -5 to 5
- cotangent: bfloat16 [16, 4096, 1024], P('doc', 'seq'), may hold values from -3 to 3
- out_weight: bfloat16 [1024, 1024], P('doc'), may hold values from -0.1875 to 0.1875
- lengths: int32 [16, 4], P('doc'), may hold values from 1 to 32, 64 in all within a row
- upweight: int32 [16, 4], P('doc'), may hold values from 1 to 6, as said below
Outputs:
- layer_out: bfloat16 [16, 4096, 1024], P('doc', 'seq')
- grad_query: bfloat16 [16, 4096, 1024], P('doc', 'seq')
- grad_key: bfloat16 [16, 4096, 1024], P('doc', 'seq')
- grad_value: bfloat16 [16, 4096, 1024], P('doc', 'seq')
- grad_weight: float32 [1024, 1024], P('doc')
The draws below stay inside these ranges and needn't reach their ends.
Inputs may be any that keep to these rules, and one draw needn't show every extreme that they name: Each sequence's documents fill it exactly: the lengths add up to 64, and the longest is 32. `upweight`: each entry is 1 or 6; every sequence has a document with factor 6.
All inputs are finite; a program needn't handle non-finite values.
Results may differ from the reference program's by a relative error of at most 0.0089.
Values may be sent and summed in bfloat16 or wider, within the bound.
A program may use at most 128 MiB of HBM per device.

```python
import math
import jax
import jax.numpy as jnp
import numpy as np
from jax import lax

HEADS = 16
HEAD_DIM = 64
D = 1024
WINDOW = 512
TOK_DEV = 128
BLOCK = 64
DOCS = 4
LAMBDA = 6
SEQS = 16
SEQ_LEN = 4096
MOST_BLOCKS = 32


def paired_draw(key):
    paired_seed = jax.random.fold_in(key, 9173)
    query_seed, key_seed = jax.random.split(paired_seed, 2)
    full_shape = (SEQS, SEQ_LEN, HEADS * HEAD_DIM)
    query_draw = jnp.clip(jax.random.normal(query_seed, full_shape, jnp.float32), -3.5, 3.5) * 1.6
    key_draw = jnp.clip(jax.random.normal(key_seed, full_shape, jnp.float32), -3.5, 3.5) * 1.6
    return (query_draw, key_draw)


def draw_queries(key, part):
    return paired_draw(key)[0].astype(jnp.bfloat16)


def draw_key_rows(key, part):
    return paired_draw(key)[1].astype(jnp.bfloat16)


def draw_upweight(key, part):
    pick_seed, forced_seed = jax.random.split(jax.random.fold_in(key, 4242))
    chosen = jax.random.randint(pick_seed, (SEQS, DOCS), 0, 3)
    forced_doc = jax.random.randint(forced_seed, (SEQS, 1), 0, DOCS)
    marked = (chosen == 0) | (jnp.arange(DOCS)[None, :] == forced_doc)
    return jnp.where(marked, LAMBDA, 1).astype(jnp.int32)


def level_of(own_key, extent, cuts, low, largest):
    factor_of = 1.0
    for position, shards_of in cuts:
        steps = jax.random.uniform(jax.random.fold_in(jax.random.fold_in(own_key, 6), position), (shards_of,), jnp.float32, low / len(cuts), largest / len(cuts))
        factor_of = factor_of * jnp.repeat(jnp.exp(steps), extent[position] // shards_of).reshape((-1,) + (1,) * (len(extent) - 1 - position))
    return factor_of


def length_profile(count, total, bound, skew):
    portions = [(1 << 20) // math.isqrt(grade ** skew) + 1 for grade in range(2, count + 1)]
    surplus, holding = total - bound - (count - 1), [1] * (count - 1)
    while surplus > 0:
        movable = [i for i in range(count - 1) if holding[i] < bound]
        pool, budget = sum([portions[i] for i in movable]), surplus
        for i in movable:
            more = min(bound - holding[i], max(1, budget * portions[i] // pool), surplus)
            holding[i] = holding[i] + more
            surplus = surplus - more
    return np.array([bound] + holding)


def uneven(stream_key, amount, total, limit, skew):
    if amount == 2:
        one = jax.random.randint(stream_key, (), max(1, total - limit), min(limit, total - 1) + 1)
        return jnp.stack([one, total - one])
    tallies = jnp.asarray(length_profile(amount, total, limit, skew), jnp.int32)
    twos = (amount - 1) // 2
    source_of, taker = tallies[1:1 + 2 * twos:2], tallies[2:2 + 2 * twos:2]
    room = jnp.minimum(source_of - 1, limit - taker)
    moved = jax.random.randint(jax.random.fold_in(stream_key, 1), (twos,), 0, 1 << 20) % (room + 1)
    tallies = tallies.at[1:1 + 2 * twos:2].set(source_of - moved).at[2:2 + 2 * twos:2].set(taker + moved)
    return tallies[jax.random.permutation(jax.random.fold_in(stream_key, 2), amount)]


def bell_draw(key, dims, scale, bound, pieces=(), kind=jnp.bfloat16):
    result = jax.random.normal(key, dims, jnp.float32) * scale
    if len(pieces) > 0:
        result = level_of(key, dims, pieces, -0.22, 0.18) * result
    return jnp.clip(result, min=-bound, max=bound).astype(kind)


def setup_inputs(seed: int = 0) -> dict:
    splits = jax.random.split(jax.random.key(seed), 8)
    return {
        "queries": draw_queries(jax.random.fold_in(splits[7], 71), 0),
        "key_rows": draw_key_rows(jax.random.fold_in(splits[7], 71), 0),
        "value_rows": bell_draw(splits[2], (SEQS, SEQ_LEN, D), 1.0, 5.0, ((0, 16), (1, 32))),
        "cotangent": bell_draw(splits[3], (SEQS, SEQ_LEN, D), 0.5, 3.0, ((0, 16), (1, 32))),
        "out_weight": bell_draw(splits[4], (D, D), D ** -0.5, 0.1875, ((0, 16),)),
        "lengths": jax.vmap(lambda own: uneven(own, DOCS, SEQ_LEN // BLOCK, MOST_BLOCKS, 2))(jax.random.split(splits[5], SEQS)).reshape((SEQS, DOCS)).astype(jnp.int32),
        "upweight": draw_upweight(jax.random.fold_in(splits[7], 71), 0),
    }


def document_ids(lengths_row, positions):
    bounds = (jnp.cumsum(lengths_row) * BLOCK).astype(jnp.int32)
    return lax.optimization_barrier(jnp.sum((positions[:, None] >= bounds[None, :]).astype(jnp.int32), axis=1)).astype(jnp.int32)

def band_mask(query_pos, key_pos, query_doc, key_doc, seq_len):
    near_band = jnp.abs(query_pos[:, None] - key_pos[None, :]) <= WINDOW
    inside = (key_pos >= 0) & (key_pos < seq_len)
    return near_band & inside[None, :] & (query_doc[:, None] == key_doc[None, :])

def soft_weights(query_blk, key_blk, allowed):
    scores = jnp.einsum('qhd,khd->hqk', query_blk.astype(jnp.float32), key_blk.astype(jnp.float32)) * HEAD_DIM ** (-0.5)
    scores = jnp.where(allowed[None], scores, -jnp.inf)
    row_peak = lax.optimization_barrier(jnp.max(scores, axis=2, keepdims=True))
    exponent = jnp.exp(scores - row_peak)
    return exponent / lax.optimization_barrier(jnp.sum(exponent, axis=2, keepdims=True))

def settle(values):
    return lax.optimization_barrier(values.astype(jnp.bfloat16)).astype(jnp.float32)

def reference(queries, key_rows, value_rows, cotangent, out_weight, lengths, upweight):
    model_width = HEADS * HEAD_DIM
    key_span = TOK_DEV + 2 * WINDOW
    block_count = SEQ_LEN // TOK_DEV
    score_scale = HEAD_DIM ** (-0.5)
    offsets = jnp.arange(TOK_DEV, dtype=jnp.int32)
    key_offsets = jnp.arange(key_span, dtype=jnp.int32)
    foreign = (key_offsets < WINDOW) | (key_offsets >= WINDOW + TOK_DEV)

    def sequence_pass(sequence_items):
        seq_query, seq_key, seq_value, seq_cot, lengths_row, upweight_row = sequence_items
        key_pad = jnp.pad(seq_key, ((WINDOW, WINDOW), (0, 0)))
        value_pad = jnp.pad(seq_value, ((WINDOW, WINDOW), (0, 0)))
        positions = jnp.arange(SEQ_LEN, dtype=jnp.int32)
        token_doc = document_ids(lengths_row, positions)
        matches = token_doc[:, None] == jnp.arange(DOCS, dtype=jnp.int32)[None, :]
        token_weight = lax.optimization_barrier(jnp.sum(jnp.where(matches, upweight_row[None, :], 0), axis=1)).astype(jnp.float32)

        def block_pieces(block_index):
            row_start = (block_index * TOK_DEV).astype(jnp.int32)
            query_blk = lax.dynamic_slice_in_dim(seq_query, row_start, TOK_DEV, 0).reshape(TOK_DEV, HEADS, HEAD_DIM)
            key_blk = lax.dynamic_slice_in_dim(key_pad, row_start, key_span, 0).reshape(key_span, HEADS, HEAD_DIM)
            value_blk = lax.dynamic_slice_in_dim(value_pad, row_start, key_span, 0).reshape(key_span, HEADS, HEAD_DIM)
            query_pos = row_start + offsets
            key_pos = row_start - WINDOW + key_offsets
            allowed = band_mask(query_pos, key_pos, document_ids(lengths_row, query_pos), document_ids(lengths_row, key_pos), SEQ_LEN)
            return (row_start, query_blk, key_blk, value_blk, allowed)

        def forward_block(block_index):
            row_start, query_blk, key_blk, value_blk, allowed = block_pieces(block_index)
            prob_half = soft_weights(query_blk, key_blk, allowed).astype(jnp.bfloat16)
            mixed_rows = jnp.einsum('hqk,khd->qhd', prob_half.astype(jnp.float32), value_blk.astype(jnp.float32))
            return mixed_rows.reshape(TOK_DEV, model_width).astype(jnp.bfloat16)
        attended = lax.map(forward_block, jnp.arange(block_count, dtype=jnp.int32)).reshape(SEQ_LEN, model_width)
        layer_out = jnp.dot(attended, out_weight, preferred_element_type=jnp.float32).astype(jnp.bfloat16)
        grad_out = (token_weight[:, None] * seq_cot.astype(jnp.float32)).astype(jnp.bfloat16)
        weight_part = jnp.dot(attended.T, grad_out, preferred_element_type=jnp.float32)
        grad_attended = jnp.dot(grad_out, out_weight.T, preferred_element_type=jnp.float32).astype(jnp.bfloat16)

        def backward_block(grad_sums, block_index):
            key_sum, value_sum = grad_sums
            row_start, query_blk, key_blk, value_blk, allowed = block_pieces(block_index)
            prob_full = soft_weights(query_blk, key_blk, allowed)
            prob_half = prob_full.astype(jnp.bfloat16)
            grad_blk = lax.dynamic_slice_in_dim(grad_attended, row_start, TOK_DEV, 0).reshape(TOK_DEV, HEADS, HEAD_DIM)
            grad_prob = jnp.einsum('qhd,khd->hqk', grad_blk.astype(jnp.float32), value_blk.astype(jnp.float32))
            centre = lax.optimization_barrier(jnp.sum(prob_full * grad_prob, axis=2, keepdims=True))
            grad_score = (prob_full * (grad_prob - centre) * score_scale).astype(jnp.bfloat16)
            grad_query_blk = jnp.einsum('hqk,khd->qhd', grad_score.astype(jnp.float32), key_blk.astype(jnp.float32))
            grad_query_blk = grad_query_blk.reshape(TOK_DEV, model_width).astype(jnp.bfloat16)
            key_part = jnp.einsum('hqk,qhd->khd', grad_score.astype(jnp.float32), query_blk.astype(jnp.float32))
            value_part = jnp.einsum('hqk,qhd->khd', prob_half.astype(jnp.float32), grad_blk.astype(jnp.float32))
            key_part = key_part.reshape(key_span, model_width)
            value_part = value_part.reshape(key_span, model_width)
            key_part = jnp.where(foreign[:, None], settle(key_part), key_part)
            value_part = jnp.where(foreign[:, None], settle(value_part), value_part)
            key_sum = lax.dynamic_update_slice_in_dim(key_sum, lax.dynamic_slice_in_dim(key_sum, row_start, key_span, 0) + key_part, row_start, 0)
            value_sum = lax.dynamic_update_slice_in_dim(value_sum, lax.dynamic_slice_in_dim(value_sum, row_start, key_span, 0) + value_part, row_start, 0)
            return ((key_sum, value_sum), grad_query_blk)
        zero_pad = jnp.zeros((SEQ_LEN + 2 * WINDOW, model_width), jnp.float32)
        (key_sum, value_sum), grad_query = lax.scan(backward_block, (zero_pad, zero_pad), jnp.arange(block_count, dtype=jnp.int32))
        grad_key = key_sum[WINDOW:WINDOW + SEQ_LEN].astype(jnp.bfloat16)
        grad_value = value_sum[WINDOW:WINDOW + SEQ_LEN].astype(jnp.bfloat16)
        return (layer_out, grad_query.reshape(SEQ_LEN, model_width), grad_key, grad_value, weight_part)
    results = lax.map(sequence_pass, (queries, key_rows, value_rows, cotangent, lengths, upweight))
    layer_out, grad_query, grad_key, grad_value, weight_parts = results
    grad_weight = lax.optimization_barrier(jnp.sum(weight_parts, axis=0)) * (1.0 / math.sqrt(SEQS * SEQ_LEN))
    return (layer_out, grad_query, grad_key, grad_value, grad_weight)
```

```python
import math

import jax
import jax.numpy as jnp
from jax import lax
from jax.experimental import pallas as pl
from jax.experimental.pallas import tpu as pltpu
from jax.sharding import PartitionSpec as P

HEAD_DIM = 64
WINDOW = 512
BLOCK = 64
DOCS = 4
ROWS = 128
LANES = 128
SPAN = 9
SLOTS = 10
STEPS = 4
WIDTH = 1024
Z = 16
OFFSETS = (-2, -1, 1, 2)
MESH = pl.DeviceIdType.MESH
BF16 = jnp.bfloat16
F32 = jnp.float32

NT = (((1,), (1,)), ((), ()))
TN = (((0,), (0,)), ((), ()))


def dot(a, b, dims=(((1,), (0,)), ((), ()))):
    return lax.dot_general(a, b, dims, preferred_element_type=F32)


def remote(src, dst, send, recv, device):
    return pltpu.make_async_remote_copy(
        src_ref=src, dst_ref=dst, send_sem=send, recv_sem=recv, device_id=device, device_id_type=MESH
    )


def layer_kernel(
    lengths, upweight, q_in, k_in, v_in, ct_in, w_in,
    lo_out, dq_out, dk_out, dv_out, gw_out,
    qbuf, kv, ctb, gout, wbuf, bias, attbuf, attpair, dqb, acc, own, rout, rin, fin,
    gkeep, g1send, g1recv, g2send, g2recv, g2sum, g3send, g3recv, g4f, g4send, g4recv,
    zag, gwh, gwo, lob, s_scr, dp_scr, p_scr, ds_scr,
    l_sem, y_send, y_recv, ct_send, ct_recv, z_send, z_recv, wx_send, wx_recv, wc_send, wc_recv,
    wy_send, wy_recv, r_send, r_recv, a_send, a_recv, dq_send, dq_recv, f_send, f_recv, o_sem,
    g1_send, g1_rsem, g2_send, g2_rsem, g3_send, g3_rsem, g4_send, g4_rsem, g5_send, g5_rsem,
    g6_send, g6_rsem,
):
    d = lax.axis_index("doc")
    s = lax.axis_index("seq")
    z, y = s // 2, s % 2
    yh, x, core = d // 8, (d // 2) % 4, d % 2
    s_pair = z * 2 + (1 - y)
    d_core = yh * 8 + x * 2 + (1 - core)
    d_far = (1 - yh) * 8 + x * 2 + core

    def at_x(offset):
        return yh * 8 + ((x + offset + 4) % 4) * 2 + core

    def at_z(offset):
        return ((z + offset + Z) % Z) * 2 + y

    def pair_of(step):
        return (x + 3 - step) % 4

    def cols(column, step):
        return pl.ds(pl.multiple_of((column * 4 + pair_of(step)) * LANES, LANES), LANES)

    pair_dev = (d, s_pair)
    core_dev = (d_core, s)
    far_dev = (d_far, s_pair)

    barrier = pltpu.get_barrier_semaphore()
    partners = [pair_dev, core_dev, far_dev, (d_far, s)] + [(at_x(o), s) for o in (1, 2, 3)]
    for device in partners:
        pl.semaphore_signal(barrier, inc=1, device_id=device, device_id_type=MESH)

    def greet(o, carry):
        pl.semaphore_signal(barrier, inc=1, device_id=(d, at_z(o)), device_id_type=MESH)
        return carry

    lax.fori_loop(1, Z, greet, 0)
    pl.semaphore_wait(barrier, len(partners) + Z - 1)

    def own_copies(i):
        mine = cols(y, i)
        return [
            pltpu.make_async_copy(k_in.at[:, mine], kv.at[i, 4 + y, 0], l_sem.at[i, 0]),
            pltpu.make_async_copy(v_in.at[:, mine], kv.at[i, 4 + y, 1], l_sem.at[i, 1]),
            pltpu.make_async_copy(q_in.at[:, mine], qbuf.at[i, y], l_sem.at[i, 2]),
        ]

    def pair_copies(i):
        theirs = cols(1 - y, i)
        return [
            remote(k_in.at[:, theirs], kv.at[i, 4 + y, 0], y_send.at[i, 0], y_recv.at[i, 0], pair_dev),
            remote(v_in.at[:, theirs], kv.at[i, 4 + y, 1], y_send.at[i, 1], y_recv.at[i, 1], pair_dev),
            remote(q_in.at[:, theirs], qbuf.at[i, y], y_send.at[i, 2], y_recv.at[i, 2], pair_dev),
        ]

    def pair_arrivals(i):
        there = 5 - y
        return [
            remote(kv.at[i, there, 0], kv.at[i, there, 0], y_send.at[i, 0], y_recv.at[i, 0], pair_dev),
            remote(kv.at[i, there, 1], kv.at[i, there, 1], y_send.at[i, 1], y_recv.at[i, 1], pair_dev),
            remote(qbuf.at[i, 1 - y], qbuf.at[i, 1 - y], y_send.at[i, 2], y_recv.at[i, 2], pair_dev),
        ]

    def halo_copy(i, n):
        o = OFFSETS[n]
        return remote(
            kv.at[i, pl.ds(4, 2)], kv.at[i, pl.ds(4 - 2 * o, 2)], z_send.at[i, n], z_recv.at[i, n], (d, at_z(o))
        )

    def halo_arrival(i, n):
        o = OFFSETS[n]
        here = kv.at[i, pl.ds(4 - 2 * o, 2)]
        return remote(here, here, z_send.at[i, n], z_recv.at[i, n], (d, at_z(o)))

    own_ct = pltpu.make_async_copy(ct_in, ctb.at[y], l_sem.at[0, 3])
    own_w = pltpu.make_async_copy(w_in, wbuf.at[d], l_sem.at[1, 3])
    send_ct = remote(ct_in, ctb.at[y], ct_send, ct_recv, pair_dev)
    take_ct = remote(ctb.at[1 - y], ctb.at[1 - y], ct_send, ct_recv, pair_dev)

    for i in range(STEPS):
        for copy in own_copies(i)[:2]:
            copy.start()
        for copy in pair_copies(i)[:2]:
            copy.start()
    own_w.start()
    for o in (1, 2, 3):
        remote(w_in, wbuf.at[d], wx_send.at[o - 1], wx_recv.at[o - 1], (at_x(o), s)).start()
    for i in range(STEPS):
        own_copies(i)[2].start()
        pair_copies(i)[2].start()
    own_ct.start()
    send_ct.start()

    bounds = []
    total = jnp.int32(0)
    for j in range(DOCS):
        total = total + lengths[0, j] * BLOCK
        bounds.append(total)

    def doc_of(position):
        ids = jnp.zeros_like(position)
        for bound in bounds:
            ids = ids + (position >= bound).astype(jnp.int32)
        return ids

    for yp in range(2):
        base = (z * 2 + yp) * ROWS

        def fill(j, carry, yp=yp, base=base):
            rows = lax.broadcasted_iota(jnp.int32, (ROWS, ROWS), 0)
            lanes = lax.broadcasted_iota(jnp.int32, (ROWS, ROWS), 1)
            key = base - WINDOW + j * ROWS + rows
            query = base + lanes
            near = jnp.abs(query - key) <= WINDOW
            inside = (key >= 0) & (key < Z * 2 * ROWS)
            ok = near & inside & (doc_of(key) == doc_of(query))
            bias[yp, j] = jnp.where(ok, 0.0, -jnp.inf).astype(F32)
            return carry

        lax.fori_loop(0, SPAN, fill, 0)

    def pump(i, carry):
        for copy in own_copies(i)[:2]:
            copy.wait()
        for copy in pair_arrivals(i)[:2]:
            copy.wait_recv()
        for n in range(4):
            halo_copy(i, n).start()
        return carry

    lax.fori_loop(0, STEPS, pump, 0)

    def w_block(high, o):
        return wbuf.at[high * 8 + ((x - o + 4) % 4) * 2 + core]

    own_w.wait()
    for o in range(4):
        block = w_block(yh, o)
        if o:
            remote(block, block, wx_send.at[o - 1], wx_recv.at[o - 1], (at_x(-o), s)).wait_recv()
        remote(block, block, wy_send.at[o], wy_recv.at[o], far_dev).start()
        remote(block, block, wc_send.at[o], wc_recv.at[o], core_dev).start()

    own_ct.wait()
    take_ct.wait_recv()
    for yp in range(2):
        position = (z * 2 + yp) * ROWS + lax.broadcasted_iota(jnp.int32, (ROWS, LANES), 0)
        ids = doc_of(position)
        weight = jnp.zeros((ROWS, LANES), jnp.int32)
        for j in range(DOCS):
            weight = weight + jnp.where(ids == j, upweight[0, j], 0)
        weight = weight.astype(F32)
        for j in range(WIDTH // LANES):
            piece = slice(j * LANES, (j + 1) * LANES)
            gout[yp, :, piece] = (weight * ctb[yp, :, piece].astype(F32)).astype(BF16)

    for o in range(4):
        block = w_block(1 - yh, o)
        remote(block, block, wy_send.at[o], wy_recv.at[o], far_dev).wait_recv()
        remote(block, block, wc_send.at[4 + o], wc_recv.at[4 + o], core_dev).start()
    for o in range(4):
        for h, high in ((0, yh), (1, 1 - yh)):
            block = wbuf.at[high * 8 + ((x - o + 4) % 4) * 2 + (1 - core)]
            remote(block, block, wc_send.at[4 * h + o], wc_recv.at[4 * h + o], core_dev).wait_recv()

    for i in range(STEPS):
        own_copies(i)[2].wait()
        pair_arrivals(i)[2].wait_recv()

    lane = lax.broadcasted_iota(jnp.int32, (ROWS, LANES), 1)

    def stacked(block):
        block = block.astype(F32)
        low = jnp.where(lane < HEAD_DIM, block, 0.0).astype(BF16)
        high = jnp.where(lane >= HEAD_DIM, block, 0.0).astype(BF16)
        return jnp.concatenate([low, high], axis=0)

    def unstacked(block):
        return jnp.concatenate([block[:HEAD_DIM, :ROWS], block[HEAD_DIM:, ROWS:]], axis=0)

    def key_block(j):
        return slice(j * ROWS, (j + 1) * ROWS)

    def unit(i, yp, w_pair):
        query2 = stacked(qbuf[i, yp])
        grad2 = stacked(dot(gout[yp], w_pair, NT).astype(BF16))
        peak = jnp.full((8, 2 * ROWS), -jnp.inf, F32)
        for j in range(SPAN):
            mask = bias[yp, j]
            score = dot(kv[i, yp + j, 0], query2, NT) + jnp.concatenate([mask, mask], axis=1)
            s_scr[key_block(j)] = score
            peak = jnp.maximum(peak, jnp.max(score.reshape(ROWS // 8, 8, 2 * ROWS), axis=0))
        peak = jnp.max(peak, axis=0, keepdims=True)
        norm = jnp.zeros((8, 2 * ROWS), F32)
        centre = jnp.zeros((8, 2 * ROWS), F32)
        for j in range(SPAN):
            power = jnp.exp((s_scr[key_block(j)] - peak) * (HEAD_DIM ** -0.5))
            slope = dot(kv[i, yp + j, 1], grad2, NT)
            s_scr[key_block(j)] = power
            dp_scr[key_block(j)] = slope
            norm = norm + jnp.sum(power.reshape(ROWS // 8, 8, 2 * ROWS), axis=0)
            centre = centre + jnp.sum((power * slope).reshape(ROWS // 8, 8, 2 * ROWS), axis=0)
        share = 1.0 / jnp.sum(norm, axis=0, keepdims=True)
        centre = jnp.sum(centre, axis=0, keepdims=True) * share
        for j in range(SPAN):
            prob = s_scr[key_block(j)] * share
            half = prob.astype(BF16)
            grad_score = (prob * (dp_scr[key_block(j)] - centre) * (HEAD_DIM ** -0.5)).astype(BF16)
            p_scr[key_block(j)] = half
            ds_scr[key_block(j)] = grad_score
            key_part = dot(grad_score, query2)
            value_part = dot(half, grad2)
            if yp == 0:
                acc[j, 0] = key_part
                acc[j, 1] = value_part
            elif j + 1 < SPAN:
                acc[j + 1, 0] += key_part
                acc[j + 1, 1] += value_part
            else:
                acc[j + 1, 0] = key_part
                acc[j + 1, 1] = value_part
        keys = kv[i, yp:yp + SPAN, 0].reshape(SPAN * ROWS, LANES)
        values = kv[i, yp:yp + SPAN, 1].reshape(SPAN * ROWS, LANES)
        mixed = unstacked(dot(values, p_scr[...], TN))
        attpair[i, yp] = mixed.T.astype(BF16)
        dqb[i, yp] = unstacked(dot(keys, ds_scr[...], TN)).T.astype(BF16)
        return dot(mixed.astype(BF16), gout[yp])

    def att_send(i):
        return remote(
            attpair.at[i, 1 - y], attbuf.at[y * 4 + pair_of(i)], a_send.at[i], a_recv.at[i], pair_dev
        )

    def att_take(i):
        here = attbuf.at[(1 - y) * 4 + pair_of(i)]
        return remote(here, here, a_send.at[i], a_recv.at[i], pair_dev)

    def dq_own(i):
        return pltpu.make_async_copy(dqb.at[i, y], dq_out.at[:, cols(y, i)], o_sem.at[i, 0])

    def dq_pair(i):
        return remote(dqb.at[i, 1 - y], dq_out.at[:, cols(y, i)], dq_send.at[i], dq_recv.at[i], pair_dev)

    def dq_take(i):
        here = dq_out.at[:, cols(1 - y, i)]
        return remote(here, here, dq_send.at[i], dq_recv.at[i], pair_dev)

    def ret_copy(i, n):
        return remote(rout.at[i, n], rin.at[i, n], r_send.at[i, n], r_recv.at[i, n], (d, at_z(OFFSETS[n])))

    def g1_copy(i):
        return remote(g1send.at[i], g1recv.at[i], g1_send.at[i], g1_rsem.at[i], core_dev)

    def g2_copy(i):
        return remote(g2send.at[i], g2recv.at[i], g2_send.at[i], g2_rsem.at[i], (at_x(-1 - i), s))

    def g2_start(i):
        g1_copy(i).wait_recv()
        g2send[i] = (gkeep[i, core] + g1recv[i].astype(F32)).astype(BF16)
        g2_copy(i).start()

    def step(i, carry):
        for n in range(4):
            halo_arrival(i, n).wait_recv()
        doc_row = y * 8 + pair_of(i) * 2
        w_pair = wbuf[pl.ds(doc_row, 2)].reshape(2 * HEAD_DIM, WIDTH)
        weight_part = unit(i, 0, w_pair)
        weight_part = weight_part + unit(i, 1, w_pair)
        att_send(i).start()
        dq_own(i).start()
        dq_pair(i).start()
        attbuf[y * 4 + pair_of(i)] = attpair[i, y]
        for n in range(4):
            first = 4 + 2 * OFFSETS[n]
            rout[i, n] = acc[first:first + 2].astype(BF16)
            ret_copy(i, n).start()
        own[i] = acc[4:6]
        gkeep[i, 0] = weight_part[:HEAD_DIM]
        gkeep[i, 1] = weight_part[HEAD_DIM:]
        g1send[i] = gkeep[i, 1 - core].astype(BF16)
        g1_copy(i).start()

        @pl.when(i > 0)
        def _():
            g2_start(i - 1)

        return carry

    lax.fori_loop(0, STEPS, step, 0)

    g1_copy(3).wait_recv()
    head = gkeep[3, core] + g1recv[3].astype(F32)
    for i in range(3):
        remote(g2recv.at[i], g2recv.at[i], g2_send.at[i], g2_rsem.at[i], (at_x(1 + i), s)).wait_recv()
        head = head + g2recv[i].astype(F32)
    for j in range(8):
        g2sum[j] = head[:, j * LANES:(j + 1) * LANES]
    g3send[...] = g2sum[pl.ds((1 - yh) * 4, 4)].astype(BF16)
    g3 = remote(g3send, g3recv, g3_send, g3_rsem, (d_far, s))
    g3.start()

    def fin_own(i):
        return [
            pltpu.make_async_copy(fin.at[i, y, n], out.at[:, cols(y, i)], o_sem.at[i, 1 + n])
            for n, out in ((0, dk_out), (1, dv_out))
        ]

    def fin_pair(i):
        return [
            remote(fin.at[i, 1 - y, n], out.at[:, cols(y, i)], f_send.at[i, n], f_recv.at[i, n], pair_dev)
            for n, out in ((0, dk_out), (1, dv_out))
        ]

    def fin_take(i):
        views = [out.at[:, cols(1 - y, i)] for out in (dk_out, dv_out)]
        return [remote(views[n], views[n], f_send.at[i, n], f_recv.at[i, n], pair_dev) for n in range(2)]

    def finish(i):
        total = own[i]
        for n in range(4):
            ret_copy(i, n).wait_recv()
            total = total + rin[i, n].astype(F32)
        fin[i] = total.astype(BF16)
        for copy in fin_pair(i) + fin_own(i):
            copy.start()

    def finish_step(i, carry):
        finish(i)
        return carry

    lax.fori_loop(0, 2, finish_step, 0)

    g3.wait_recv()
    half_sum = g2sum[pl.ds(yh * 4, 4)] + g3recv[...].astype(F32)
    g4f[...] = half_sum.reshape(Z, 16, LANES)
    g4send[...] = g4f[...].astype(BF16)

    def g4_copy(o):
        return remote(
            g4send.at[(z + o) % Z], g4recv.at[o], g4_send.at[o], g4_rsem.at[o], (d, at_z(o))
        )

    def g4_start(o, carry):
        g4_copy(o).start()
        return carry

    lax.fori_loop(1, Z, g4_start, 0)

    for i in range(STEPS):
        att_take(i).wait_recv()
    rows = jnp.concatenate([attbuf[j] for j in range(8)], axis=1)
    for j in range(4):
        piece = slice(j * 256, (j + 1) * 256)
        lob[:, piece] = dot(rows, wbuf[:, :, piece].reshape(WIDTH, 256)).astype(BF16)
    lo_copy = pltpu.make_async_copy(lob, lo_out, o_sem.at[0, 3])
    lo_copy.start()

    def g4_wait(o, total):
        g4_copy(o).wait_recv()
        return total + g4recv[o].astype(F32)

    piece_sum = lax.fori_loop(1, Z, g4_wait, g4f[z])
    zag[z] = piece_sum * (1.0 / math.sqrt(Z * 2 * ROWS * 16))

    def g5_copy(o):
        return remote(zag.at[z], zag.at[z], g5_send.at[o], g5_rsem.at[o], (d, at_z(o)))

    def g5_take(o):
        here = zag.at[(z - o + Z) % Z]
        return remote(here, here, g5_send.at[o], g5_rsem.at[o], (d, at_z(o)))

    def g5_start(o, carry):
        g5_copy(o).start()
        return carry

    lax.fori_loop(1, Z, g5_start, 0)
    lax.fori_loop(2, STEPS, finish_step, 0)

    def g5_wait(o, carry):
        g5_take(o).wait_recv()
        return carry

    lax.fori_loop(1, Z, g5_wait, 0)

    def g6_copy(n, device):
        return remote(zag, gwh.at[yh], g6_send.at[n], g6_rsem.at[yh], device)

    def g6_take(part):
        return remote(gwh.at[part], gwh.at[part], g6_send.at[0], g6_rsem.at[part], pair_dev)

    @pl.when(yh == y)
    def _():
        g6_copy(0, pair_dev).start()
        gwh[yh] = zag[...]
        g6_take(1 - yh).wait_recv()
        g6_copy(0, pair_dev).wait_send()

    @pl.when(yh != y)
    def _():
        g6_copy(0, far_dev).start()
        g6_copy(1, (d_far, s)).start()
        g6_take(0).wait_recv()
        g6_take(1).wait_recv()
        g6_copy(0, far_dev).wait_send()
        g6_copy(1, (d_far, s)).wait_send()

    for part in range(2):
        for j in range(4):
            lanes = slice((part * 4 + j) * LANES, (part * 4 + j + 1) * LANES)
            gwo[:, lanes] = gwh[part, 4 * j:4 * j + 4].reshape(HEAD_DIM, LANES)
    gw_copy = pltpu.make_async_copy(gwo, gw_out, o_sem.at[1, 3])
    gw_copy.start()

    def drain(i, carry):
        for copy in pair_copies(i):
            copy.wait_send()
        for n in range(4):
            halo_copy(i, n).wait_send()
            ret_copy(i, n).wait_send()
        att_send(i).wait_send()
        dq_own(i).wait()
        dq_pair(i).wait_send()
        dq_take(i).wait_recv()
        g1_copy(i).wait_send()
        for copy in fin_own(i):
            copy.wait()
        for copy in fin_pair(i):
            copy.wait_send()
        for copy in fin_take(i):
            copy.wait_recv()
        return carry

    lax.fori_loop(0, STEPS, drain, 0)
    send_ct.wait_send()
    for o in (1, 2, 3):
        remote(w_in, wbuf.at[d], wx_send.at[o - 1], wx_recv.at[o - 1], (at_x(o), s)).wait_send()
        g2_copy(o - 1).wait_send()
    for o in range(4):
        block = w_block(yh, o)
        remote(block, block, wy_send.at[o], wy_recv.at[o], far_dev).wait_send()
        remote(block, block, wc_send.at[o], wc_recv.at[o], core_dev).wait_send()
        block = w_block(1 - yh, o)
        remote(block, block, wc_send.at[4 + o], wc_recv.at[4 + o], core_dev).wait_send()
    g3.wait_send()

    def drain_pieces(o, carry):
        g4_copy(o).wait_send()
        g5_copy(o).wait_send()
        return carry

    lax.fori_loop(1, Z, drain_pieces, 0)
    lo_copy.wait()
    gw_copy.wait()


def body(queries, key_rows, value_rows, cotangent, out_weight, lengths, upweight):
    vm = pltpu.VMEM
    dma = pltpu.SemaphoreType.DMA
    block = (ROWS, LANES)
    any_space = pl.BlockSpec(memory_space=pl.ANY)
    scalar = pl.BlockSpec(memory_space=pltpu.SMEM)
    rows_shape = jax.ShapeDtypeStruct((ROWS, WIDTH), BF16)
    outs = pl.pallas_call(
        layer_kernel,
        out_shape=(rows_shape,) * 4 + (jax.ShapeDtypeStruct((HEAD_DIM, WIDTH), F32),),
        in_specs=[scalar, scalar] + [any_space] * 5,
        out_specs=(any_space,) * 5,
        scratch_shapes=[
            vm((STEPS, 2) + block, BF16),
            vm((STEPS, SLOTS, 2) + block, BF16),
            vm((2, ROWS, WIDTH), BF16),
            vm((2, ROWS, WIDTH), BF16),
            vm((16, HEAD_DIM, WIDTH), BF16),
            vm((2, SPAN) + block, F32),
            vm((8,) + block, BF16),
            vm((STEPS, 2) + block, BF16),
            vm((STEPS, 2) + block, BF16),
            vm((SLOTS, 2) + block, F32),
            vm((STEPS, 2, 2) + block, F32),
            vm((STEPS, 4, 2, 2) + block, BF16),
            vm((STEPS, 4, 2, 2) + block, BF16),
            vm((STEPS, 2, 2) + block, BF16),
            vm((STEPS, 2, HEAD_DIM, WIDTH), F32),
            vm((STEPS, HEAD_DIM, WIDTH), BF16),
            vm((STEPS, HEAD_DIM, WIDTH), BF16),
            vm((3, HEAD_DIM, WIDTH), BF16),
            vm((3, HEAD_DIM, WIDTH), BF16),
            vm((8, HEAD_DIM, LANES), F32),
            vm((4, HEAD_DIM, LANES), BF16),
            vm((4, HEAD_DIM, LANES), BF16),
            vm((Z, 16, LANES), F32),
            vm((Z, 16, LANES), BF16),
            vm((Z, 16, LANES), BF16),
            vm((Z, 16, LANES), F32),
            vm((2, Z, 16, LANES), F32),
            vm((HEAD_DIM, WIDTH), F32),
            vm((ROWS, WIDTH), BF16),
            vm((SPAN * ROWS, 2 * ROWS), F32),
            vm((SPAN * ROWS, 2 * ROWS), F32),
            vm((SPAN * ROWS, 2 * ROWS), BF16),
            vm((SPAN * ROWS, 2 * ROWS), BF16),
            dma((STEPS, 4)),
            dma((STEPS, 3)), dma((STEPS, 3)),
            dma, dma,
            dma((STEPS, 4)), dma((STEPS, 4)),
            dma((3,)), dma((3,)),
            dma((8,)), dma((8,)),
            dma((4,)), dma((4,)),
            dma((STEPS, 4)), dma((STEPS, 4)),
            dma((STEPS,)), dma((STEPS,)),
            dma((STEPS,)), dma((STEPS,)),
            dma((STEPS, 2)), dma((STEPS, 2)),
            dma((STEPS, 4)),
            dma((STEPS,)), dma((STEPS,)),
            dma((3,)), dma((3,)),
            dma, dma,
            dma((Z,)), dma((Z,)),
            dma((Z,)), dma((Z,)),
            dma((2,)), dma((2,)),
        ],
        compiler_params=pltpu.CompilerParams(
            collective_id=0, has_side_effects=True, vmem_limit_bytes=56 * 2**20
        ),
        name="layer",
    )(lengths, upweight, queries[0], key_rows[0], value_rows[0], cotangent[0], out_weight)
    layer_out, grad_query, grad_key, grad_value, grad_weight = outs
    return (layer_out[None], grad_query[None], grad_key[None], grad_value[None], grad_weight)


def solution(mesh):
    rows = P("doc", "seq", None)
    flat = P("doc", None)
    return jax.shard_map(
        body,
        mesh=mesh,
        in_specs=(rows, rows, rows, rows, flat, flat, flat),
        out_specs=(rows, rows, rows, rows, flat),
        check_vma=False,
    )
```

```python
import math

import jax
import jax.numpy as jnp
from jax import lax
from jax.experimental import pallas as pl
from jax.experimental.pallas import tpu as pltpu
from jax.sharding import PartitionSpec as P

HEAD_DIM = 64
WINDOW = 512
BLOCK = 64
DOCS = 4
ROWS = 128
LANES = 128
SPAN = 9
SLOTS = 10
STEPS = 4
WIDTH = 1024
Z = 16
SIDES = (-1, 1)
MESH = pl.DeviceIdType.MESH
BF16 = jnp.bfloat16
F32 = jnp.float32

NT = (((1,), (1,)), ((), ()))
TN = (((0,), (0,)), ((), ()))


def dot(a, b, dims=(((1,), (0,)), ((), ()))):
    return lax.dot_general(a, b, dims, preferred_element_type=F32)


def remote(src, dst, send, recv, device):
    return pltpu.make_async_remote_copy(
        src_ref=src, dst_ref=dst, send_sem=send, recv_sem=recv, device_id=device, device_id_type=MESH
    )


def layer_kernel(
    lengths, upweight, q_in, k_in, v_in, ct_in, w_in,
    lo_out, dq_out, dk_out, dv_out, gw_out,
    qbuf, kv, ctb, gout, wbuf, bias, attbuf, attpair, dqb, acc, own, fout, fhere, rout, rin, fin,
    near, gkeep, g1send, g1recv, g2send, g2recv, g4f, g4send, g4recv, part, parts, zag, gwo, lob,
    s_scr, dp_scr, p_scr, ds_scr,
    l_sem, y_send, y_recv, ct_send, ct_recv, z_send, z_recv, zf_send, zf_recv, wx_send, wx_recv,
    wc_send, wc_recv, wy_send, wy_recv, r_send, r_recv, rf_send, rf_recv, a_send, a_recv,
    dq_send, dq_recv, f_send, f_recv, o_sem, g1_send, g1_rsem, g2_send, g2_rsem,
    g3_send, g3_rsem, g4_send, g4_rsem, g5_send, g5_rsem,
):
    d = lax.axis_index("doc")
    s = lax.axis_index("seq")
    z, y = s // 2, s % 2
    yh, x, core = d // 8, (d // 2) % 4, d % 2
    s_pair = z * 2 + (1 - y)
    d_core = yh * 8 + x * 2 + (1 - core)
    d_far = (1 - yh) * 8 + x * 2 + core

    def at_x(offset):
        return yh * 8 + ((x + offset + 4) % 4) * 2 + core

    def at_z(offset):
        return ((z + offset + Z) % Z) * 2 + y

    def pair_of(step):
        return (x + 3 - step) % 4

    def cols(column, step):
        return pl.ds(pl.multiple_of((column * 4 + pair_of(step)) * LANES, LANES), LANES)

    pair_dev = (d, s_pair)
    core_dev = (d_core, s)
    far_dev = (d_far, s_pair)

    barrier = pltpu.get_barrier_semaphore()
    partners = [pair_dev, core_dev, far_dev, (d_far, s)] + [(at_x(o), s) for o in (1, 2, 3)]
    for device in partners:
        pl.semaphore_signal(barrier, inc=1, device_id=device, device_id_type=MESH)

    def greet(o, carry):
        pl.semaphore_signal(barrier, inc=1, device_id=(d, at_z(o)), device_id_type=MESH)
        return carry

    lax.fori_loop(1, Z, greet, 0)
    pl.semaphore_wait(barrier, len(partners) + Z - 1)

    def own_kv(i):
        mine = cols(y, i)
        return [
            pltpu.make_async_copy(k_in.at[:, mine], kv.at[i, 4 + y, 0], l_sem.at[i, 0]),
            pltpu.make_async_copy(v_in.at[:, mine], kv.at[i, 4 + y, 1], l_sem.at[i, 1]),
        ]

    def own_q(i):
        return pltpu.make_async_copy(q_in.at[:, cols(y, i)], qbuf.at[i, y], l_sem.at[i, 2])

    def pair_kv(i):
        theirs = cols(1 - y, i)
        return [
            remote(k_in.at[:, theirs], kv.at[i, 4 + y, 0], y_send.at[i, 0], y_recv.at[i, 0], pair_dev),
            remote(v_in.at[:, theirs], kv.at[i, 4 + y, 1], y_send.at[i, 1], y_recv.at[i, 1], pair_dev),
        ]

    def pair_q(i):
        return remote(
            q_in.at[:, cols(1 - y, i)], qbuf.at[i, y], y_send.at[i, 2], y_recv.at[i, 2], pair_dev
        )

    def take_kv(i):
        views = [kv.at[i, 5 - y, n] for n in range(2)]
        return [remote(views[n], views[n], y_send.at[i, n], y_recv.at[i, n], pair_dev) for n in range(2)]

    def take_q(i):
        here = qbuf.at[i, 1 - y]
        return remote(here, here, y_send.at[i, 2], y_recv.at[i, 2], pair_dev)

    def halo(i, n, far, arrival=False):
        o = SIDES[n]
        to = 4 - 2 * o * (2 if far else 1)
        here = to if arrival else (4 - 2 * o if far else 4)
        send, recv = (zf_send, zf_recv) if far else (z_send, z_recv)
        return remote(
            kv.at[i, pl.ds(here, 2)], kv.at[i, pl.ds(to, 2)], send.at[i, n], recv.at[i, n], (d, at_z(o))
        )

    own_ct = pltpu.make_async_copy(ct_in, ctb.at[y], l_sem.at[0, 3])
    own_w = pltpu.make_async_copy(w_in, wbuf.at[d], l_sem.at[1, 3])
    send_ct = remote(ct_in, ctb.at[y], ct_send, ct_recv, pair_dev)
    take_ct = remote(ctb.at[1 - y], ctb.at[1 - y], ct_send, ct_recv, pair_dev)

    def start_kv(i):
        for copy in own_kv(i) + pair_kv(i):
            copy.start()

    def start_q(i):
        own_q(i).start()
        pair_q(i).start()

    def start_near(i):
        for copy in own_kv(i):
            copy.wait()
        for copy in take_kv(i):
            copy.wait_recv()
        for n in range(2):
            halo(i, n, False).start()

    def forward(i):
        for n in range(2):
            halo(i, n, False, True).wait_recv()
            halo(i, n, True).start()

    start_kv(0)
    start_kv(1)
    start_q(0)
    own_w.start()
    for o in (1, 2, 3):
        remote(w_in, wbuf.at[d], wx_send.at[o - 1], wx_recv.at[o - 1], (at_x(o), s)).start()
    own_ct.start()
    start_near(0)
    start_kv(2)
    start_q(1)
    start_near(1)
    start_kv(3)
    start_q(2)
    start_q(3)
    send_ct.start()

    bounds = []
    total = jnp.int32(0)
    for j in range(DOCS):
        total = total + lengths[0, j] * BLOCK
        bounds.append(total)

    def doc_of(position):
        ids = jnp.zeros_like(position)
        for bound in bounds:
            ids = ids + (position >= bound).astype(jnp.int32)
        return ids

    for yp in range(2):
        base = (z * 2 + yp) * ROWS

        def fill(j, carry, yp=yp, base=base):
            rows = lax.broadcasted_iota(jnp.int32, (ROWS, ROWS), 0)
            lanes = lax.broadcasted_iota(jnp.int32, (ROWS, ROWS), 1)
            key = base - WINDOW + j * ROWS + rows
            query = base + lanes
            near = jnp.abs(query - key) <= WINDOW
            inside = (key >= 0) & (key < Z * 2 * ROWS)
            ok = near & inside & (doc_of(key) == doc_of(query))
            bias[yp, j] = jnp.where(ok, 0.0, -jnp.inf).astype(F32)
            return carry

        lax.fori_loop(0, SPAN, fill, 0)

    def w_block(high, o):
        return wbuf.at[high * 8 + ((x - o + 4) % 4) * 2 + core]

    own_w.wait()
    for o in range(4):
        block = w_block(yh, o)
        if o:
            remote(block, block, wx_send.at[o - 1], wx_recv.at[o - 1], (at_x(-o), s)).wait_recv()
        remote(block, block, wy_send.at[o], wy_recv.at[o], far_dev).start()
        remote(block, block, wc_send.at[o], wc_recv.at[o], core_dev).start()

    forward(0)
    start_near(2)

    def grad_out_rows():
        own_ct.wait()
        take_ct.wait_recv()
        for yp in range(2):
            position = (z * 2 + yp) * ROWS + lax.broadcasted_iota(jnp.int32, (ROWS, LANES), 0)
            ids = doc_of(position)
            weight = jnp.zeros((ROWS, LANES), jnp.int32)
            for j in range(DOCS):
                weight = weight + jnp.where(ids == j, upweight[0, j], 0)
            weight = weight.astype(F32)
            for j in range(WIDTH // LANES):
                piece = slice(j * LANES, (j + 1) * LANES)
                gout[yp, :, piece] = (weight * ctb[yp, :, piece].astype(F32)).astype(BF16)

    def projection_rows():
        for o in range(4):
            block = w_block(1 - yh, o)
            remote(block, block, wy_send.at[o], wy_recv.at[o], far_dev).wait_recv()
            remote(block, block, wc_send.at[4 + o], wc_recv.at[4 + o], core_dev).start()
        for o in range(4):
            for h, high in ((0, yh), (1, 1 - yh)):
                block = wbuf.at[high * 8 + ((x - o + 4) % 4) * 2 + (1 - core)]
                remote(block, block, wc_send.at[4 * h + o], wc_recv.at[4 * h + o], core_dev).wait_recv()

    lane = lax.broadcasted_iota(jnp.int32, (ROWS, LANES), 1)

    def stacked(block):
        block = block.astype(F32)
        low = jnp.where(lane < HEAD_DIM, block, 0.0).astype(BF16)
        high = jnp.where(lane >= HEAD_DIM, block, 0.0).astype(BF16)
        return jnp.concatenate([low, high], axis=0)

    def unstacked(block):
        return jnp.concatenate([block[:HEAD_DIM, :ROWS], block[HEAD_DIM:, ROWS:]], axis=0)

    def key_block(j):
        return slice(j * ROWS, (j + 1) * ROWS)

    def ahead(i, yp):
        query2 = stacked(qbuf[i, yp])
        peak = jnp.full((8, 2 * ROWS), -jnp.inf, F32)
        for j in range(SPAN):
            mask = bias[yp, j]
            score = dot(kv[i, yp + j, 0], query2, NT) + jnp.concatenate([mask, mask], axis=1)
            s_scr[yp, key_block(j)] = score
            peak = jnp.maximum(peak, jnp.max(score.reshape(ROWS // 8, 8, 2 * ROWS), axis=0))
        peak = jnp.max(peak, axis=0, keepdims=True)
        norm = jnp.zeros((8, 2 * ROWS), F32)
        for j in range(SPAN):
            power = jnp.exp((s_scr[yp, key_block(j)] - peak) * (HEAD_DIM ** -0.5))
            s_scr[yp, key_block(j)] = power
            norm = norm + jnp.sum(power.reshape(ROWS // 8, 8, 2 * ROWS), axis=0)
        share = 1.0 / jnp.sum(norm, axis=0, keepdims=True)
        for j in range(SPAN):
            prob = s_scr[yp, key_block(j)] * share
            s_scr[yp, key_block(j)] = prob
            p_scr[yp, key_block(j)] = prob.astype(BF16)
        values = kv[i, yp:yp + SPAN, 1].reshape(SPAN * ROWS, LANES)
        mixed = unstacked(dot(values, p_scr[yp], TN))
        attpair[i, yp] = mixed.T.astype(BF16)
        return mixed.astype(BF16)

    def back(i, yp, w_pair):
        query2 = stacked(qbuf[i, yp])
        grad2 = stacked(dot(gout[yp], w_pair, NT).astype(BF16))
        centre = jnp.zeros((8, 2 * ROWS), F32)
        for j in range(SPAN):
            slope = dot(kv[i, yp + j, 1], grad2, NT)
            dp_scr[key_block(j)] = slope
            weighted = s_scr[yp, key_block(j)] * slope
            centre = centre + jnp.sum(weighted.reshape(ROWS // 8, 8, 2 * ROWS), axis=0)
        centre = jnp.sum(centre, axis=0, keepdims=True)
        for j in range(SPAN):
            prob = s_scr[yp, key_block(j)]
            grad_score = (prob * (dp_scr[key_block(j)] - centre) * (HEAD_DIM ** -0.5)).astype(BF16)
            ds_scr[key_block(j)] = grad_score
            key_part = dot(grad_score, query2)
            value_part = dot(p_scr[yp, key_block(j)], grad2)
            if yp == 0:
                acc[j, 0] = key_part
                acc[j, 1] = value_part
            elif j + 1 < SPAN:
                acc[j + 1, 0] += key_part
                acc[j + 1, 1] += value_part
            else:
                acc[j + 1, 0] = key_part
                acc[j + 1, 1] = value_part
        keys = kv[i, yp:yp + SPAN, 0].reshape(SPAN * ROWS, LANES)
        dqb[i, yp] = unstacked(dot(keys, ds_scr[...], TN)).T.astype(BF16)

    def att_send(i):
        return remote(
            attpair.at[i, 1 - y], attbuf.at[y * 4 + pair_of(i)], a_send.at[i], a_recv.at[i], pair_dev
        )

    def att_take(i):
        here = attbuf.at[(1 - y) * 4 + pair_of(i)]
        return remote(here, here, a_send.at[i], a_recv.at[i], pair_dev)

    def dq_own(i):
        return pltpu.make_async_copy(dqb.at[i, y], dq_out.at[:, cols(y, i)], o_sem.at[i, 0])

    def dq_pair(i):
        return remote(dqb.at[i, 1 - y], dq_out.at[:, cols(y, i)], dq_send.at[i], dq_recv.at[i], pair_dev)

    def dq_take(i):
        here = dq_out.at[:, cols(1 - y, i)]
        return remote(here, here, dq_send.at[i], dq_recv.at[i], pair_dev)

    def far_copy(i, n):
        return remote(fout.at[i, n], fhere.at[i, n], rf_send.at[i, n], rf_recv.at[i, n], (d, at_z(SIDES[n])))

    def ret_copy(i, n):
        return remote(rout.at[i, n], rin.at[i, n], r_send.at[i, n], r_recv.at[i, n], (d, at_z(SIDES[n])))

    def ret_start(i):
        for n in range(2):
            far_copy(i, n).wait_recv()
            rout[i, n] = (near[i, n] + fhere[i, n].astype(F32)).astype(BF16)
            ret_copy(i, n).start()

    def g1_copy(i):
        return remote(g1send.at[i], g1recv.at[i], g1_send.at[i], g1_rsem.at[i], core_dev)

    def g2_copy(i):
        return remote(g2send.at[i], g2recv.at[i], g2_send.at[i], g2_rsem.at[i], (at_x(-1 - i), s))

    def g2_start(i):
        g1_copy(i).wait_recv()
        g2send[i] = (gkeep[i, core] + g1recv[i].astype(F32)).astype(BF16)
        g2_copy(i).start()

    def fin_own(i):
        return [
            pltpu.make_async_copy(fin.at[i, y, n], out.at[:, cols(y, i)], o_sem.at[i, 1 + n])
            for n, out in ((0, dk_out), (1, dv_out))
        ]

    def fin_pair(i):
        return [
            remote(fin.at[i, 1 - y, n], out.at[:, cols(y, i)], f_send.at[i, n], f_recv.at[i, n], pair_dev)
            for n, out in ((0, dk_out), (1, dv_out))
        ]

    def fin_take(i):
        views = [out.at[:, cols(1 - y, i)] for out in (dk_out, dv_out)]
        return [remote(views[n], views[n], f_send.at[i, n], f_recv.at[i, n], pair_dev) for n in range(2)]

    def finish(i):
        total = own[i]
        for n in range(2):
            ret_copy(i, n).wait_recv()
            total = total + rin[i, n].astype(F32)
        fin[i] = total.astype(BF16)
        for copy in fin_pair(i) + fin_own(i):
            copy.start()

    def g4_copy(o):
        return remote(g4send.at[(z + o) % Z], g4recv.at[o], g4_send.at[o], g4_rsem.at[o], (d, at_z(o)))

    def head_sum():
        g1_copy(3).wait_recv()
        head = gkeep[3, core] + g1recv[3].astype(F32)
        for i in range(3):
            remote(g2recv.at[i], g2recv.at[i], g2_send.at[i], g2_rsem.at[i], (at_x(1 + i), s)).wait_recv()
            head = head + g2recv[i].astype(F32)
        for j in range(8):
            for half in range(2):
                g4f[2 * j + half] = head[half * 32:half * 32 + 32, j * LANES:(j + 1) * LANES]
        g4send[...] = g4f[...].astype(BF16)

        def g4_start(o, carry):
            g4_copy(o).start()
            return carry

        lax.fori_loop(1, Z, g4_start, 0)

    def step(i, carry):
        @pl.when(i < 3)
        def _():
            forward(i + 1)

        @pl.when(i == 0)
        def _():
            start_near(3)

        @pl.when(i > 0)
        def _():
            g2_start(i - 1)

        own_q(i).wait()
        take_q(i).wait_recv()
        for n in range(2):
            halo(i, n, True, True).wait_recv()
        mixed = [ahead(i, yp) for yp in range(2)]
        att_send(i).start()
        attbuf[y * 4 + pair_of(i)] = attpair[i, y]

        @pl.when(i == 0)
        def _():
            grad_out_rows()

        weight_part = dot(mixed[0], gout[0]) + dot(mixed[1], gout[1])
        gkeep[i, 0] = weight_part[:HEAD_DIM]
        gkeep[i, 1] = weight_part[HEAD_DIM:]
        g1send[i] = gkeep[i, 1 - core].astype(BF16)
        g1_copy(i).start()

        @pl.when(i == 0)
        def _():
            projection_rows()

        doc_row = y * 8 + pair_of(i) * 2
        w_pair = wbuf[pl.ds(doc_row, 2)].reshape(2 * HEAD_DIM, WIDTH)
        back(i, 0, w_pair)

        @pl.when(i == 3)
        def _():
            head_sum()

        back(i, 1, w_pair)
        for n in range(2):
            first = 8 * n
            fout[i, n] = acc[first:first + 2].astype(BF16)
            far_copy(i, n).start()
            near[i, n] = acc[2 + 4 * n:4 + 4 * n]
        own[i] = acc[4:6]
        dq_own(i).start()
        dq_pair(i).start()

        @pl.when(i > 0)
        def _():
            ret_start(i - 1)

        @pl.when(i > 1)
        def _():
            finish(i - 2)

        return carry

    lax.fori_loop(0, STEPS, step, 0)
    ret_start(3)
    finish(2)

    for i in range(STEPS):
        att_take(i).wait_recv()
    rows = jnp.concatenate([attbuf[j] for j in range(8)], axis=1)
    for j in range(4):
        piece = slice(j * 256, (j + 1) * 256)
        lob[:, piece] = dot(rows, wbuf[:, :, piece].reshape(WIDTH, 256)).astype(BF16)
    lo_copy = pltpu.make_async_copy(lob, lo_out, o_sem.at[0, 3])
    lo_copy.start()

    def g4_wait(o, total):
        g4_copy(o).wait_recv()
        return total + g4recv[o].astype(F32)

    part[...] = lax.fori_loop(1, Z, g4_wait, g4f[z])

    def g3_copy(n, device):
        slot = (yh + y) % 2
        return remote(part, parts.at[slot], g3_send.at[n], g3_rsem.at[slot], device)

    def g3_take(slot):
        return remote(parts.at[slot], parts.at[slot], g3_send.at[0], g3_rsem.at[slot], pair_dev)

    @pl.when(yh == y)
    def _():
        g3_copy(0, pair_dev).start()
        parts[0] = part[...]
        g3_take(1).wait_recv()
        g3_copy(0, pair_dev).wait_send()

    @pl.when(yh != y)
    def _():
        g3_copy(0, far_dev).start()
        g3_copy(1, (d_far, s)).start()
        g3_take(0).wait_recv()
        g3_take(1).wait_recv()
        g3_copy(0, far_dev).wait_send()
        g3_copy(1, (d_far, s)).wait_send()

    zag[z] = ((parts[0] + parts[1]) * (1.0 / math.sqrt(Z * 2 * ROWS * 16))).astype(BF16)

    def g5_copy(o):
        return remote(zag.at[z], zag.at[z], g5_send.at[o], g5_rsem.at[o], (d, at_z(o)))

    def g5_take(o):
        here = zag.at[(z - o + Z) % Z]
        return remote(here, here, g5_send.at[o], g5_rsem.at[o], (d, at_z(o)))

    def g5_start(o, carry):
        g5_copy(o).start()
        return carry

    lax.fori_loop(1, Z, g5_start, 0)
    finish(3)

    def g5_wait(o, carry):
        g5_take(o).wait_recv()
        return carry

    lax.fori_loop(1, Z, g5_wait, 0)
    for j in range(8):
        for half in range(2):
            gwo[half * 32:half * 32 + 32, j * LANES:(j + 1) * LANES] = zag[2 * j + half].astype(F32)
    gw_copy = pltpu.make_async_copy(gwo, gw_out, o_sem.at[1, 3])
    gw_copy.start()

    def drain(i, carry):
        for copy in pair_kv(i):
            copy.wait_send()
        pair_q(i).wait_send()
        for n in range(2):
            halo(i, n, False).wait_send()
            halo(i, n, True).wait_send()
            far_copy(i, n).wait_send()
            ret_copy(i, n).wait_send()
        att_send(i).wait_send()
        dq_own(i).wait()
        dq_pair(i).wait_send()
        dq_take(i).wait_recv()
        g1_copy(i).wait_send()
        for copy in fin_own(i):
            copy.wait()
        for copy in fin_pair(i):
            copy.wait_send()
        for copy in fin_take(i):
            copy.wait_recv()
        return carry

    lax.fori_loop(0, STEPS, drain, 0)
    send_ct.wait_send()
    for o in (1, 2, 3):
        remote(w_in, wbuf.at[d], wx_send.at[o - 1], wx_recv.at[o - 1], (at_x(o), s)).wait_send()
        g2_copy(o - 1).wait_send()
    for o in range(4):
        block = w_block(yh, o)
        remote(block, block, wy_send.at[o], wy_recv.at[o], far_dev).wait_send()
        remote(block, block, wc_send.at[o], wc_recv.at[o], core_dev).wait_send()
        block = w_block(1 - yh, o)
        remote(block, block, wc_send.at[4 + o], wc_recv.at[4 + o], core_dev).wait_send()

    def drain_pieces(o, carry):
        g4_copy(o).wait_send()
        g5_copy(o).wait_send()
        return carry

    lax.fori_loop(1, Z, drain_pieces, 0)
    lo_copy.wait()
    gw_copy.wait()


def copy_kernel(*refs):
    count = len(refs) // 2
    sems = refs[-1]
    copies = [pltpu.make_async_copy(refs[n], refs[count + n], sems.at[n]) for n in range(count)]
    for copy in copies:
        copy.start()
    for copy in copies:
        copy.wait()


def body(queries, key_rows, value_rows, cotangent, out_weight, lengths, upweight):
    vm = pltpu.VMEM
    dma = pltpu.SemaphoreType.DMA
    block = (ROWS, LANES)
    any_space = pl.BlockSpec(memory_space=pl.ANY)
    scalar = pl.BlockSpec(memory_space=pltpu.SMEM)
    rows_shape = jax.ShapeDtypeStruct((ROWS, WIDTH), BF16)
    outs = pl.pallas_call(
        layer_kernel,
        out_shape=(rows_shape,) * 4 + (jax.ShapeDtypeStruct((HEAD_DIM, WIDTH), F32),),
        in_specs=[scalar, scalar] + [any_space] * 5,
        out_specs=(any_space,) * 5,
        scratch_shapes=[
            vm((STEPS, 2) + block, BF16),
            vm((STEPS, SLOTS, 2) + block, BF16),
            vm((2, ROWS, WIDTH), BF16),
            vm((2, ROWS, WIDTH), BF16),
            vm((16, HEAD_DIM, WIDTH), BF16),
            vm((2, SPAN) + block, F32),
            vm((8,) + block, BF16),
            vm((STEPS, 2) + block, BF16),
            vm((STEPS, 2) + block, BF16),
            vm((SLOTS, 2) + block, F32),
            vm((STEPS, 2, 2) + block, F32),
            vm((STEPS, 2, 2, 2) + block, BF16),
            vm((STEPS, 2, 2, 2) + block, BF16),
            vm((STEPS, 2, 2, 2) + block, BF16),
            vm((STEPS, 2, 2, 2) + block, BF16),
            vm((STEPS, 2, 2) + block, BF16),
            vm((STEPS, 2, 2, 2) + block, F32),
            vm((STEPS, 2, HEAD_DIM, WIDTH), F32),
            vm((STEPS, HEAD_DIM, WIDTH), BF16),
            vm((STEPS, HEAD_DIM, WIDTH), BF16),
            vm((3, HEAD_DIM, WIDTH), BF16),
            vm((3, HEAD_DIM, WIDTH), BF16),
            vm((Z, 32, LANES), F32),
            vm((Z, 32, LANES), BF16),
            vm((Z, 32, LANES), BF16),
            vm((32, LANES), F32),
            vm((2, 32, LANES), F32),
            vm((Z, 32, LANES), BF16),
            vm((HEAD_DIM, WIDTH), F32),
            vm((ROWS, WIDTH), BF16),
            vm((2, SPAN * ROWS, 2 * ROWS), F32),
            vm((SPAN * ROWS, 2 * ROWS), F32),
            vm((2, SPAN * ROWS, 2 * ROWS), BF16),
            vm((SPAN * ROWS, 2 * ROWS), BF16),
            dma((STEPS, 4)),
            dma((STEPS, 3)), dma((STEPS, 3)),
            dma, dma,
            dma((STEPS, 2)), dma((STEPS, 2)),
            dma((STEPS, 2)), dma((STEPS, 2)),
            dma((3,)), dma((3,)),
            dma((8,)), dma((8,)),
            dma((4,)), dma((4,)),
            dma((STEPS, 2)), dma((STEPS, 2)),
            dma((STEPS, 2)), dma((STEPS, 2)),
            dma((STEPS,)), dma((STEPS,)),
            dma((STEPS,)), dma((STEPS,)),
            dma((STEPS, 2)), dma((STEPS, 2)),
            dma((STEPS, 4)),
            dma((STEPS,)), dma((STEPS,)),
            dma((3,)), dma((3,)),
            dma((2,)), dma((2,)),
            dma((Z,)), dma((Z,)),
            dma((Z,)), dma((Z,)),
        ],
        compiler_params=pltpu.CompilerParams(
            collective_id=0, has_side_effects=True, vmem_limit_bytes=56 * 2**20
        ),
        name="layer",
    )(lengths, upweight, queries[0], key_rows[0], value_rows[0], cotangent[0], out_weight)
    outs = pl.pallas_call(
        copy_kernel,
        out_shape=tuple(jax.ShapeDtypeStruct(a.shape, a.dtype) for a in outs),
        in_specs=[any_space] * 5,
        out_specs=(any_space,) * 5,
        scratch_shapes=[dma((5,))],
        name="outputs",
    )(*outs)
    layer_out, grad_query, grad_key, grad_value, grad_weight = outs
    return (layer_out[None], grad_query[None], grad_key[None], grad_value[None], grad_weight)


def solution(mesh):
    rows = P("doc", "seq", None)
    flat = P("doc", None)
    return jax.shard_map(
        body,
        mesh=mesh,
        in_specs=(rows, rows, rows, rows, flat, flat, flat),
        out_specs=(rows, rows, rows, rows, flat),
        check_vma=False,
    )
```

```python
import math

import jax
import jax.numpy as jnp
from jax import lax
from jax.experimental import pallas as pl
from jax.experimental.pallas import tpu as pltpu
from jax.sharding import PartitionSpec as P

HEAD_DIM = 64
WINDOW = 512
BLOCK = 64
DOCS = 4
ROWS = 128
LANES = 128
SPAN = 9
SLOTS = 10
STEPS = 4
WIDTH = 1024
Z = 16
SIDES = (-1, 1)
MESH = pl.DeviceIdType.MESH
BF16 = jnp.bfloat16
F32 = jnp.float32

NT = (((1,), (1,)), ((), ()))
TN = (((0,), (0,)), ((), ()))


def dot(a, b, dims=(((1,), (0,)), ((), ()))):
    return lax.dot_general(a, b, dims, preferred_element_type=F32)


def remote(src, dst, send, recv, device):
    return pltpu.make_async_remote_copy(
        src_ref=src, dst_ref=dst, send_sem=send, recv_sem=recv, device_id=device, device_id_type=MESH
    )


def layer_kernel(
    lengths, upweight, q_in, k_in, v_in, ct_in, w_in,
    lo_out, dq_out, dk_out, dv_out, gw_out,
    qbuf, kv, ctb, gout, wbuf, bias, attbuf, attpair, dqb, acc, own, fout, fhere, rout, rin, fin,
    near, gkeep, g1send, g1recv, g2send, g2recv, g4f, g4send, g4recv, part, parts, zag, gwo, lob,
    s_scr, dp_scr, p_scr, ds_scr,
    l_sem, y_send, y_recv, ct_send, ct_recv, z_send, z_recv, zf_send, zf_recv, wx_send, wx_recv,
    wc_send, wc_recv, wy_send, wy_recv, r_send, r_recv, rf_send, rf_recv, a_send, a_recv,
    dq_send, dq_recv, f_send, f_recv, o_sem, g1_send, g1_rsem, g2_send, g2_rsem,
    g3_send, g3_rsem, g4_send, g4_rsem, g5_send, g5_rsem,
):
    d = lax.axis_index("doc")
    s = lax.axis_index("seq")
    z, y = s // 2, s % 2
    yh, x, core = d // 8, (d // 2) % 4, d % 2
    s_pair = z * 2 + (1 - y)
    d_core = yh * 8 + x * 2 + (1 - core)
    d_far = (1 - yh) * 8 + x * 2 + core

    def at_x(offset):
        return yh * 8 + ((x + offset + 4) % 4) * 2 + core

    def at_z(offset):
        return ((z + offset + Z) % Z) * 2 + y

    def pair_of(step):
        return (x + 3 - step) % 4

    def cols(column, step):
        return pl.ds(pl.multiple_of((column * 4 + pair_of(step)) * LANES, LANES), LANES)

    pair_dev = (d, s_pair)
    core_dev = (d_core, s)
    far_dev = (d_far, s_pair)

    barrier = pltpu.get_barrier_semaphore()
    partners = [pair_dev, core_dev, far_dev, (d_far, s)] + [(at_x(o), s) for o in (1, 2, 3)]
    for device in partners:
        pl.semaphore_signal(barrier, inc=1, device_id=device, device_id_type=MESH)

    def greet(o, carry):
        pl.semaphore_signal(barrier, inc=1, device_id=(d, at_z(o)), device_id_type=MESH)
        return carry

    lax.fori_loop(1, Z, greet, 0)
    pl.semaphore_wait(barrier, len(partners) + Z - 1)

    def own_kv(i):
        mine = cols(y, i)
        return [
            pltpu.make_async_copy(k_in.at[:, mine], kv.at[i, 4 + y, 0], l_sem.at[i, 0]),
            pltpu.make_async_copy(v_in.at[:, mine], kv.at[i, 4 + y, 1], l_sem.at[i, 1]),
        ]

    def own_q(i):
        return pltpu.make_async_copy(q_in.at[:, cols(y, i)], qbuf.at[i, y], l_sem.at[i, 2])

    def pair_kv(i):
        theirs = cols(1 - y, i)
        return [
            remote(k_in.at[:, theirs], kv.at[i, 4 + y, 0], y_send.at[i, 0], y_recv.at[i, 0], pair_dev),
            remote(v_in.at[:, theirs], kv.at[i, 4 + y, 1], y_send.at[i, 1], y_recv.at[i, 1], pair_dev),
        ]

    def pair_q(i):
        return remote(
            q_in.at[:, cols(1 - y, i)], qbuf.at[i, y], y_send.at[i, 2], y_recv.at[i, 2], pair_dev
        )

    def take_kv(i):
        views = [kv.at[i, 5 - y, n] for n in range(2)]
        return [remote(views[n], views[n], y_send.at[i, n], y_recv.at[i, n], pair_dev) for n in range(2)]

    def take_q(i):
        here = qbuf.at[i, 1 - y]
        return remote(here, here, y_send.at[i, 2], y_recv.at[i, 2], pair_dev)

    def halo(i, n, far, arrival=False):
        o = SIDES[n]
        to = 4 - 2 * o * (2 if far else 1)
        here = to if arrival else (4 - 2 * o if far else 4)
        send, recv = (zf_send, zf_recv) if far else (z_send, z_recv)
        return remote(
            kv.at[i, pl.ds(here, 2)], kv.at[i, pl.ds(to, 2)], send.at[i, n], recv.at[i, n], (d, at_z(o))
        )

    own_ct = pltpu.make_async_copy(ct_in, ctb.at[y], l_sem.at[0, 3])
    own_w = pltpu.make_async_copy(w_in, wbuf.at[d], l_sem.at[1, 3])
    send_ct = remote(ct_in, ctb.at[y], ct_send, ct_recv, pair_dev)
    take_ct = remote(ctb.at[1 - y], ctb.at[1 - y], ct_send, ct_recv, pair_dev)

    def start_kv(i):
        for copy in own_kv(i) + pair_kv(i):
            copy.start()

    def start_q(i):
        own_q(i).start()
        pair_q(i).start()

    def start_near(i):
        for copy in own_kv(i):
            copy.wait()
        for copy in take_kv(i):
            copy.wait_recv()
        for n in range(2):
            halo(i, n, False).start()

    def forward(i):
        for n in range(2):
            halo(i, n, False, True).wait_recv()
            halo(i, n, True).start()

    start_kv(0)
    start_kv(1)
    start_q(0)
    own_w.start()
    for o in (1, 2, 3):
        remote(w_in, wbuf.at[d], wx_send.at[o - 1], wx_recv.at[o - 1], (at_x(o), s)).start()
    own_ct.start()
    start_near(0)
    start_kv(2)
    start_q(1)
    start_near(1)
    start_kv(3)
    start_q(2)
    start_q(3)
    send_ct.start()

    bounds = []
    total = jnp.int32(0)
    for j in range(DOCS):
        total = total + lengths[0, j] * BLOCK
        bounds.append(total)

    def doc_of(position):
        ids = jnp.zeros_like(position)
        for bound in bounds:
            ids = ids + (position >= bound).astype(jnp.int32)
        return ids

    for yp in range(2):
        base = (z * 2 + yp) * ROWS

        def fill(j, carry, yp=yp, base=base):
            rows = lax.broadcasted_iota(jnp.int32, (ROWS, ROWS), 0)
            lanes = lax.broadcasted_iota(jnp.int32, (ROWS, ROWS), 1)
            key = base - WINDOW + j * ROWS + rows
            query = base + lanes
            near = jnp.abs(query - key) <= WINDOW
            inside = (key >= 0) & (key < Z * 2 * ROWS)
            ok = near & inside & (doc_of(key) == doc_of(query))
            bias[yp, j] = jnp.where(ok, 0.0, -jnp.inf).astype(F32)
            return carry

        lax.fori_loop(0, SPAN, fill, 0)

    def w_block(high, o):
        return wbuf.at[high * 8 + ((x - o + 4) % 4) * 2 + core]

    own_w.wait()
    for o in range(4):
        block = w_block(yh, o)
        if o:
            remote(block, block, wx_send.at[o - 1], wx_recv.at[o - 1], (at_x(-o), s)).wait_recv()
        remote(block, block, wy_send.at[o], wy_recv.at[o], far_dev).start()
        remote(block, block, wc_send.at[o], wc_recv.at[o], core_dev).start()

    forward(0)
    start_near(2)

    def grad_out_rows():
        own_ct.wait()
        take_ct.wait_recv()
        for yp in range(2):
            position = (z * 2 + yp) * ROWS + lax.broadcasted_iota(jnp.int32, (ROWS, LANES), 0)
            ids = doc_of(position)
            weight = jnp.zeros((ROWS, LANES), jnp.int32)
            for j in range(DOCS):
                weight = weight + jnp.where(ids == j, upweight[0, j], 0)
            weight = weight.astype(F32)
            for j in range(WIDTH // LANES):
                piece = slice(j * LANES, (j + 1) * LANES)
                gout[yp, :, piece] = (weight * ctb[yp, :, piece].astype(F32)).astype(BF16)

    def projection_rows():
        for o in range(4):
            block = w_block(1 - yh, o)
            remote(block, block, wy_send.at[o], wy_recv.at[o], far_dev).wait_recv()
            remote(block, block, wc_send.at[4 + o], wc_recv.at[4 + o], core_dev).start()
        for o in range(4):
            for h, high in ((0, yh), (1, 1 - yh)):
                block = wbuf.at[high * 8 + ((x - o + 4) % 4) * 2 + (1 - core)]
                remote(block, block, wc_send.at[4 * h + o], wc_recv.at[4 * h + o], core_dev).wait_recv()

    lane = lax.broadcasted_iota(jnp.int32, (ROWS, LANES), 1)

    def stacked(block):
        block = block.astype(F32)
        low = jnp.where(lane < HEAD_DIM, block, 0.0).astype(BF16)
        high = jnp.where(lane >= HEAD_DIM, block, 0.0).astype(BF16)
        return jnp.concatenate([low, high], axis=0)

    def unstacked(block):
        return jnp.concatenate([block[:HEAD_DIM, :ROWS], block[HEAD_DIM:, ROWS:]], axis=0)

    def key_block(j):
        return slice(j * ROWS, (j + 1) * ROWS)

    def ahead(i, yp):
        query2 = stacked(qbuf[i, yp])
        peak = jnp.full((8, 2 * ROWS), -jnp.inf, F32)
        for j in range(SPAN):
            mask = bias[yp, j]
            score = dot(kv[i, yp + j, 0], query2, NT) + jnp.concatenate([mask, mask], axis=1)
            s_scr[yp, key_block(j)] = score
            peak = jnp.maximum(peak, jnp.max(score.reshape(ROWS // 8, 8, 2 * ROWS), axis=0))
        peak = jnp.max(peak, axis=0, keepdims=True)
        norm = jnp.zeros((8, 2 * ROWS), F32)
        for j in range(SPAN):
            power = jnp.exp((s_scr[yp, key_block(j)] - peak) * (HEAD_DIM ** -0.5))
            s_scr[yp, key_block(j)] = power
            norm = norm + jnp.sum(power.reshape(ROWS // 8, 8, 2 * ROWS), axis=0)
        share = 1.0 / jnp.sum(norm, axis=0, keepdims=True)
        for j in range(SPAN):
            prob = s_scr[yp, key_block(j)] * share
            s_scr[yp, key_block(j)] = prob
            p_scr[yp, key_block(j)] = prob.astype(BF16)
        values = kv[i, yp:yp + SPAN, 1].reshape(SPAN * ROWS, LANES)
        mixed = unstacked(dot(values, p_scr[yp], TN))
        attpair[i, yp] = mixed.T.astype(BF16)
        return mixed.astype(BF16)

    def back(i, yp, w_pair):
        query2 = stacked(qbuf[i, yp])
        grad2 = stacked(dot(gout[yp], w_pair, NT).astype(BF16))
        centre = jnp.zeros((8, 2 * ROWS), F32)
        for j in range(SPAN):
            slope = dot(kv[i, yp + j, 1], grad2, NT)
            dp_scr[key_block(j)] = slope
            weighted = s_scr[yp, key_block(j)] * slope
            centre = centre + jnp.sum(weighted.reshape(ROWS // 8, 8, 2 * ROWS), axis=0)
        centre = jnp.sum(centre, axis=0, keepdims=True)
        for j in range(SPAN):
            prob = s_scr[yp, key_block(j)]
            grad_score = (prob * (dp_scr[key_block(j)] - centre) * (HEAD_DIM ** -0.5)).astype(BF16)
            ds_scr[key_block(j)] = grad_score
            key_part = dot(grad_score, query2)
            value_part = dot(p_scr[yp, key_block(j)], grad2)
            if yp == 0:
                acc[j, 0] = key_part
                acc[j, 1] = value_part
            elif j + 1 < SPAN:
                acc[j + 1, 0] += key_part
                acc[j + 1, 1] += value_part
            else:
                acc[j + 1, 0] = key_part
                acc[j + 1, 1] = value_part
        keys = kv[i, yp:yp + SPAN, 0].reshape(SPAN * ROWS, LANES)
        dqb[i, yp] = unstacked(dot(keys, ds_scr[...], TN)).T.astype(BF16)

    def att_send(i):
        return remote(
            attpair.at[i, 1 - y], attbuf.at[y * 4 + pair_of(i)], a_send.at[i], a_recv.at[i], pair_dev
        )

    def att_take(i):
        here = attbuf.at[(1 - y) * 4 + pair_of(i)]
        return remote(here, here, a_send.at[i], a_recv.at[i], pair_dev)

    def dq_own(i):
        return pltpu.make_async_copy(dqb.at[i, y], dq_out.at[:, cols(y, i)], o_sem.at[i, 0])

    def dq_pair(i):
        return remote(dqb.at[i, 1 - y], dq_out.at[:, cols(y, i)], dq_send.at[i], dq_recv.at[i], pair_dev)

    def dq_take(i):
        here = dq_out.at[:, cols(1 - y, i)]
        return remote(here, here, dq_send.at[i], dq_recv.at[i], pair_dev)

    def far_copy(i, n):
        return remote(fout.at[i, n], fhere.at[i, n], rf_send.at[i, n], rf_recv.at[i, n], (d, at_z(SIDES[n])))

    def ret_copy(i, n):
        return remote(rout.at[i, n], rin.at[i, n], r_send.at[i, n], r_recv.at[i, n], (d, at_z(SIDES[n])))

    def ret_start(i):
        for n in range(2):
            far_copy(i, n).wait_recv()
            rout[i, n] = (near[i, n] + fhere[i, n].astype(F32)).astype(BF16)
            ret_copy(i, n).start()

    def g1_copy(i):
        return remote(g1send.at[i], g1recv.at[i], g1_send.at[i], g1_rsem.at[i], core_dev)

    def g2_copy(i):
        return remote(g2send.at[i], g2recv.at[i], g2_send.at[i], g2_rsem.at[i], (at_x(-1 - i), s))

    def g2_start(i):
        g1_copy(i).wait_recv()
        g2send[i] = (gkeep[i, core] + g1recv[i].astype(F32)).astype(BF16)
        g2_copy(i).start()

    def fin_own(i):
        return [
            pltpu.make_async_copy(fin.at[i, y, n], out.at[:, cols(y, i)], o_sem.at[i, 1 + n])
            for n, out in ((0, dk_out), (1, dv_out))
        ]

    def fin_pair(i):
        return [
            remote(fin.at[i, 1 - y, n], out.at[:, cols(y, i)], f_send.at[i, n], f_recv.at[i, n], pair_dev)
            for n, out in ((0, dk_out), (1, dv_out))
        ]

    def fin_take(i):
        views = [out.at[:, cols(1 - y, i)] for out in (dk_out, dv_out)]
        return [remote(views[n], views[n], f_send.at[i, n], f_recv.at[i, n], pair_dev) for n in range(2)]

    def finish(i):
        total = own[i]
        for n in range(2):
            ret_copy(i, n).wait_recv()
            total = total + rin[i, n].astype(F32)
        fin[i] = total.astype(BF16)
        for copy in fin_pair(i) + fin_own(i):
            copy.start()

    def g4_copy(o):
        return remote(g4send.at[(z + o) % Z], g4recv.at[o], g4_send.at[o], g4_rsem.at[o], (d, at_z(o)))

    def head_sum():
        g1_copy(3).wait_recv()
        head = gkeep[3, core] + g1recv[3].astype(F32)
        for i in range(3):
            remote(g2recv.at[i], g2recv.at[i], g2_send.at[i], g2_rsem.at[i], (at_x(1 + i), s)).wait_recv()
            head = head + g2recv[i].astype(F32)
        for j in range(8):
            for half in range(2):
                g4f[2 * j + half] = head[half * 32:half * 32 + 32, j * LANES:(j + 1) * LANES]
        g4send[...] = g4f[...].astype(BF16)

        def g4_start(o, carry):
            g4_copy(o).start()
            return carry

        lax.fori_loop(1, Z, g4_start, 0)

    def step(i, carry):
        @pl.when(i < 3)
        def _():
            forward(i + 1)

        @pl.when(i == 0)
        def _():
            start_near(3)

        @pl.when(i > 0)
        def _():
            g2_start(i - 1)

        own_q(i).wait()
        take_q(i).wait_recv()
        for n in range(2):
            halo(i, n, True, True).wait_recv()
        mixed = [ahead(i, yp) for yp in range(2)]
        att_send(i).start()
        attbuf[y * 4 + pair_of(i)] = attpair[i, y]

        @pl.when(i == 0)
        def _():
            grad_out_rows()

        weight_part = dot(mixed[0], gout[0]) + dot(mixed[1], gout[1])
        gkeep[i, 0] = weight_part[:HEAD_DIM]
        gkeep[i, 1] = weight_part[HEAD_DIM:]
        g1send[i] = gkeep[i, 1 - core].astype(BF16)
        g1_copy(i).start()

        @pl.when(i == 0)
        def _():
            projection_rows()

        doc_row = y * 8 + pair_of(i) * 2
        w_pair = wbuf[pl.ds(doc_row, 2)].reshape(2 * HEAD_DIM, WIDTH)
        back(i, 0, w_pair)

        @pl.when(i == 3)
        def _():
            head_sum()

        back(i, 1, w_pair)
        for n in range(2):
            first = 8 * n
            fout[i, n] = acc[first:first + 2].astype(BF16)
            far_copy(i, n).start()
            near[i, n] = acc[2 + 4 * n:4 + 4 * n]
        own[i] = acc[4:6]
        dq_own(i).start()
        dq_pair(i).start()

        @pl.when(i > 0)
        def _():
            ret_start(i - 1)

        @pl.when(i > 1)
        def _():
            finish(i - 2)

        return carry

    lax.fori_loop(0, STEPS, step, 0)
    ret_start(3)
    finish(2)

    for i in range(STEPS):
        att_take(i).wait_recv()
    rows = jnp.concatenate([attbuf[j] for j in range(8)], axis=1)
    for j in range(4):
        piece = slice(j * 256, (j + 1) * 256)
        lob[:, piece] = dot(rows, wbuf[:, :, piece].reshape(WIDTH, 256)).astype(BF16)
    lo_copy = pltpu.make_async_copy(lob, lo_out, o_sem.at[0, 3])
    lo_copy.start()

    def g4_wait(o, total):
        g4_copy(o).wait_recv()
        return total + g4recv[o].astype(F32)

    part[...] = lax.fori_loop(1, Z, g4_wait, g4f[z])

    def g3_copy(n, device):
        slot = (yh + y) % 2
        return remote(part, parts.at[slot], g3_send.at[n], g3_rsem.at[slot], device)

    def g3_take(slot):
        return remote(parts.at[slot], parts.at[slot], g3_send.at[0], g3_rsem.at[slot], pair_dev)

    @pl.when(yh == y)
    def _():
        g3_copy(0, pair_dev).start()
        parts[0] = part[...]
        g3_take(1).wait_recv()
        g3_copy(0, pair_dev).wait_send()

    @pl.when(yh != y)
    def _():
        g3_copy(0, far_dev).start()
        g3_copy(1, (d_far, s)).start()
        g3_take(0).wait_recv()
        g3_take(1).wait_recv()
        g3_copy(0, far_dev).wait_send()
        g3_copy(1, (d_far, s)).wait_send()

    zag[z] = ((parts[0] + parts[1]) * (1.0 / math.sqrt(Z * 2 * ROWS * 16))).astype(BF16)

    def g5_copy(o):
        return remote(zag.at[z], zag.at[z], g5_send.at[o], g5_rsem.at[o], (d, at_z(o)))

    def g5_take(o):
        here = zag.at[(z - o + Z) % Z]
        return remote(here, here, g5_send.at[o], g5_rsem.at[o], (d, at_z(o)))

    def g5_start(o, carry):
        g5_copy(o).start()
        return carry

    lax.fori_loop(1, Z, g5_start, 0)
    finish(3)

    def g5_wait(o, carry):
        g5_take(o).wait_recv()
        return carry

    lax.fori_loop(1, Z, g5_wait, 0)
    for j in range(8):
        for half in range(2):
            gwo[half * 32:half * 32 + 32, j * LANES:(j + 1) * LANES] = zag[2 * j + half].astype(F32)
    gw_copy = pltpu.make_async_copy(gwo, gw_out, o_sem.at[1, 3])
    gw_copy.start()

    def drain(i, carry):
        for copy in pair_kv(i):
            copy.wait_send()
        pair_q(i).wait_send()
        for n in range(2):
            halo(i, n, False).wait_send()
            halo(i, n, True).wait_send()
            far_copy(i, n).wait_send()
            ret_copy(i, n).wait_send()
        att_send(i).wait_send()
        dq_own(i).wait()
        dq_pair(i).wait_send()
        dq_take(i).wait_recv()
        g1_copy(i).wait_send()
        for copy in fin_own(i):
            copy.wait()
        for copy in fin_pair(i):
            copy.wait_send()
        for copy in fin_take(i):
            copy.wait_recv()
        return carry

    lax.fori_loop(0, STEPS, drain, 0)
    send_ct.wait_send()
    for o in (1, 2, 3):
        remote(w_in, wbuf.at[d], wx_send.at[o - 1], wx_recv.at[o - 1], (at_x(o), s)).wait_send()
        g2_copy(o - 1).wait_send()
    for o in range(4):
        block = w_block(yh, o)
        remote(block, block, wy_send.at[o], wy_recv.at[o], far_dev).wait_send()
        remote(block, block, wc_send.at[o], wc_recv.at[o], core_dev).wait_send()
        block = w_block(1 - yh, o)
        remote(block, block, wc_send.at[4 + o], wc_recv.at[4 + o], core_dev).wait_send()

    def drain_pieces(o, carry):
        g4_copy(o).wait_send()
        g5_copy(o).wait_send()
        return carry

    lax.fori_loop(1, Z, drain_pieces, 0)
    lo_copy.wait()
    gw_copy.wait()


def copy_kernel(*refs):
    sources, targets, rooms, sems = refs[:5], refs[5:10], refs[10:15], refs[15]
    loads = [pltpu.make_async_copy(sources[n], rooms[n], sems.at[n]) for n in range(5)]
    stores = [pltpu.make_async_copy(rooms[n], targets[n], sems.at[5 + n]) for n in range(5)]
    for load in loads:
        load.start()
    for load, store in zip(loads, stores):
        load.wait()
        store.start()
    for store in stores:
        store.wait()


def body(queries, key_rows, value_rows, cotangent, out_weight, lengths, upweight):
    vm = pltpu.VMEM
    dma = pltpu.SemaphoreType.DMA
    block = (ROWS, LANES)
    any_space = pl.BlockSpec(memory_space=pl.ANY)
    scalar = pl.BlockSpec(memory_space=pltpu.SMEM)
    rows_shape = jax.ShapeDtypeStruct((ROWS, WIDTH), BF16)
    outs = pl.pallas_call(
        layer_kernel,
        out_shape=(rows_shape,) * 4 + (jax.ShapeDtypeStruct((HEAD_DIM, WIDTH), F32),),
        in_specs=[scalar, scalar] + [any_space] * 5,
        out_specs=(any_space,) * 5,
        scratch_shapes=[
            vm((STEPS, 2) + block, BF16),
            vm((STEPS, SLOTS, 2) + block, BF16),
            vm((2, ROWS, WIDTH), BF16),
            vm((2, ROWS, WIDTH), BF16),
            vm((16, HEAD_DIM, WIDTH), BF16),
            vm((2, SPAN) + block, F32),
            vm((8,) + block, BF16),
            vm((STEPS, 2) + block, BF16),
            vm((STEPS, 2) + block, BF16),
            vm((SLOTS, 2) + block, F32),
            vm((STEPS, 2, 2) + block, F32),
            vm((STEPS, 2, 2, 2) + block, BF16),
            vm((STEPS, 2, 2, 2) + block, BF16),
            vm((STEPS, 2, 2, 2) + block, BF16),
            vm((STEPS, 2, 2, 2) + block, BF16),
            vm((STEPS, 2, 2) + block, BF16),
            vm((STEPS, 2, 2, 2) + block, F32),
            vm((STEPS, 2, HEAD_DIM, WIDTH), F32),
            vm((STEPS, HEAD_DIM, WIDTH), BF16),
            vm((STEPS, HEAD_DIM, WIDTH), BF16),
            vm((3, HEAD_DIM, WIDTH), BF16),
            vm((3, HEAD_DIM, WIDTH), BF16),
            vm((Z, 32, LANES), F32),
            vm((Z, 32, LANES), BF16),
            vm((Z, 32, LANES), BF16),
            vm((32, LANES), F32),
            vm((2, 32, LANES), F32),
            vm((Z, 32, LANES), BF16),
            vm((HEAD_DIM, WIDTH), F32),
            vm((ROWS, WIDTH), BF16),
            vm((2, SPAN * ROWS, 2 * ROWS), F32),
            vm((SPAN * ROWS, 2 * ROWS), F32),
            vm((2, SPAN * ROWS, 2 * ROWS), BF16),
            vm((SPAN * ROWS, 2 * ROWS), BF16),
            dma((STEPS, 4)),
            dma((STEPS, 3)), dma((STEPS, 3)),
            dma, dma,
            dma((STEPS, 2)), dma((STEPS, 2)),
            dma((STEPS, 2)), dma((STEPS, 2)),
            dma((3,)), dma((3,)),
            dma((8,)), dma((8,)),
            dma((4,)), dma((4,)),
            dma((STEPS, 2)), dma((STEPS, 2)),
            dma((STEPS, 2)), dma((STEPS, 2)),
            dma((STEPS,)), dma((STEPS,)),
            dma((STEPS,)), dma((STEPS,)),
            dma((STEPS, 2)), dma((STEPS, 2)),
            dma((STEPS, 4)),
            dma((STEPS,)), dma((STEPS,)),
            dma((3,)), dma((3,)),
            dma((2,)), dma((2,)),
            dma((Z,)), dma((Z,)),
            dma((Z,)), dma((Z,)),
        ],
        compiler_params=pltpu.CompilerParams(
            collective_id=0, has_side_effects=True, vmem_limit_bytes=56 * 2**20
        ),
        name="layer",
    )(lengths, upweight, queries[0], key_rows[0], value_rows[0], cotangent[0], out_weight)
    outs = pl.pallas_call(
        copy_kernel,
        out_shape=tuple(jax.ShapeDtypeStruct(a.shape, a.dtype) for a in outs),
        in_specs=[any_space] * 5,
        out_specs=(any_space,) * 5,
        scratch_shapes=[vm(a.shape, a.dtype) for a in outs] + [dma((10,))],
        name="outputs",
    )(*outs)
    layer_out, grad_query, grad_key, grad_value, grad_weight = outs
    return (layer_out[None], grad_query[None], grad_key[None], grad_value[None], grad_weight)


def solution(mesh):
    rows = P("doc", "seq", None)
    flat = P("doc", None)
    return jax.shard_map(
        body,
        mesh=mesh,
        in_specs=(rows, rows, rows, rows, flat, flat, flat),
        out_specs=(rows, rows, rows, rows, flat),
        check_vma=False,
    )
```

```python
import math

import jax
import jax.numpy as jnp
from jax import lax
from jax.experimental import pallas as pl
from jax.experimental.pallas import tpu as pltpu
from jax.sharding import PartitionSpec as P

HEAD_DIM = 64
WINDOW = 512
BLOCK = 64
DOCS = 4
ROWS = 128
LANES = 128
SPAN = 9
SLOTS = 10
STEPS = 4
WIDTH = 1024
Z = 16
SIDES = (-1, 1)
MESH = pl.DeviceIdType.MESH
BF16 = jnp.bfloat16
F32 = jnp.float32

NT = (((1,), (1,)), ((), ()))
TN = (((0,), (0,)), ((), ()))


def dot(a, b, dims=(((1,), (0,)), ((), ()))):
    return lax.dot_general(a, b, dims, preferred_element_type=F32)


def remote(src, dst, send, recv, device):
    return pltpu.make_async_remote_copy(
        src_ref=src, dst_ref=dst, send_sem=send, recv_sem=recv, device_id=device, device_id_type=MESH
    )


def layer_kernel(
    lengths, upweight, q_in, k_in, v_in, ct_in, w_in,
    lo_out, dq_out, dk_out, dv_out, gw_out,
    qbuf, kv, ctb, gout, wbuf, bias, attbuf, attpair, dqb, acc, own, fout, fhere, rout, rin, fin,
    near, gkeep, g1send, g1recv, g2send, g2recv, g4f, g4send, g4recv, part, parts, zag, gwo, lob,
    s_scr, dp_scr, p_scr, ds_scr,
    l_sem, y_send, y_recv, ct_send, ct_recv, z_send, z_recv, zf_send, zf_recv, wx_send, wx_recv,
    wc_send, wc_recv, wy_send, wy_recv, r_send, r_recv, rf_send, rf_recv, a_send, a_recv,
    dq_send, dq_recv, f_send, f_recv, o_sem, g1_send, g1_rsem, g2_send, g2_rsem,
    g3_send, g3_rsem, g4_send, g4_rsem, g5_send, g5_rsem,
):
    d = lax.axis_index("doc")
    s = lax.axis_index("seq")
    z, y = s // 2, s % 2
    yh, x, core = d // 8, (d // 2) % 4, d % 2
    s_pair = z * 2 + (1 - y)
    d_core = yh * 8 + x * 2 + (1 - core)
    d_far = (1 - yh) * 8 + x * 2 + core

    def at_x(offset):
        return yh * 8 + ((x + offset + 4) % 4) * 2 + core

    def at_z(offset):
        return ((z + offset + Z) % Z) * 2 + y

    def pair_of(step):
        return (x + 3 - step) % 4

    def cols(column, step):
        return pl.ds(pl.multiple_of((column * 4 + pair_of(step)) * LANES, LANES), LANES)

    pair_dev = (d, s_pair)
    core_dev = (d_core, s)
    far_dev = (d_far, s_pair)

    barrier = pltpu.get_barrier_semaphore()
    partners = [pair_dev, core_dev, far_dev, (d_far, s)] + [(at_x(o), s) for o in (1, 2, 3)]
    for device in partners:
        pl.semaphore_signal(barrier, inc=1, device_id=device, device_id_type=MESH)

    def greet(o, carry):
        pl.semaphore_signal(barrier, inc=1, device_id=(d, at_z(o)), device_id_type=MESH)
        return carry

    lax.fori_loop(1, Z, greet, 0)
    pl.semaphore_wait(barrier, len(partners) + Z - 1)

    def own_kv(i):
        mine = cols(y, i)
        return [
            pltpu.make_async_copy(k_in.at[:, mine], kv.at[i, 4 + y, 0], l_sem.at[i, 0]),
            pltpu.make_async_copy(v_in.at[:, mine], kv.at[i, 4 + y, 1], l_sem.at[i, 1]),
        ]

    def own_q(i):
        return pltpu.make_async_copy(q_in.at[:, cols(y, i)], qbuf.at[i, y], l_sem.at[i, 2])

    def pair_kv(i):
        theirs = cols(1 - y, i)
        return [
            remote(k_in.at[:, theirs], kv.at[i, 4 + y, 0], y_send.at[i, 0], y_recv.at[i, 0], pair_dev),
            remote(v_in.at[:, theirs], kv.at[i, 4 + y, 1], y_send.at[i, 1], y_recv.at[i, 1], pair_dev),
        ]

    def pair_q(i):
        return remote(
            q_in.at[:, cols(1 - y, i)], qbuf.at[i, y], y_send.at[i, 2], y_recv.at[i, 2], pair_dev
        )

    def take_kv(i):
        views = [kv.at[i, 5 - y, n] for n in range(2)]
        return [remote(views[n], views[n], y_send.at[i, n], y_recv.at[i, n], pair_dev) for n in range(2)]

    def take_q(i):
        here = qbuf.at[i, 1 - y]
        return remote(here, here, y_send.at[i, 2], y_recv.at[i, 2], pair_dev)

    def halo(i, n, far, arrival=False):
        o = SIDES[n]
        to = 4 - 2 * o * (2 if far else 1)
        here = to if arrival else (4 - 2 * o if far else 4)
        send, recv = (zf_send, zf_recv) if far else (z_send, z_recv)
        return remote(
            kv.at[i, pl.ds(here, 2)], kv.at[i, pl.ds(to, 2)], send.at[i, n], recv.at[i, n], (d, at_z(o))
        )

    own_ct = pltpu.make_async_copy(ct_in, ctb.at[y], l_sem.at[0, 3])
    own_w = pltpu.make_async_copy(w_in, wbuf.at[d], l_sem.at[1, 3])
    send_ct = remote(ct_in, ctb.at[y], ct_send, ct_recv, pair_dev)
    take_ct = remote(ctb.at[1 - y], ctb.at[1 - y], ct_send, ct_recv, pair_dev)

    def start_kv(i):
        for copy in own_kv(i) + pair_kv(i):
            copy.start()

    def start_q(i):
        own_q(i).start()
        pair_q(i).start()

    def start_near(i):
        for copy in own_kv(i):
            copy.wait()
        for copy in take_kv(i):
            copy.wait_recv()
        for n in range(2):
            halo(i, n, False).start()

    def forward(i):
        for n in range(2):
            halo(i, n, False, True).wait_recv()
            halo(i, n, True).start()

    start_kv(0)
    start_kv(1)
    start_q(0)
    own_w.start()
    for o in (1, 2, 3):
        remote(w_in, wbuf.at[d], wx_send.at[o - 1], wx_recv.at[o - 1], (at_x(o), s)).start()
    own_ct.start()
    start_near(0)
    start_kv(2)
    start_q(1)
    start_near(1)
    start_kv(3)
    start_q(2)
    start_q(3)
    send_ct.start()

    bounds = []
    total = jnp.int32(0)
    for j in range(DOCS):
        total = total + lengths[0, j] * BLOCK
        bounds.append(total)

    def doc_of(position):
        ids = jnp.zeros_like(position)
        for bound in bounds:
            ids = ids + (position >= bound).astype(jnp.int32)
        return ids

    for yp in range(2):
        base = (z * 2 + yp) * ROWS

        def fill(j, carry, yp=yp, base=base):
            rows = lax.broadcasted_iota(jnp.int32, (ROWS, ROWS), 0)
            lanes = lax.broadcasted_iota(jnp.int32, (ROWS, ROWS), 1)
            key = base - WINDOW + j * ROWS + rows
            query = base + lanes
            near = jnp.abs(query - key) <= WINDOW
            inside = (key >= 0) & (key < Z * 2 * ROWS)
            ok = near & inside & (doc_of(key) == doc_of(query))
            bias[yp, j] = jnp.where(ok, 0.0, -jnp.inf).astype(F32)
            return carry

        lax.fori_loop(0, SPAN, fill, 0)

    def w_block(high, o):
        return wbuf.at[high * 8 + ((x - o + 4) % 4) * 2 + core]

    own_w.wait()
    for o in range(4):
        block = w_block(yh, o)
        if o:
            remote(block, block, wx_send.at[o - 1], wx_recv.at[o - 1], (at_x(-o), s)).wait_recv()
        remote(block, block, wy_send.at[o], wy_recv.at[o], far_dev).start()
        remote(block, block, wc_send.at[o], wc_recv.at[o], core_dev).start()

    forward(0)
    start_near(2)

    def grad_out_rows():
        own_ct.wait()
        take_ct.wait_recv()
        for yp in range(2):
            position = (z * 2 + yp) * ROWS + lax.broadcasted_iota(jnp.int32, (ROWS, LANES), 0)
            ids = doc_of(position)
            weight = jnp.zeros((ROWS, LANES), jnp.int32)
            for j in range(DOCS):
                weight = weight + jnp.where(ids == j, upweight[0, j], 0)
            weight = weight.astype(F32)
            for j in range(WIDTH // LANES):
                piece = slice(j * LANES, (j + 1) * LANES)
                gout[yp, :, piece] = (weight * ctb[yp, :, piece].astype(F32)).astype(BF16)

    def projection_rows():
        for o in range(4):
            block = w_block(1 - yh, o)
            remote(block, block, wy_send.at[o], wy_recv.at[o], far_dev).wait_recv()
            remote(block, block, wc_send.at[4 + o], wc_recv.at[4 + o], core_dev).start()
        for o in range(4):
            for h, high in ((0, yh), (1, 1 - yh)):
                block = wbuf.at[high * 8 + ((x - o + 4) % 4) * 2 + (1 - core)]
                remote(block, block, wc_send.at[4 * h + o], wc_recv.at[4 * h + o], core_dev).wait_recv()

    lane = lax.broadcasted_iota(jnp.int32, (ROWS, LANES), 1)

    def stacked(block):
        block = block.astype(F32)
        low = jnp.where(lane < HEAD_DIM, block, 0.0).astype(BF16)
        high = jnp.where(lane >= HEAD_DIM, block, 0.0).astype(BF16)
        return jnp.concatenate([low, high], axis=0)

    def unstacked(block):
        return jnp.concatenate([block[:HEAD_DIM, :ROWS], block[HEAD_DIM:, ROWS:]], axis=0)

    def key_block(j):
        return slice(j * ROWS, (j + 1) * ROWS)

    def ahead(i, yp):
        query2 = stacked(qbuf[i, yp])
        peak = jnp.full((8, 2 * ROWS), -jnp.inf, F32)
        for j in range(SPAN):
            mask = bias[yp, j]
            score = dot(kv[i, yp + j, 0], query2, NT) + jnp.concatenate([mask, mask], axis=1)
            s_scr[i % 2, yp, key_block(j)] = score
            peak = jnp.maximum(peak, jnp.max(score.reshape(ROWS // 8, 8, 2 * ROWS), axis=0))
        peak = jnp.max(peak, axis=0, keepdims=True)
        norm = jnp.zeros((8, 2 * ROWS), F32)
        for j in range(SPAN):
            power = jnp.exp((s_scr[i % 2, yp, key_block(j)] - peak) * (HEAD_DIM ** -0.5))
            s_scr[i % 2, yp, key_block(j)] = power
            norm = norm + jnp.sum(power.reshape(ROWS // 8, 8, 2 * ROWS), axis=0)
        share = 1.0 / jnp.sum(norm, axis=0, keepdims=True)
        for j in range(SPAN):
            prob = s_scr[i % 2, yp, key_block(j)] * share
            s_scr[i % 2, yp, key_block(j)] = prob
            p_scr[i % 2, yp, key_block(j)] = prob.astype(BF16)
        values = kv[i, yp:yp + SPAN, 1].reshape(SPAN * ROWS, LANES)
        mixed = unstacked(dot(values, p_scr[i % 2, yp], TN))
        attpair[i, yp] = mixed.T.astype(BF16)

    def back(i, yp, w_pair):
        query2 = stacked(qbuf[i, yp])
        grad2 = stacked(dot(gout[yp], w_pair, NT).astype(BF16))
        centre = jnp.zeros((8, 2 * ROWS), F32)
        for j in range(SPAN):
            slope = dot(kv[i, yp + j, 1], grad2, NT)
            dp_scr[key_block(j)] = slope
            weighted = s_scr[i % 2, yp, key_block(j)] * slope
            centre = centre + jnp.sum(weighted.reshape(ROWS // 8, 8, 2 * ROWS), axis=0)
        centre = jnp.sum(centre, axis=0, keepdims=True)
        for j in range(SPAN):
            prob = s_scr[i % 2, yp, key_block(j)]
            grad_score = (prob * (dp_scr[key_block(j)] - centre) * (HEAD_DIM ** -0.5)).astype(BF16)
            ds_scr[key_block(j)] = grad_score
            key_part = dot(grad_score, query2)
            value_part = dot(p_scr[i % 2, yp, key_block(j)], grad2)
            if yp == 0:
                acc[j, 0] = key_part
                acc[j, 1] = value_part
            elif j + 1 < SPAN:
                acc[j + 1, 0] += key_part
                acc[j + 1, 1] += value_part
            else:
                acc[j + 1, 0] = key_part
                acc[j + 1, 1] = value_part
        keys = kv[i, yp:yp + SPAN, 0].reshape(SPAN * ROWS, LANES)
        dqb[i, yp] = unstacked(dot(keys, ds_scr[...], TN)).T.astype(BF16)

    def att_send(i):
        return remote(
            attpair.at[i, 1 - y], attbuf.at[y * 4 + pair_of(i)], a_send.at[i], a_recv.at[i], pair_dev
        )

    def att_take(i):
        here = attbuf.at[(1 - y) * 4 + pair_of(i)]
        return remote(here, here, a_send.at[i], a_recv.at[i], pair_dev)

    def dq_own(i):
        return pltpu.make_async_copy(dqb.at[i, y], dq_out.at[:, cols(y, i)], o_sem.at[i, 0])

    def dq_pair(i):
        return remote(dqb.at[i, 1 - y], dq_out.at[:, cols(y, i)], dq_send.at[i], dq_recv.at[i], pair_dev)

    def dq_take(i):
        here = dq_out.at[:, cols(1 - y, i)]
        return remote(here, here, dq_send.at[i], dq_recv.at[i], pair_dev)

    def far_copy(i, n):
        return remote(fout.at[i, n], fhere.at[i, n], rf_send.at[i, n], rf_recv.at[i, n], (d, at_z(SIDES[n])))

    def ret_copy(i, n):
        return remote(rout.at[i, n], rin.at[i, n], r_send.at[i, n], r_recv.at[i, n], (d, at_z(SIDES[n])))

    def ret_start(i):
        for n in range(2):
            far_copy(i, n).wait_recv()
            rout[i, n] = (near[i, n] + fhere[i, n].astype(F32)).astype(BF16)
            ret_copy(i, n).start()

    def g1_copy(i):
        return remote(g1send.at[i], g1recv.at[i], g1_send.at[i], g1_rsem.at[i], core_dev)

    def g2_copy(i):
        return remote(g2send.at[i], g2recv.at[i], g2_send.at[i], g2_rsem.at[i], (at_x(-1 - i), s))

    def g2_start(i):
        g1_copy(i).wait_recv()
        g2send[i] = (gkeep[i, core] + g1recv[i].astype(F32)).astype(BF16)
        g2_copy(i).start()

    def fin_own(i):
        return [
            pltpu.make_async_copy(fin.at[i, y, n], out.at[:, cols(y, i)], o_sem.at[i, 1 + n])
            for n, out in ((0, dk_out), (1, dv_out))
        ]

    def fin_pair(i):
        return [
            remote(fin.at[i, 1 - y, n], out.at[:, cols(y, i)], f_send.at[i, n], f_recv.at[i, n], pair_dev)
            for n, out in ((0, dk_out), (1, dv_out))
        ]

    def fin_take(i):
        views = [out.at[:, cols(1 - y, i)] for out in (dk_out, dv_out)]
        return [remote(views[n], views[n], f_send.at[i, n], f_recv.at[i, n], pair_dev) for n in range(2)]

    def finish(i):
        total = own[i]
        for n in range(2):
            ret_copy(i, n).wait_recv()
            total = total + rin[i, n].astype(F32)
        fin[i] = total.astype(BF16)
        for copy in fin_pair(i) + fin_own(i):
            copy.start()

    def g4_copy(o):
        return remote(g4send.at[(z + o) % Z], g4recv.at[o], g4_send.at[o], g4_rsem.at[o], (d, at_z(o)))

    def head_sum():
        g1_copy(3).wait_recv()
        head = gkeep[3, core] + g1recv[3].astype(F32)
        for i in range(3):
            remote(g2recv.at[i], g2recv.at[i], g2_send.at[i], g2_rsem.at[i], (at_x(1 + i), s)).wait_recv()
            head = head + g2recv[i].astype(F32)
        for j in range(8):
            for half in range(2):
                g4f[2 * j + half] = head[half * 32:half * 32 + 32, j * LANES:(j + 1) * LANES]
        g4send[...] = g4f[...].astype(BF16)

        def g4_start(o, carry):
            g4_copy(o).start()
            return carry

        lax.fori_loop(1, Z, g4_start, 0)

    def weigh(i):
        weight_part = dot(attpair[i, 0], gout[0], TN) + dot(attpair[i, 1], gout[1], TN)
        gkeep[i, 0] = weight_part[:HEAD_DIM]
        gkeep[i, 1] = weight_part[HEAD_DIM:]
        g1send[i] = gkeep[i, 1 - core].astype(BF16)
        g1_copy(i).start()

    def step(i, carry):
        @pl.when(i < 3)
        def _():
            forward(i + 1)

        @pl.when(i == 0)
        def _():
            start_near(3)

        @pl.when(i == 2)
        def _():
            g2_start(0)

        @pl.when((i > 1) & (i < STEPS))
        def _():
            g2_start(i - 1)

        @pl.when(i < STEPS)
        def _():
            own_q(i).wait()
            take_q(i).wait_recv()
            for n in range(2):
                halo(i, n, True, True).wait_recv()
            for yp in range(2):
                ahead(i, yp)
            att_send(i).start()
            attbuf[y * 4 + pair_of(i)] = attpair[i, y]

        @pl.when(i == 1)
        def _():
            grad_out_rows()
            weigh(0)

        @pl.when((i > 0) & (i < STEPS))
        def _():
            weigh(i)

        @pl.when(i == 1)
        def _():
            projection_rows()

        @pl.when(i == STEPS)
        def _():
            head_sum()

        @pl.when(i > 0)
        def _():
            behind(i - 1)

        return carry

    def behind(i):
        doc_row = y * 8 + pair_of(i) * 2
        w_pair = wbuf[pl.ds(doc_row, 2)].reshape(2 * HEAD_DIM, WIDTH)
        back(i, 0, w_pair)
        back(i, 1, w_pair)
        for n in range(2):
            first = 8 * n
            fout[i, n] = acc[first:first + 2].astype(BF16)
            far_copy(i, n).start()
            near[i, n] = acc[2 + 4 * n:4 + 4 * n]
        own[i] = acc[4:6]
        dq_own(i).start()
        dq_pair(i).start()

        @pl.when(i > 0)
        def _():
            ret_start(i - 1)

        @pl.when(i > 1)
        def _():
            finish(i - 2)

    lax.fori_loop(0, STEPS + 1, step, 0)
    ret_start(3)
    finish(2)

    for i in range(STEPS):
        att_take(i).wait_recv()
    rows = jnp.concatenate([attbuf[j] for j in range(8)], axis=1)
    for j in range(4):
        piece = slice(j * 256, (j + 1) * 256)
        lob[:, piece] = dot(rows, wbuf[:, :, piece].reshape(WIDTH, 256)).astype(BF16)
    lo_copy = pltpu.make_async_copy(lob, lo_out, o_sem.at[0, 3])
    lo_copy.start()

    def g4_wait(o, total):
        g4_copy(o).wait_recv()
        return total + g4recv[o].astype(F32)

    part[...] = lax.fori_loop(1, Z, g4_wait, g4f[z])

    def g3_copy(n, device):
        slot = (yh + y) % 2
        return remote(part, parts.at[slot], g3_send.at[n], g3_rsem.at[slot], device)

    def g3_take(slot):
        return remote(parts.at[slot], parts.at[slot], g3_send.at[0], g3_rsem.at[slot], pair_dev)

    @pl.when(yh == y)
    def _():
        g3_copy(0, pair_dev).start()
        parts[0] = part[...]
        g3_take(1).wait_recv()
        g3_copy(0, pair_dev).wait_send()

    @pl.when(yh != y)
    def _():
        g3_copy(0, far_dev).start()
        g3_copy(1, (d_far, s)).start()
        g3_take(0).wait_recv()
        g3_take(1).wait_recv()
        g3_copy(0, far_dev).wait_send()
        g3_copy(1, (d_far, s)).wait_send()

    zag[z] = ((parts[0] + parts[1]) * (1.0 / math.sqrt(Z * 2 * ROWS * 16))).astype(BF16)

    def g5_copy(o):
        return remote(zag.at[z], zag.at[z], g5_send.at[o], g5_rsem.at[o], (d, at_z(o)))

    def g5_take(o):
        here = zag.at[(z - o + Z) % Z]
        return remote(here, here, g5_send.at[o], g5_rsem.at[o], (d, at_z(o)))

    def g5_start(o, carry):
        g5_copy(o).start()
        return carry

    lax.fori_loop(1, Z, g5_start, 0)
    finish(3)

    def g5_wait(o, carry):
        g5_take(o).wait_recv()
        return carry

    lax.fori_loop(1, Z, g5_wait, 0)
    for j in range(8):
        for half in range(2):
            gwo[half * 32:half * 32 + 32, j * LANES:(j + 1) * LANES] = zag[2 * j + half].astype(F32)
    gw_copy = pltpu.make_async_copy(gwo, gw_out, o_sem.at[1, 3])
    gw_copy.start()

    def drain(i, carry):
        for copy in pair_kv(i):
            copy.wait_send()
        pair_q(i).wait_send()
        for n in range(2):
            halo(i, n, False).wait_send()
            halo(i, n, True).wait_send()
            far_copy(i, n).wait_send()
            ret_copy(i, n).wait_send()
        att_send(i).wait_send()
        dq_own(i).wait()
        dq_pair(i).wait_send()
        dq_take(i).wait_recv()
        g1_copy(i).wait_send()
        for copy in fin_own(i):
            copy.wait()
        for copy in fin_pair(i):
            copy.wait_send()
        for copy in fin_take(i):
            copy.wait_recv()
        return carry

    lax.fori_loop(0, STEPS, drain, 0)
    send_ct.wait_send()
    for o in (1, 2, 3):
        remote(w_in, wbuf.at[d], wx_send.at[o - 1], wx_recv.at[o - 1], (at_x(o), s)).wait_send()
        g2_copy(o - 1).wait_send()
    for o in range(4):
        block = w_block(yh, o)
        remote(block, block, wy_send.at[o], wy_recv.at[o], far_dev).wait_send()
        remote(block, block, wc_send.at[o], wc_recv.at[o], core_dev).wait_send()
        block = w_block(1 - yh, o)
        remote(block, block, wc_send.at[4 + o], wc_recv.at[4 + o], core_dev).wait_send()

    def drain_pieces(o, carry):
        g4_copy(o).wait_send()
        g5_copy(o).wait_send()
        return carry

    lax.fori_loop(1, Z, drain_pieces, 0)
    lo_copy.wait()
    gw_copy.wait()


def copy_kernel(*refs):
    sources, targets, rooms, sems = refs[:5], refs[5:10], refs[10:15], refs[15]
    loads = [pltpu.make_async_copy(sources[n], rooms[n], sems.at[n]) for n in range(5)]
    stores = [pltpu.make_async_copy(rooms[n], targets[n], sems.at[5 + n]) for n in range(5)]
    for load in loads:
        load.start()
    for load, store in zip(loads, stores):
        load.wait()
        store.start()
    for store in stores:
        store.wait()


def body(queries, key_rows, value_rows, cotangent, out_weight, lengths, upweight):
    vm = pltpu.VMEM
    dma = pltpu.SemaphoreType.DMA
    block = (ROWS, LANES)
    any_space = pl.BlockSpec(memory_space=pl.ANY)
    scalar = pl.BlockSpec(memory_space=pltpu.SMEM)
    rows_shape = jax.ShapeDtypeStruct((ROWS, WIDTH), BF16)
    outs = pl.pallas_call(
        layer_kernel,
        out_shape=(rows_shape,) * 4 + (jax.ShapeDtypeStruct((HEAD_DIM, WIDTH), F32),),
        in_specs=[scalar, scalar] + [any_space] * 5,
        out_specs=(any_space,) * 5,
        scratch_shapes=[
            vm((STEPS, 2) + block, BF16),
            vm((STEPS, SLOTS, 2) + block, BF16),
            vm((2, ROWS, WIDTH), BF16),
            vm((2, ROWS, WIDTH), BF16),
            vm((16, HEAD_DIM, WIDTH), BF16),
            vm((2, SPAN) + block, F32),
            vm((8,) + block, BF16),
            vm((STEPS, 2) + block, BF16),
            vm((STEPS, 2) + block, BF16),
            vm((SLOTS, 2) + block, F32),
            vm((STEPS, 2, 2) + block, F32),
            vm((STEPS, 2, 2, 2) + block, BF16),
            vm((STEPS, 2, 2, 2) + block, BF16),
            vm((STEPS, 2, 2, 2) + block, BF16),
            vm((STEPS, 2, 2, 2) + block, BF16),
            vm((STEPS, 2, 2) + block, BF16),
            vm((STEPS, 2, 2, 2) + block, F32),
            vm((STEPS, 2, HEAD_DIM, WIDTH), F32),
            vm((STEPS, HEAD_DIM, WIDTH), BF16),
            vm((STEPS, HEAD_DIM, WIDTH), BF16),
            vm((3, HEAD_DIM, WIDTH), BF16),
            vm((3, HEAD_DIM, WIDTH), BF16),
            vm((Z, 32, LANES), F32),
            vm((Z, 32, LANES), BF16),
            vm((Z, 32, LANES), BF16),
            vm((32, LANES), F32),
            vm((2, 32, LANES), F32),
            vm((Z, 32, LANES), BF16),
            vm((HEAD_DIM, WIDTH), F32),
            vm((ROWS, WIDTH), BF16),
            vm((2, 2, SPAN * ROWS, 2 * ROWS), F32),
            vm((SPAN * ROWS, 2 * ROWS), F32),
            vm((2, 2, SPAN * ROWS, 2 * ROWS), BF16),
            vm((SPAN * ROWS, 2 * ROWS), BF16),
            dma((STEPS, 4)),
            dma((STEPS, 3)), dma((STEPS, 3)),
            dma, dma,
            dma((STEPS, 2)), dma((STEPS, 2)),
            dma((STEPS, 2)), dma((STEPS, 2)),
            dma((3,)), dma((3,)),
            dma((8,)), dma((8,)),
            dma((4,)), dma((4,)),
            dma((STEPS, 2)), dma((STEPS, 2)),
            dma((STEPS, 2)), dma((STEPS, 2)),
            dma((STEPS,)), dma((STEPS,)),
            dma((STEPS,)), dma((STEPS,)),
            dma((STEPS, 2)), dma((STEPS, 2)),
            dma((STEPS, 4)),
            dma((STEPS,)), dma((STEPS,)),
            dma((3,)), dma((3,)),
            dma((2,)), dma((2,)),
            dma((Z,)), dma((Z,)),
            dma((Z,)), dma((Z,)),
        ],
        compiler_params=pltpu.CompilerParams(
            collective_id=0, has_side_effects=True, vmem_limit_bytes=56 * 2**20
        ),
        name="layer",
    )(lengths, upweight, queries[0], key_rows[0], value_rows[0], cotangent[0], out_weight)
    outs = pl.pallas_call(
        copy_kernel,
        out_shape=tuple(jax.ShapeDtypeStruct(a.shape, a.dtype) for a in outs),
        in_specs=[any_space] * 5,
        out_specs=(any_space,) * 5,
        scratch_shapes=[vm(a.shape, a.dtype) for a in outs] + [dma((10,))],
        name="outputs",
    )(*outs)
    layer_out, grad_query, grad_key, grad_value, grad_weight = outs
    return (layer_out[None], grad_query[None], grad_key[None], grad_value[None], grad_weight)


def solution(mesh):
    rows = P("doc", "seq", None)
    flat = P("doc", None)
    return jax.shard_map(
        body,
        mesh=mesh,
        in_specs=(rows, rows, rows, rows, flat, flat, flat),
        out_specs=(rows, rows, rows, rows, flat),
        check_vma=False,
    )
```

```python
import math

import jax
import jax.numpy as jnp
from jax import lax
from jax.experimental import pallas as pl
from jax.experimental.pallas import tpu as pltpu
from jax.sharding import PartitionSpec as P

HEAD_DIM = 64
WINDOW = 512
BLOCK = 64
DOCS = 4
ROWS = 128
LANES = 128
SPAN = 9
SLOTS = 10
STEPS = 4
WIDTH = 1024
Z = 16
SIDES = (-1, 1)
OFFSETS = (-2, -1, 1, 2)
MESH = pl.DeviceIdType.MESH
BF16 = jnp.bfloat16
F32 = jnp.float32

NT = (((1,), (1,)), ((), ()))
TN = (((0,), (0,)), ((), ()))


def dot(a, b, dims=(((1,), (0,)), ((), ()))):
    return lax.dot_general(a, b, dims, preferred_element_type=F32)


def remote(src, dst, send, recv, device):
    return pltpu.make_async_remote_copy(
        src_ref=src, dst_ref=dst, send_sem=send, recv_sem=recv, device_id=device, device_id_type=MESH
    )


def layer_kernel(
    lengths, upweight, q_in, k_in, v_in, ct_in, w_in,
    lo_out, dq_out, dk_out, dv_out, gw_out,
    qbuf, kv, ctb, gout, wbuf, bias, attbuf, attpair, dqb, acc, own, rout, rin, fin,
    gkeep, g1send, g1recv, g2send, g2recv, g4f, g4send, g4recv, part, parts, zag, gwo, lob,
    s_scr, dp_scr, p_scr, ds_scr,
    l_sem, y_send, y_recv, ct_send, ct_recv, z_send, z_recv, zf_send, zf_recv, wx_send, wx_recv,
    wc_send, wc_recv, wy_send, wy_recv, r_send, r_recv, a_send, a_recv,
    dq_send, dq_recv, f_send, f_recv, o_sem, g1_send, g1_rsem, g2_send, g2_rsem,
    g3_send, g3_rsem, g4_send, g4_rsem, g5_send, g5_rsem,
):
    d = lax.axis_index("doc")
    s = lax.axis_index("seq")
    z, y = s // 2, s % 2
    yh, x, core = d // 8, (d // 2) % 4, d % 2
    s_pair = z * 2 + (1 - y)
    d_core = yh * 8 + x * 2 + (1 - core)
    d_far = (1 - yh) * 8 + x * 2 + core

    def at_x(offset):
        return yh * 8 + ((x + offset + 4) % 4) * 2 + core

    def at_z(offset):
        return ((z + offset + Z) % Z) * 2 + y

    def pair_of(step):
        return (x + 3 - step) % 4

    def cols(column, step):
        return pl.ds(pl.multiple_of((column * 4 + pair_of(step)) * LANES, LANES), LANES)

    pair_dev = (d, s_pair)
    core_dev = (d_core, s)
    far_dev = (d_far, s_pair)

    barrier = pltpu.get_barrier_semaphore()
    partners = [pair_dev, core_dev, far_dev, (d_far, s)] + [(at_x(o), s) for o in (1, 2, 3)]
    for device in partners:
        pl.semaphore_signal(barrier, inc=1, device_id=device, device_id_type=MESH)

    def greet(o, carry):
        pl.semaphore_signal(barrier, inc=1, device_id=(d, at_z(o)), device_id_type=MESH)
        return carry

    lax.fori_loop(1, Z, greet, 0)
    pl.semaphore_wait(barrier, len(partners) + Z - 1)

    def own_kv(i):
        mine = cols(y, i)
        return [
            pltpu.make_async_copy(k_in.at[:, mine], kv.at[i, 4 + y, 0], l_sem.at[i, 0]),
            pltpu.make_async_copy(v_in.at[:, mine], kv.at[i, 4 + y, 1], l_sem.at[i, 1]),
        ]

    def own_q(i):
        return pltpu.make_async_copy(q_in.at[:, cols(y, i)], qbuf.at[i, y], l_sem.at[i, 2])

    def pair_kv(i):
        theirs = cols(1 - y, i)
        return [
            remote(k_in.at[:, theirs], kv.at[i, 4 + y, 0], y_send.at[i, 0], y_recv.at[i, 0], pair_dev),
            remote(v_in.at[:, theirs], kv.at[i, 4 + y, 1], y_send.at[i, 1], y_recv.at[i, 1], pair_dev),
        ]

    def pair_q(i):
        return remote(
            q_in.at[:, cols(1 - y, i)], qbuf.at[i, y], y_send.at[i, 2], y_recv.at[i, 2], pair_dev
        )

    def take_kv(i):
        views = [kv.at[i, 5 - y, n] for n in range(2)]
        return [remote(views[n], views[n], y_send.at[i, n], y_recv.at[i, n], pair_dev) for n in range(2)]

    def take_q(i):
        here = qbuf.at[i, 1 - y]
        return remote(here, here, y_send.at[i, 2], y_recv.at[i, 2], pair_dev)

    def halo(i, n, far, arrival=False):
        o = SIDES[n]
        to = 4 - 2 * o * (2 if far else 1)
        here = to if arrival else (4 - 2 * o if far else 4)
        send, recv = (zf_send, zf_recv) if far else (z_send, z_recv)
        return remote(
            kv.at[i, pl.ds(here, 2)], kv.at[i, pl.ds(to, 2)], send.at[i, n], recv.at[i, n], (d, at_z(o))
        )

    own_ct = pltpu.make_async_copy(ct_in, ctb.at[y], l_sem.at[0, 3])
    own_w = pltpu.make_async_copy(w_in, wbuf.at[d], l_sem.at[1, 3])
    send_ct = remote(ct_in, ctb.at[y], ct_send, ct_recv, pair_dev)
    take_ct = remote(ctb.at[1 - y], ctb.at[1 - y], ct_send, ct_recv, pair_dev)

    def start_kv(i):
        for copy in own_kv(i) + pair_kv(i):
            copy.start()

    def start_q(i):
        own_q(i).start()
        pair_q(i).start()

    def start_near(i):
        for copy in own_kv(i):
            copy.wait()
        for copy in take_kv(i):
            copy.wait_recv()
        for n in range(2):
            halo(i, n, False).start()

    def forward(i):
        for n in range(2):
            halo(i, n, False, True).wait_recv()
            halo(i, n, True).start()

    start_kv(0)
    start_kv(1)
    start_q(0)
    own_w.start()
    for o in (1, 2, 3):
        remote(w_in, wbuf.at[d], wx_send.at[o - 1], wx_recv.at[o - 1], (at_x(o), s)).start()
    own_ct.start()
    start_near(0)
    start_kv(2)
    start_q(1)
    start_near(1)
    start_kv(3)
    start_q(2)
    start_q(3)
    send_ct.start()

    bounds = []
    total = jnp.int32(0)
    for j in range(DOCS):
        total = total + lengths[0, j] * BLOCK
        bounds.append(total)

    def doc_of(position):
        ids = jnp.zeros_like(position)
        for bound in bounds:
            ids = ids + (position >= bound).astype(jnp.int32)
        return ids

    for yp in range(2):
        base = (z * 2 + yp) * ROWS

        def fill(j, carry, yp=yp, base=base):
            rows = lax.broadcasted_iota(jnp.int32, (ROWS, ROWS), 0)
            lanes = lax.broadcasted_iota(jnp.int32, (ROWS, ROWS), 1)
            key = base - WINDOW + j * ROWS + rows
            query = base + lanes
            near = jnp.abs(query - key) <= WINDOW
            inside = (key >= 0) & (key < Z * 2 * ROWS)
            ok = near & inside & (doc_of(key) == doc_of(query))
            bias[yp, j] = jnp.where(ok, 0.0, -jnp.inf).astype(F32)
            return carry

        lax.fori_loop(0, SPAN, fill, 0)

    def w_block(high, o):
        return wbuf.at[high * 8 + ((x - o + 4) % 4) * 2 + core]

    own_w.wait()
    for o in range(4):
        block = w_block(yh, o)
        if o:
            remote(block, block, wx_send.at[o - 1], wx_recv.at[o - 1], (at_x(-o), s)).wait_recv()
        remote(block, block, wy_send.at[o], wy_recv.at[o], far_dev).start()
        remote(block, block, wc_send.at[o], wc_recv.at[o], core_dev).start()

    forward(0)
    start_near(2)

    def grad_out_rows():
        own_ct.wait()
        take_ct.wait_recv()
        for yp in range(2):
            position = (z * 2 + yp) * ROWS + lax.broadcasted_iota(jnp.int32, (ROWS, LANES), 0)
            ids = doc_of(position)
            weight = jnp.zeros((ROWS, LANES), jnp.int32)
            for j in range(DOCS):
                weight = weight + jnp.where(ids == j, upweight[0, j], 0)
            weight = weight.astype(F32)
            for j in range(WIDTH // LANES):
                piece = slice(j * LANES, (j + 1) * LANES)
                gout[yp, :, piece] = (weight * ctb[yp, :, piece].astype(F32)).astype(BF16)

    def projection_rows():
        for o in range(4):
            block = w_block(1 - yh, o)
            remote(block, block, wy_send.at[o], wy_recv.at[o], far_dev).wait_recv()
            remote(block, block, wc_send.at[4 + o], wc_recv.at[4 + o], core_dev).start()
        for o in range(4):
            for h, high in ((0, yh), (1, 1 - yh)):
                block = wbuf.at[high * 8 + ((x - o + 4) % 4) * 2 + (1 - core)]
                remote(block, block, wc_send.at[4 * h + o], wc_recv.at[4 * h + o], core_dev).wait_recv()

    lane = lax.broadcasted_iota(jnp.int32, (ROWS, LANES), 1)

    def stacked(block):
        block = block.astype(F32)
        low = jnp.where(lane < HEAD_DIM, block, 0.0).astype(BF16)
        high = jnp.where(lane >= HEAD_DIM, block, 0.0).astype(BF16)
        return jnp.concatenate([low, high], axis=0)

    def unstacked(block):
        return jnp.concatenate([block[:HEAD_DIM, :ROWS], block[HEAD_DIM:, ROWS:]], axis=0)

    def key_block(j):
        return slice(j * ROWS, (j + 1) * ROWS)

    def ahead(i, yp):
        query2 = stacked(qbuf[i, yp])
        peak = jnp.full((8, 2 * ROWS), -jnp.inf, F32)
        for j in range(SPAN):
            mask = bias[yp, j]
            score = dot(kv[i, yp + j, 0], query2, NT) + jnp.concatenate([mask, mask], axis=1)
            s_scr[i % 2, yp, key_block(j)] = score
            peak = jnp.maximum(peak, jnp.max(score.reshape(ROWS // 8, 8, 2 * ROWS), axis=0))
        peak = jnp.max(peak, axis=0, keepdims=True)
        norm = jnp.zeros((8, 2 * ROWS), F32)
        for j in range(SPAN):
            power = jnp.exp((s_scr[i % 2, yp, key_block(j)] - peak) * (HEAD_DIM ** -0.5))
            s_scr[i % 2, yp, key_block(j)] = power
            norm = norm + jnp.sum(power.reshape(ROWS // 8, 8, 2 * ROWS), axis=0)
        share = 1.0 / jnp.sum(norm, axis=0, keepdims=True)
        for j in range(SPAN):
            prob = s_scr[i % 2, yp, key_block(j)] * share
            s_scr[i % 2, yp, key_block(j)] = prob
            p_scr[i % 2, yp, key_block(j)] = prob.astype(BF16)
        values = kv[i, yp:yp + SPAN, 1].reshape(SPAN * ROWS, LANES)
        mixed = unstacked(dot(values, p_scr[i % 2, yp], TN))
        attpair[i, yp] = mixed.T.astype(BF16)

    def back(i, yp, w_pair):
        query2 = stacked(qbuf[i, yp])
        grad2 = stacked(dot(gout[yp], w_pair, NT).astype(BF16))
        centre = jnp.zeros((8, 2 * ROWS), F32)
        for j in range(SPAN):
            slope = dot(kv[i, yp + j, 1], grad2, NT)
            dp_scr[key_block(j)] = slope
            weighted = s_scr[i % 2, yp, key_block(j)] * slope
            centre = centre + jnp.sum(weighted.reshape(ROWS // 8, 8, 2 * ROWS), axis=0)
        centre = jnp.sum(centre, axis=0, keepdims=True)
        for j in range(SPAN):
            prob = s_scr[i % 2, yp, key_block(j)]
            grad_score = (prob * (dp_scr[key_block(j)] - centre) * (HEAD_DIM ** -0.5)).astype(BF16)
            ds_scr[key_block(j)] = grad_score
            key_part = dot(grad_score, query2)
            value_part = dot(p_scr[i % 2, yp, key_block(j)], grad2)
            if yp == 0:
                acc[j, 0] = key_part
                acc[j, 1] = value_part
            elif j + 1 < SPAN:
                acc[j + 1, 0] += key_part
                acc[j + 1, 1] += value_part
            else:
                acc[j + 1, 0] = key_part
                acc[j + 1, 1] = value_part
        keys = kv[i, yp:yp + SPAN, 0].reshape(SPAN * ROWS, LANES)
        dqb[i, yp] = unstacked(dot(keys, ds_scr[...], TN)).T.astype(BF16)

    def att_send(i):
        return remote(
            attpair.at[i, 1 - y], attbuf.at[y * 4 + pair_of(i)], a_send.at[i], a_recv.at[i], pair_dev
        )

    def att_take(i):
        here = attbuf.at[(1 - y) * 4 + pair_of(i)]
        return remote(here, here, a_send.at[i], a_recv.at[i], pair_dev)

    def dq_own(i):
        return pltpu.make_async_copy(dqb.at[i, y], dq_out.at[:, cols(y, i)], o_sem.at[i, 0])

    def dq_pair(i):
        return remote(dqb.at[i, 1 - y], dq_out.at[:, cols(y, i)], dq_send.at[i], dq_recv.at[i], pair_dev)

    def dq_take(i):
        here = dq_out.at[:, cols(1 - y, i)]
        return remote(here, here, dq_send.at[i], dq_recv.at[i], pair_dev)

    def ret_copy(i, n):
        return remote(rout.at[i, n], rin.at[i, n], r_send.at[i, n], r_recv.at[i, n], (d, at_z(OFFSETS[n])))

    def g1_copy(i):
        return remote(g1send.at[i], g1recv.at[i], g1_send.at[i], g1_rsem.at[i], core_dev)

    def g2_copy(i):
        return remote(g2send.at[i], g2recv.at[i], g2_send.at[i], g2_rsem.at[i], (at_x(-1 - i), s))

    def g2_start(i):
        g1_copy(i).wait_recv()
        g2send[i] = (gkeep[i, core] + g1recv[i].astype(F32)).astype(BF16)
        g2_copy(i).start()

    def fin_own(i):
        return [
            pltpu.make_async_copy(fin.at[i, y, n], out.at[:, cols(y, i)], o_sem.at[i, 1 + n])
            for n, out in ((0, dk_out), (1, dv_out))
        ]

    def fin_pair(i):
        return [
            remote(fin.at[i, 1 - y, n], out.at[:, cols(y, i)], f_send.at[i, n], f_recv.at[i, n], pair_dev)
            for n, out in ((0, dk_out), (1, dv_out))
        ]

    def fin_take(i):
        views = [out.at[:, cols(1 - y, i)] for out in (dk_out, dv_out)]
        return [remote(views[n], views[n], f_send.at[i, n], f_recv.at[i, n], pair_dev) for n in range(2)]

    def finish(i):
        total = own[i]
        for n in range(4):
            ret_copy(i, n).wait_recv()
            total = total + rin[i, n].astype(F32)
        fin[i] = total.astype(BF16)
        for copy in fin_pair(i) + fin_own(i):
            copy.start()

    def g4_copy(o):
        return remote(g4send.at[(z + o) % Z], g4recv.at[o], g4_send.at[o], g4_rsem.at[o], (d, at_z(o)))

    def head_sum():
        g1_copy(3).wait_recv()
        head = gkeep[3, core] + g1recv[3].astype(F32)
        for i in range(3):
            remote(g2recv.at[i], g2recv.at[i], g2_send.at[i], g2_rsem.at[i], (at_x(1 + i), s)).wait_recv()
            head = head + g2recv[i].astype(F32)
        for j in range(8):
            for half in range(2):
                g4f[2 * j + half] = head[half * 32:half * 32 + 32, j * LANES:(j + 1) * LANES]
        g4send[...] = g4f[...].astype(BF16)

        def g4_start(o, carry):
            g4_copy(o).start()
            return carry

        lax.fori_loop(1, Z, g4_start, 0)

    def weigh(i):
        weight_part = dot(attpair[i, 0], gout[0], TN) + dot(attpair[i, 1], gout[1], TN)
        gkeep[i, 0] = weight_part[:HEAD_DIM]
        gkeep[i, 1] = weight_part[HEAD_DIM:]
        g1send[i] = gkeep[i, 1 - core].astype(BF16)
        g1_copy(i).start()

    def step(i, carry):
        @pl.when(i < 3)
        def _():
            forward(i + 1)

        @pl.when(i == 0)
        def _():
            start_near(3)

        @pl.when(i == 2)
        def _():
            g2_start(0)

        @pl.when((i > 1) & (i < STEPS))
        def _():
            g2_start(i - 1)

        @pl.when(i < STEPS)
        def _():
            own_q(i).wait()
            take_q(i).wait_recv()
            for n in range(2):
                halo(i, n, True, True).wait_recv()
            for yp in range(2):
                ahead(i, yp)
            att_send(i).start()
            attbuf[y * 4 + pair_of(i)] = attpair[i, y]

        @pl.when(i == 1)
        def _():
            grad_out_rows()
            weigh(0)

        @pl.when((i > 0) & (i < STEPS))
        def _():
            weigh(i)

        @pl.when(i == 1)
        def _():
            projection_rows()

        @pl.when(i == STEPS)
        def _():
            head_sum()

        @pl.when(i > 0)
        def _():
            behind(i - 1)

        return carry

    def behind(i):
        doc_row = y * 8 + pair_of(i) * 2
        w_pair = wbuf[pl.ds(doc_row, 2)].reshape(2 * HEAD_DIM, WIDTH)
        back(i, 0, w_pair)
        back(i, 1, w_pair)
        for n in range(4):
            first = 4 + 2 * OFFSETS[n]
            rout[i, n] = acc[first:first + 2].astype(BF16)
            ret_copy(i, n).start()
        own[i] = acc[4:6]
        dq_own(i).start()
        dq_pair(i).start()

        @pl.when(i > 1)
        def _():
            finish(i - 2)

    lax.fori_loop(0, STEPS + 1, step, 0)

    for i in range(STEPS):
        att_take(i).wait_recv()
    rows = jnp.concatenate([attbuf[j] for j in range(8)], axis=1)
    for j in range(4):
        piece = slice(j * 256, (j + 1) * 256)
        lob[:, piece] = dot(rows, wbuf[:, :, piece].reshape(WIDTH, 256)).astype(BF16)
    lo_copy = pltpu.make_async_copy(lob, lo_out, o_sem.at[0, 3])
    lo_copy.start()
    finish(2)

    def g4_wait(o, total):
        g4_copy(o).wait_recv()
        return total + g4recv[o].astype(F32)

    part[...] = lax.fori_loop(1, Z, g4_wait, g4f[z])

    def g3_copy(n, device):
        slot = (yh + y) % 2
        return remote(part, parts.at[slot], g3_send.at[n], g3_rsem.at[slot], device)

    def g3_take(slot):
        return remote(parts.at[slot], parts.at[slot], g3_send.at[0], g3_rsem.at[slot], pair_dev)

    @pl.when(yh == y)
    def _():
        g3_copy(0, pair_dev).start()
        parts[0] = part[...]

    @pl.when(yh != y)
    def _():
        g3_copy(0, far_dev).start()
        g3_copy(1, (d_far, s)).start()

    finish(3)

    @pl.when(yh == y)
    def _():
        g3_take(1).wait_recv()
        g3_copy(0, pair_dev).wait_send()

    @pl.when(yh != y)
    def _():
        g3_take(0).wait_recv()
        g3_take(1).wait_recv()
        g3_copy(0, far_dev).wait_send()
        g3_copy(1, (d_far, s)).wait_send()

    zag[z] = ((parts[0] + parts[1]) * (1.0 / math.sqrt(Z * 2 * ROWS * 16))).astype(BF16)

    def g5_copy(o):
        return remote(zag.at[z], zag.at[z], g5_send.at[o], g5_rsem.at[o], (d, at_z(o)))

    def g5_take(o):
        here = zag.at[(z - o + Z) % Z]
        return remote(here, here, g5_send.at[o], g5_rsem.at[o], (d, at_z(o)))

    def g5_start(o, carry):
        g5_copy(o).start()
        return carry

    lax.fori_loop(1, Z, g5_start, 0)

    def g5_wait(o, carry):
        g5_take(o).wait_recv()
        return carry

    lax.fori_loop(1, Z, g5_wait, 0)
    for j in range(8):
        for half in range(2):
            gwo[half * 32:half * 32 + 32, j * LANES:(j + 1) * LANES] = zag[2 * j + half].astype(F32)
    gw_copy = pltpu.make_async_copy(gwo, gw_out, o_sem.at[1, 3])
    gw_copy.start()

    def drain(i, carry):
        for copy in pair_kv(i):
            copy.wait_send()
        pair_q(i).wait_send()
        for n in range(2):
            halo(i, n, False).wait_send()
            halo(i, n, True).wait_send()
        for n in range(4):
            ret_copy(i, n).wait_send()
        att_send(i).wait_send()
        dq_own(i).wait()
        dq_pair(i).wait_send()
        dq_take(i).wait_recv()
        g1_copy(i).wait_send()
        for copy in fin_own(i):
            copy.wait()
        for copy in fin_pair(i):
            copy.wait_send()
        for copy in fin_take(i):
            copy.wait_recv()
        return carry

    lax.fori_loop(0, STEPS, drain, 0)
    send_ct.wait_send()
    for o in (1, 2, 3):
        remote(w_in, wbuf.at[d], wx_send.at[o - 1], wx_recv.at[o - 1], (at_x(o), s)).wait_send()
        g2_copy(o - 1).wait_send()
    for o in range(4):
        block = w_block(yh, o)
        remote(block, block, wy_send.at[o], wy_recv.at[o], far_dev).wait_send()
        remote(block, block, wc_send.at[o], wc_recv.at[o], core_dev).wait_send()
        block = w_block(1 - yh, o)
        remote(block, block, wc_send.at[4 + o], wc_recv.at[4 + o], core_dev).wait_send()

    def drain_pieces(o, carry):
        g4_copy(o).wait_send()
        g5_copy(o).wait_send()
        return carry

    lax.fori_loop(1, Z, drain_pieces, 0)
    lo_copy.wait()
    gw_copy.wait()


def copy_kernel(*refs):
    sources, targets, rooms, sems = refs[:5], refs[5:10], refs[10:15], refs[15]
    loads = [pltpu.make_async_copy(sources[n], rooms[n], sems.at[n]) for n in range(5)]
    stores = [pltpu.make_async_copy(rooms[n], targets[n], sems.at[5 + n]) for n in range(5)]
    for load in loads:
        load.start()
    for load, store in zip(loads, stores):
        load.wait()
        store.start()
    for store in stores:
        store.wait()


def body(queries, key_rows, value_rows, cotangent, out_weight, lengths, upweight):
    vm = pltpu.VMEM
    dma = pltpu.SemaphoreType.DMA
    block = (ROWS, LANES)
    any_space = pl.BlockSpec(memory_space=pl.ANY)
    scalar = pl.BlockSpec(memory_space=pltpu.SMEM)
    rows_shape = jax.ShapeDtypeStruct((ROWS, WIDTH), BF16)
    outs = pl.pallas_call(
        layer_kernel,
        out_shape=(rows_shape,) * 4 + (jax.ShapeDtypeStruct((HEAD_DIM, WIDTH), F32),),
        in_specs=[scalar, scalar] + [any_space] * 5,
        out_specs=(any_space,) * 5,
        scratch_shapes=[
            vm((STEPS, 2) + block, BF16),
            vm((STEPS, SLOTS, 2) + block, BF16),
            vm((2, ROWS, WIDTH), BF16),
            vm((2, ROWS, WIDTH), BF16),
            vm((16, HEAD_DIM, WIDTH), BF16),
            vm((2, SPAN) + block, F32),
            vm((8,) + block, BF16),
            vm((STEPS, 2) + block, BF16),
            vm((STEPS, 2) + block, BF16),
            vm((SLOTS, 2) + block, F32),
            vm((STEPS, 2, 2) + block, F32),
            vm((STEPS, 4, 2, 2) + block, BF16),
            vm((STEPS, 4, 2, 2) + block, BF16),
            vm((STEPS, 2, 2) + block, BF16),
            vm((STEPS, 2, HEAD_DIM, WIDTH), F32),
            vm((STEPS, HEAD_DIM, WIDTH), BF16),
            vm((STEPS, HEAD_DIM, WIDTH), BF16),
            vm((3, HEAD_DIM, WIDTH), BF16),
            vm((3, HEAD_DIM, WIDTH), BF16),
            vm((Z, 32, LANES), F32),
            vm((Z, 32, LANES), BF16),
            vm((Z, 32, LANES), BF16),
            vm((32, LANES), F32),
            vm((2, 32, LANES), F32),
            vm((Z, 32, LANES), BF16),
            vm((HEAD_DIM, WIDTH), F32),
            vm((ROWS, WIDTH), BF16),
            vm((2, 2, SPAN * ROWS, 2 * ROWS), F32),
            vm((SPAN * ROWS, 2 * ROWS), F32),
            vm((2, 2, SPAN * ROWS, 2 * ROWS), BF16),
            vm((SPAN * ROWS, 2 * ROWS), BF16),
            dma((STEPS, 4)),
            dma((STEPS, 3)), dma((STEPS, 3)),
            dma, dma,
            dma((STEPS, 2)), dma((STEPS, 2)),
            dma((STEPS, 2)), dma((STEPS, 2)),
            dma((3,)), dma((3,)),
            dma((8,)), dma((8,)),
            dma((4,)), dma((4,)),
            dma((STEPS, 4)), dma((STEPS, 4)),
            dma((STEPS,)), dma((STEPS,)),
            dma((STEPS,)), dma((STEPS,)),
            dma((STEPS, 2)), dma((STEPS, 2)),
            dma((STEPS, 4)),
            dma((STEPS,)), dma((STEPS,)),
            dma((3,)), dma((3,)),
            dma((2,)), dma((2,)),
            dma((Z,)), dma((Z,)),
            dma((Z,)), dma((Z,)),
        ],
        compiler_params=pltpu.CompilerParams(
            collective_id=0, has_side_effects=True, vmem_limit_bytes=56 * 2**20
        ),
        name="layer",
    )(lengths, upweight, queries[0], key_rows[0], value_rows[0], cotangent[0], out_weight)
    outs = pl.pallas_call(
        copy_kernel,
        out_shape=tuple(jax.ShapeDtypeStruct(a.shape, a.dtype) for a in outs),
        in_specs=[any_space] * 5,
        out_specs=(any_space,) * 5,
        scratch_shapes=[vm(a.shape, a.dtype) for a in outs] + [dma((10,))],
        name="outputs",
    )(*outs)
    layer_out, grad_query, grad_key, grad_value, grad_weight = outs
    return (layer_out[None], grad_query[None], grad_key[None], grad_value[None], grad_weight)


def solution(mesh):
    rows = P("doc", "seq", None)
    flat = P("doc", None)
    return jax.shard_map(
        body,
        mesh=mesh,
        in_specs=(rows, rows, rows, rows, flat, flat, flat),
        out_specs=(rows, rows, rows, rows, flat),
        check_vma=False,
    )
```

```python
import math

import jax
import jax.numpy as jnp
from jax import lax
from jax.experimental import pallas as pl
from jax.experimental.pallas import tpu as pltpu
from jax.sharding import PartitionSpec as P

HEAD_DIM = 64
WINDOW = 512
BLOCK = 64
DOCS = 4
ROWS = 128
LANES = 128
SPAN = 9
SLOTS = 10
STEPS = 4
WIDTH = 1024
Z = 16
SIDES = (-1, 1)
MESH = pl.DeviceIdType.MESH
BF16 = jnp.bfloat16
F32 = jnp.float32

NT = (((1,), (1,)), ((), ()))
TN = (((0,), (0,)), ((), ()))


def dot(a, b, dims=(((1,), (0,)), ((), ()))):
    return lax.dot_general(a, b, dims, preferred_element_type=F32)


def remote(src, dst, send, recv, device):
    return pltpu.make_async_remote_copy(
        src_ref=src, dst_ref=dst, send_sem=send, recv_sem=recv, device_id=device, device_id_type=MESH
    )


def layer_kernel(
    lengths, upweight, q_in, k_in, v_in, ct_in, w_in,
    lo_out, dq_out, dk_out, dv_out, gw_out,
    qbuf, kv, ctb, gout, wbuf, bias, attbuf, attpair, dqb, acc, own, fout, fhere, rout, rin, fin,
    near, gkeep, g1send, g1recv, g2send, g2recv, g2sum, g3send, g3recv, g4f, g4send, g4recv, zag, gwh, gwo, lob,
    s_scr, dp_scr, p_scr, ds_scr,
    l_sem, y_send, y_recv, ct_send, ct_recv, z_send, z_recv, zf_send, zf_recv, wx_send, wx_recv,
    wc_send, wc_recv, wy_send, wy_recv, r_send, r_recv, rf_send, rf_recv, a_send, a_recv,
    dq_send, dq_recv, f_send, f_recv, o_sem, g1_send, g1_rsem, g2_send, g2_rsem,
    g3_send, g3_rsem, g4_send, g4_rsem, g5_send, g5_rsem, g6_send, g6_rsem,
):
    d = lax.axis_index("doc")
    s = lax.axis_index("seq")
    z, y = s // 2, s % 2
    yh, x, core = d // 8, (d // 2) % 4, d % 2
    s_pair = z * 2 + (1 - y)
    d_core = yh * 8 + x * 2 + (1 - core)
    d_far = (1 - yh) * 8 + x * 2 + core

    def at_x(offset):
        return yh * 8 + ((x + offset + 4) % 4) * 2 + core

    def at_z(offset):
        return ((z + offset + Z) % Z) * 2 + y

    def pair_of(step):
        return (x + 3 - step) % 4

    def cols(column, step):
        return pl.ds(pl.multiple_of((column * 4 + pair_of(step)) * LANES, LANES), LANES)

    pair_dev = (d, s_pair)
    core_dev = (d_core, s)
    far_dev = (d_far, s_pair)

    barrier = pltpu.get_barrier_semaphore()
    partners = [pair_dev, core_dev, far_dev, (d_far, s)] + [(at_x(o), s) for o in (1, 2, 3)]
    for device in partners:
        pl.semaphore_signal(barrier, inc=1, device_id=device, device_id_type=MESH)

    def greet(o, carry):
        pl.semaphore_signal(barrier, inc=1, device_id=(d, at_z(o)), device_id_type=MESH)
        return carry

    lax.fori_loop(1, Z, greet, 0)
    pl.semaphore_wait(barrier, len(partners) + Z - 1)

    def own_kv(i):
        mine = cols(y, i)
        return [
            pltpu.make_async_copy(k_in.at[:, mine], kv.at[i, 4 + y, 0], l_sem.at[i, 0]),
            pltpu.make_async_copy(v_in.at[:, mine], kv.at[i, 4 + y, 1], l_sem.at[i, 1]),
        ]

    def own_q(i):
        return pltpu.make_async_copy(q_in.at[:, cols(y, i)], qbuf.at[i, y], l_sem.at[i, 2])

    def pair_kv(i):
        theirs = cols(1 - y, i)
        return [
            remote(k_in.at[:, theirs], kv.at[i, 4 + y, 0], y_send.at[i, 0], y_recv.at[i, 0], pair_dev),
            remote(v_in.at[:, theirs], kv.at[i, 4 + y, 1], y_send.at[i, 1], y_recv.at[i, 1], pair_dev),
        ]

    def pair_q(i):
        return remote(
            q_in.at[:, cols(1 - y, i)], qbuf.at[i, y], y_send.at[i, 2], y_recv.at[i, 2], pair_dev
        )

    def take_kv(i):
        views = [kv.at[i, 5 - y, n] for n in range(2)]
        return [remote(views[n], views[n], y_send.at[i, n], y_recv.at[i, n], pair_dev) for n in range(2)]

    def take_q(i):
        here = qbuf.at[i, 1 - y]
        return remote(here, here, y_send.at[i, 2], y_recv.at[i, 2], pair_dev)

    def halo(i, n, far, arrival=False):
        o = SIDES[n]
        to = 4 - 2 * o * (2 if far else 1)
        here = to if arrival else (4 - 2 * o if far else 4)
        send, recv = (zf_send, zf_recv) if far else (z_send, z_recv)
        return remote(
            kv.at[i, pl.ds(here, 2)], kv.at[i, pl.ds(to, 2)], send.at[i, n], recv.at[i, n], (d, at_z(o))
        )

    own_ct = pltpu.make_async_copy(ct_in, ctb.at[y], l_sem.at[0, 3])
    own_w = pltpu.make_async_copy(w_in, wbuf.at[d], l_sem.at[1, 3])
    send_ct = remote(ct_in, ctb.at[y], ct_send, ct_recv, pair_dev)
    take_ct = remote(ctb.at[1 - y], ctb.at[1 - y], ct_send, ct_recv, pair_dev)

    def start_kv(i):
        for copy in own_kv(i) + pair_kv(i):
            copy.start()

    def start_q(i):
        own_q(i).start()
        pair_q(i).start()

    def start_near(i):
        for copy in own_kv(i):
            copy.wait()
        for copy in take_kv(i):
            copy.wait_recv()
        for n in range(2):
            halo(i, n, False).start()

    def forward(i):
        for n in range(2):
            halo(i, n, False, True).wait_recv()
            halo(i, n, True).start()

    start_kv(0)
    start_kv(1)
    start_q(0)
    own_w.start()
    for o in (1, 2, 3):
        remote(w_in, wbuf.at[d], wx_send.at[o - 1], wx_recv.at[o - 1], (at_x(o), s)).start()
    own_ct.start()
    start_near(0)
    start_kv(2)
    start_q(1)
    start_near(1)
    start_kv(3)
    start_q(2)
    start_q(3)
    send_ct.start()

    bounds = []
    total = jnp.int32(0)
    for j in range(DOCS):
        total = total + lengths[0, j] * BLOCK
        bounds.append(total)

    def doc_of(position):
        ids = jnp.zeros_like(position)
        for bound in bounds:
            ids = ids + (position >= bound).astype(jnp.int32)
        return ids

    for yp in range(2):
        base = (z * 2 + yp) * ROWS

        def fill(j, carry, yp=yp, base=base):
            rows = lax.broadcasted_iota(jnp.int32, (ROWS, ROWS), 0)
            lanes = lax.broadcasted_iota(jnp.int32, (ROWS, ROWS), 1)
            key = base - WINDOW + j * ROWS + rows
            query = base + lanes
            near = jnp.abs(query - key) <= WINDOW
            inside = (key >= 0) & (key < Z * 2 * ROWS)
            ok = near & inside & (doc_of(key) == doc_of(query))
            bias[yp, j] = jnp.where(ok, 0.0, -jnp.inf).astype(F32)
            return carry

        lax.fori_loop(0, SPAN, fill, 0)

    def w_block(high, o):
        return wbuf.at[high * 8 + ((x - o + 4) % 4) * 2 + core]

    own_w.wait()
    for o in range(4):
        block = w_block(yh, o)
        if o:
            remote(block, block, wx_send.at[o - 1], wx_recv.at[o - 1], (at_x(-o), s)).wait_recv()
        remote(block, block, wy_send.at[o], wy_recv.at[o], far_dev).start()
        remote(block, block, wc_send.at[o], wc_recv.at[o], core_dev).start()

    forward(0)
    start_near(2)

    def grad_out_rows():
        own_ct.wait()
        take_ct.wait_recv()
        for yp in range(2):
            position = (z * 2 + yp) * ROWS + lax.broadcasted_iota(jnp.int32, (ROWS, LANES), 0)
            ids = doc_of(position)
            weight = jnp.zeros((ROWS, LANES), jnp.int32)
            for j in range(DOCS):
                weight = weight + jnp.where(ids == j, upweight[0, j], 0)
            weight = weight.astype(F32)
            for j in range(WIDTH // LANES):
                piece = slice(j * LANES, (j + 1) * LANES)
                gout[yp, :, piece] = (weight * ctb[yp, :, piece].astype(F32)).astype(BF16)

    def projection_rows():
        for o in range(4):
            block = w_block(1 - yh, o)
            remote(block, block, wy_send.at[o], wy_recv.at[o], far_dev).wait_recv()
            remote(block, block, wc_send.at[4 + o], wc_recv.at[4 + o], core_dev).start()
        for o in range(4):
            for h, high in ((0, yh), (1, 1 - yh)):
                block = wbuf.at[high * 8 + ((x - o + 4) % 4) * 2 + (1 - core)]
                remote(block, block, wc_send.at[4 * h + o], wc_recv.at[4 * h + o], core_dev).wait_recv()

    lane = lax.broadcasted_iota(jnp.int32, (ROWS, LANES), 1)

    def stacked(block):
        block = block.astype(F32)
        low = jnp.where(lane < HEAD_DIM, block, 0.0).astype(BF16)
        high = jnp.where(lane >= HEAD_DIM, block, 0.0).astype(BF16)
        return jnp.concatenate([low, high], axis=0)

    def unstacked(block):
        return jnp.concatenate([block[:HEAD_DIM, :ROWS], block[HEAD_DIM:, ROWS:]], axis=0)

    def key_block(j):
        return slice(j * ROWS, (j + 1) * ROWS)

    def ahead(i, yp):
        query2 = stacked(qbuf[i, yp])
        peak = jnp.full((8, 2 * ROWS), -jnp.inf, F32)
        for j in range(SPAN):
            mask = bias[yp, j]
            score = dot(kv[i, yp + j, 0], query2, NT) + jnp.concatenate([mask, mask], axis=1)
            s_scr[yp, key_block(j)] = score
            peak = jnp.maximum(peak, jnp.max(score.reshape(ROWS // 8, 8, 2 * ROWS), axis=0))
        peak = jnp.max(peak, axis=0, keepdims=True)
        norm = jnp.zeros((8, 2 * ROWS), F32)
        for j in range(SPAN):
            power = jnp.exp((s_scr[yp, key_block(j)] - peak) * (HEAD_DIM ** -0.5))
            s_scr[yp, key_block(j)] = power
            norm = norm + jnp.sum(power.reshape(ROWS // 8, 8, 2 * ROWS), axis=0)
        share = 1.0 / jnp.sum(norm, axis=0, keepdims=True)
        for j in range(SPAN):
            prob = s_scr[yp, key_block(j)] * share
            s_scr[yp, key_block(j)] = prob
            p_scr[yp, key_block(j)] = prob.astype(BF16)
        values = kv[i, yp:yp + SPAN, 1].reshape(SPAN * ROWS, LANES)
        mixed = unstacked(dot(values, p_scr[yp], TN))
        attpair[i, yp] = mixed.T.astype(BF16)
        return mixed.astype(BF16)

    def back(i, yp, w_pair):
        query2 = stacked(qbuf[i, yp])
        grad2 = stacked(dot(gout[yp], w_pair, NT).astype(BF16))
        centre = jnp.zeros((8, 2 * ROWS), F32)
        for j in range(SPAN):
            slope = dot(kv[i, yp + j, 1], grad2, NT)
            dp_scr[key_block(j)] = slope
            weighted = s_scr[yp, key_block(j)] * slope
            centre = centre + jnp.sum(weighted.reshape(ROWS // 8, 8, 2 * ROWS), axis=0)
        centre = jnp.sum(centre, axis=0, keepdims=True)
        for j in range(SPAN):
            prob = s_scr[yp, key_block(j)]
            grad_score = (prob * (dp_scr[key_block(j)] - centre) * (HEAD_DIM ** -0.5)).astype(BF16)
            ds_scr[key_block(j)] = grad_score
            key_part = dot(grad_score, query2)
            value_part = dot(p_scr[yp, key_block(j)], grad2)
            if yp == 0:
                acc[j, 0] = key_part
                acc[j, 1] = value_part
            elif j + 1 < SPAN:
                acc[j + 1, 0] += key_part
                acc[j + 1, 1] += value_part
            else:
                acc[j + 1, 0] = key_part
                acc[j + 1, 1] = value_part
        keys = kv[i, yp:yp + SPAN, 0].reshape(SPAN * ROWS, LANES)
        dqb[i, yp] = unstacked(dot(keys, ds_scr[...], TN)).T.astype(BF16)

    def att_send(i):
        return remote(
            attpair.at[i, 1 - y], attbuf.at[y * 4 + pair_of(i)], a_send.at[i], a_recv.at[i], pair_dev
        )

    def att_take(i):
        here = attbuf.at[(1 - y) * 4 + pair_of(i)]
        return remote(here, here, a_send.at[i], a_recv.at[i], pair_dev)

    def dq_own(i):
        return pltpu.make_async_copy(dqb.at[i, y], dq_out.at[:, cols(y, i)], o_sem.at[i, 0])

    def dq_pair(i):
        return remote(dqb.at[i, 1 - y], dq_out.at[:, cols(y, i)], dq_send.at[i], dq_recv.at[i], pair_dev)

    def dq_take(i):
        here = dq_out.at[:, cols(1 - y, i)]
        return remote(here, here, dq_send.at[i], dq_recv.at[i], pair_dev)

    def far_copy(i, n):
        return remote(fout.at[i, n], fhere.at[i, n], rf_send.at[i, n], rf_recv.at[i, n], (d, at_z(SIDES[n])))

    def ret_copy(i, n):
        return remote(rout.at[i, n], rin.at[i, n], r_send.at[i, n], r_recv.at[i, n], (d, at_z(SIDES[n])))

    def ret_start(i):
        for n in range(2):
            far_copy(i, n).wait_recv()
            rout[i, n] = (near[i, n] + fhere[i, n].astype(F32)).astype(BF16)
            ret_copy(i, n).start()

    def g1_copy(i):
        return remote(g1send.at[i], g1recv.at[i], g1_send.at[i], g1_rsem.at[i], core_dev)

    def g2_copy(i):
        return remote(g2send.at[i], g2recv.at[i], g2_send.at[i], g2_rsem.at[i], (at_x(-1 - i), s))

    def g2_start(i):
        g1_copy(i).wait_recv()
        g2send[i] = (gkeep[i, core] + g1recv[i].astype(F32)).astype(BF16)
        g2_copy(i).start()

    def fin_own(i):
        return [
            pltpu.make_async_copy(fin.at[i, y, n], out.at[:, cols(y, i)], o_sem.at[i, 1 + n])
            for n, out in ((0, dk_out), (1, dv_out))
        ]

    def fin_pair(i):
        return [
            remote(fin.at[i, 1 - y, n], out.at[:, cols(y, i)], f_send.at[i, n], f_recv.at[i, n], pair_dev)
            for n, out in ((0, dk_out), (1, dv_out))
        ]

    def fin_take(i):
        views = [out.at[:, cols(1 - y, i)] for out in (dk_out, dv_out)]
        return [remote(views[n], views[n], f_send.at[i, n], f_recv.at[i, n], pair_dev) for n in range(2)]

    def finish(i):
        total = own[i]
        for n in range(2):
            ret_copy(i, n).wait_recv()
            total = total + rin[i, n].astype(F32)
        fin[i] = total.astype(BF16)
        for copy in fin_pair(i) + fin_own(i):
            copy.start()

    def g4_copy(o):
        return remote(g4send.at[(z + o) % Z], g4recv.at[o], g4_send.at[o], g4_rsem.at[o], (d, at_z(o)))

    def head_sum():
        g1_copy(3).wait_recv()
        head = gkeep[3, core] + g1recv[3].astype(F32)
        for i in range(3):
            remote(g2recv.at[i], g2recv.at[i], g2_send.at[i], g2_rsem.at[i], (at_x(1 + i), s)).wait_recv()
            head = head + g2recv[i].astype(F32)
        for j in range(8):
            g2sum[j] = head[:, j * LANES:(j + 1) * LANES]
        g3send[...] = g2sum[pl.ds((1 - yh) * 4, 4)].astype(BF16)
        g3.start()

    g3 = remote(g3send, g3recv, g3_send, g3_rsem, (d_far, s))

    def z_pieces():
        g3.wait_recv()
        half_sum = g2sum[pl.ds(yh * 4, 4)] + g3recv[...].astype(F32)
        g4f[...] = half_sum.reshape(Z, 16, LANES)
        g4send[...] = g4f[...].astype(BF16)

        def g4_start(o, carry):
            g4_copy(o).start()
            return carry

        lax.fori_loop(1, Z, g4_start, 0)

    def step(i, carry):
        @pl.when(i < 3)
        def _():
            forward(i + 1)

        @pl.when(i == 0)
        def _():
            start_near(3)

        @pl.when(i > 0)
        def _():
            g2_start(i - 1)

        own_q(i).wait()
        take_q(i).wait_recv()
        for n in range(2):
            halo(i, n, True, True).wait_recv()
        mixed = [ahead(i, yp) for yp in range(2)]
        att_send(i).start()
        attbuf[y * 4 + pair_of(i)] = attpair[i, y]

        @pl.when(i == 0)
        def _():
            grad_out_rows()

        weight_part = dot(mixed[0], gout[0]) + dot(mixed[1], gout[1])
        gkeep[i, 0] = weight_part[:HEAD_DIM]
        gkeep[i, 1] = weight_part[HEAD_DIM:]
        g1send[i] = gkeep[i, 1 - core].astype(BF16)
        g1_copy(i).start()

        @pl.when(i == 0)
        def _():
            projection_rows()

        doc_row = y * 8 + pair_of(i) * 2
        w_pair = wbuf[pl.ds(doc_row, 2)].reshape(2 * HEAD_DIM, WIDTH)
        back(i, 0, w_pair)

        @pl.when(i == 3)
        def _():
            head_sum()

        back(i, 1, w_pair)
        for n in range(2):
            first = 8 * n
            fout[i, n] = acc[first:first + 2].astype(BF16)
            far_copy(i, n).start()
            near[i, n] = acc[2 + 4 * n:4 + 4 * n]
        own[i] = acc[4:6]
        dq_own(i).start()
        dq_pair(i).start()

        @pl.when(i == 3)
        def _():
            z_pieces()

        @pl.when(i > 0)
        def _():
            ret_start(i - 1)

        @pl.when(i > 1)
        def _():
            finish(i - 2)

        return carry

    lax.fori_loop(0, STEPS, step, 0)
    ret_start(3)
    finish(2)

    for i in range(STEPS):
        att_take(i).wait_recv()
    rows = jnp.concatenate([attbuf[j] for j in range(8)], axis=1)
    for j in range(4):
        piece = slice(j * 256, (j + 1) * 256)
        lob[:, piece] = dot(rows, wbuf[:, :, piece].reshape(WIDTH, 256)).astype(BF16)
    lo_copy = pltpu.make_async_copy(lob, lo_out, o_sem.at[0, 3])
    lo_copy.start()

    def g4_wait(o, total):
        g4_copy(o).wait_recv()
        return total + g4recv[o].astype(F32)

    piece_sum = lax.fori_loop(1, Z, g4_wait, g4f[z])
    zag[z] = (piece_sum * (1.0 / math.sqrt(Z * 2 * ROWS * 16))).astype(BF16)

    def g5_copy(o):
        return remote(zag.at[z], zag.at[z], g5_send.at[o], g5_rsem.at[o], (d, at_z(o)))

    def g5_take(o):
        here = zag.at[(z - o + Z) % Z]
        return remote(here, here, g5_send.at[o], g5_rsem.at[o], (d, at_z(o)))

    def g5_start(o, carry):
        g5_copy(o).start()
        return carry

    lax.fori_loop(1, Z, g5_start, 0)
    finish(3)

    def g5_wait(o, carry):
        g5_take(o).wait_recv()
        return carry

    lax.fori_loop(1, Z, g5_wait, 0)
    def g6_copy(n, device):
        return remote(zag, gwh.at[yh], g6_send.at[n], g6_rsem.at[yh], device)

    def g6_take(part):
        return remote(gwh.at[part], gwh.at[part], g6_send.at[0], g6_rsem.at[part], pair_dev)

    @pl.when(yh == y)
    def _():
        g6_copy(0, pair_dev).start()
        gwh[yh] = zag[...]
        g6_take(1 - yh).wait_recv()
        g6_copy(0, pair_dev).wait_send()

    @pl.when(yh != y)
    def _():
        g6_copy(0, far_dev).start()
        g6_copy(1, (d_far, s)).start()
        g6_take(0).wait_recv()
        g6_take(1).wait_recv()
        g6_copy(0, far_dev).wait_send()
        g6_copy(1, (d_far, s)).wait_send()

    for part in range(2):
        for j in range(4):
            lanes = slice((part * 4 + j) * LANES, (part * 4 + j + 1) * LANES)
            gwo[:, lanes] = gwh[part, 4 * j:4 * j + 4].reshape(HEAD_DIM, LANES).astype(F32)
    gw_copy = pltpu.make_async_copy(gwo, gw_out, o_sem.at[1, 3])
    gw_copy.start()

    def drain(i, carry):
        for copy in pair_kv(i):
            copy.wait_send()
        pair_q(i).wait_send()
        for n in range(2):
            halo(i, n, False).wait_send()
            halo(i, n, True).wait_send()
            far_copy(i, n).wait_send()
            ret_copy(i, n).wait_send()
        att_send(i).wait_send()
        dq_own(i).wait()
        dq_pair(i).wait_send()
        dq_take(i).wait_recv()
        g1_copy(i).wait_send()
        for copy in fin_own(i):
            copy.wait()
        for copy in fin_pair(i):
            copy.wait_send()
        for copy in fin_take(i):
            copy.wait_recv()
        return carry

    lax.fori_loop(0, STEPS, drain, 0)
    send_ct.wait_send()
    for o in (1, 2, 3):
        remote(w_in, wbuf.at[d], wx_send.at[o - 1], wx_recv.at[o - 1], (at_x(o), s)).wait_send()
        g2_copy(o - 1).wait_send()
    for o in range(4):
        block = w_block(yh, o)
        remote(block, block, wy_send.at[o], wy_recv.at[o], far_dev).wait_send()
        remote(block, block, wc_send.at[o], wc_recv.at[o], core_dev).wait_send()
        block = w_block(1 - yh, o)
        remote(block, block, wc_send.at[4 + o], wc_recv.at[4 + o], core_dev).wait_send()

    g3.wait_send()

    def drain_pieces(o, carry):
        g4_copy(o).wait_send()
        g5_copy(o).wait_send()
        return carry

    lax.fori_loop(1, Z, drain_pieces, 0)
    lo_copy.wait()
    gw_copy.wait()


def copy_kernel(*refs):
    sources, targets, rooms, sems = refs[:5], refs[5:10], refs[10:15], refs[15]
    loads = [pltpu.make_async_copy(sources[n], rooms[n], sems.at[n]) for n in range(5)]
    stores = [pltpu.make_async_copy(rooms[n], targets[n], sems.at[5 + n]) for n in range(5)]
    for load in loads:
        load.start()
    for load, store in zip(loads, stores):
        load.wait()
        store.start()
    for store in stores:
        store.wait()


def body(queries, key_rows, value_rows, cotangent, out_weight, lengths, upweight):
    vm = pltpu.VMEM
    dma = pltpu.SemaphoreType.DMA
    block = (ROWS, LANES)
    any_space = pl.BlockSpec(memory_space=pl.ANY)
    scalar = pl.BlockSpec(memory_space=pltpu.SMEM)
    rows_shape = jax.ShapeDtypeStruct((ROWS, WIDTH), BF16)
    outs = pl.pallas_call(
        layer_kernel,
        out_shape=(rows_shape,) * 4 + (jax.ShapeDtypeStruct((HEAD_DIM, WIDTH), F32),),
        in_specs=[scalar, scalar] + [any_space] * 5,
        out_specs=(any_space,) * 5,
        scratch_shapes=[
            vm((STEPS, 2) + block, BF16),
            vm((STEPS, SLOTS, 2) + block, BF16),
            vm((2, ROWS, WIDTH), BF16),
            vm((2, ROWS, WIDTH), BF16),
            vm((16, HEAD_DIM, WIDTH), BF16),
            vm((2, SPAN) + block, F32),
            vm((8,) + block, BF16),
            vm((STEPS, 2) + block, BF16),
            vm((STEPS, 2) + block, BF16),
            vm((SLOTS, 2) + block, F32),
            vm((STEPS, 2, 2) + block, F32),
            vm((STEPS, 2, 2, 2) + block, BF16),
            vm((STEPS, 2, 2, 2) + block, BF16),
            vm((STEPS, 2, 2, 2) + block, BF16),
            vm((STEPS, 2, 2, 2) + block, BF16),
            vm((STEPS, 2, 2) + block, BF16),
            vm((STEPS, 2, 2, 2) + block, F32),
            vm((STEPS, 2, HEAD_DIM, WIDTH), F32),
            vm((STEPS, HEAD_DIM, WIDTH), BF16),
            vm((STEPS, HEAD_DIM, WIDTH), BF16),
            vm((3, HEAD_DIM, WIDTH), BF16),
            vm((3, HEAD_DIM, WIDTH), BF16),
            vm((8, HEAD_DIM, LANES), F32),
            vm((4, HEAD_DIM, LANES), BF16),
            vm((4, HEAD_DIM, LANES), BF16),
            vm((Z, 16, LANES), F32),
            vm((Z, 16, LANES), BF16),
            vm((Z, 16, LANES), BF16),
            vm((Z, 16, LANES), BF16),
            vm((2, Z, 16, LANES), BF16),
            vm((HEAD_DIM, WIDTH), F32),
            vm((ROWS, WIDTH), BF16),
            vm((2, SPAN * ROWS, 2 * ROWS), F32),
            vm((SPAN * ROWS, 2 * ROWS), F32),
            vm((2, SPAN * ROWS, 2 * ROWS), BF16),
            vm((SPAN * ROWS, 2 * ROWS), BF16),
            dma((STEPS, 4)),
            dma((STEPS, 3)), dma((STEPS, 3)),
            dma, dma,
            dma((STEPS, 2)), dma((STEPS, 2)),
            dma((STEPS, 2)), dma((STEPS, 2)),
            dma((3,)), dma((3,)),
            dma((8,)), dma((8,)),
            dma((4,)), dma((4,)),
            dma((STEPS, 2)), dma((STEPS, 2)),
            dma((STEPS, 2)), dma((STEPS, 2)),
            dma((STEPS,)), dma((STEPS,)),
            dma((STEPS,)), dma((STEPS,)),
            dma((STEPS, 2)), dma((STEPS, 2)),
            dma((STEPS, 4)),
            dma((STEPS,)), dma((STEPS,)),
            dma((3,)), dma((3,)),
            dma, dma,
            dma((Z,)), dma((Z,)),
            dma((Z,)), dma((Z,)),
            dma((2,)), dma((2,)),
        ],
        compiler_params=pltpu.CompilerParams(
            collective_id=0, has_side_effects=True, vmem_limit_bytes=56 * 2**20
        ),
        name="layer",
    )(lengths, upweight, queries[0], key_rows[0], value_rows[0], cotangent[0], out_weight)
    outs = pl.pallas_call(
        copy_kernel,
        out_shape=tuple(jax.ShapeDtypeStruct(a.shape, a.dtype) for a in outs),
        in_specs=[any_space] * 5,
        out_specs=(any_space,) * 5,
        scratch_shapes=[vm(a.shape, a.dtype) for a in outs] + [dma((10,))],
        name="outputs",
    )(*outs)
    layer_out, grad_query, grad_key, grad_value, grad_weight = outs
    return (layer_out[None], grad_query[None], grad_key[None], grad_value[None], grad_weight)


def solution(mesh):
    rows = P("doc", "seq", None)
    flat = P("doc", None)
    return jax.shard_map(
        body,
        mesh=mesh,
        in_specs=(rows, rows, rows, rows, flat, flat, flat),
        out_specs=(rows, rows, rows, rows, flat),
        check_vma=False,
    )
```

```python
import math

import jax
import jax.numpy as jnp
from jax import lax
from jax.experimental import pallas as pl
from jax.experimental.pallas import tpu as pltpu
from jax.sharding import PartitionSpec as P

HEAD_DIM = 64
WINDOW = 512
BLOCK = 64
DOCS = 4
ROWS = 128
LANES = 128
SPAN = 9
SLOTS = 10
STEPS = 4
WIDTH = 1024
Z = 16
SIDES = (-1, 1)
MESH = pl.DeviceIdType.MESH
BF16 = jnp.bfloat16
F32 = jnp.float32

NT = (((1,), (1,)), ((), ()))
TN = (((0,), (0,)), ((), ()))


def dot(a, b, dims=(((1,), (0,)), ((), ()))):
    return lax.dot_general(a, b, dims, preferred_element_type=F32)


def remote(src, dst, send, recv, device):
    return pltpu.make_async_remote_copy(
        src_ref=src, dst_ref=dst, send_sem=send, recv_sem=recv, device_id=device, device_id_type=MESH
    )


def layer_kernel(
    lengths, upweight, q_in, k_in, v_in, ct_in, w_in,
    lo_out, dq_out, dk_out, dv_out, gw_out,
    qbuf, kv, ctb, gout, wbuf, bias, attbuf, attpair, dqb, acc, own, fout, fhere, rout, rin, fin,
    near, gkeep, g1send, g1recv, g2send, g2recv, g2sum, g3send, g3recv, g4f, g4send, g4recv, zag, gwh, gwo, lob,
    s_scr, dp_scr, p_scr, ds_scr,
    l_sem, y_send, y_recv, ct_send, ct_recv, z_send, z_recv, zf_send, zf_recv, wx_send, wx_recv,
    wc_send, wc_recv, wy_send, wy_recv, r_send, r_recv, rf_send, rf_recv, a_send, a_recv,
    dq_send, dq_recv, f_send, f_recv, o_sem, g1_send, g1_rsem, g2_send, g2_rsem,
    g3_send, g3_rsem, g4_send, g4_rsem, g5_send, g5_rsem, g6_send, g6_rsem,
):
    d = lax.axis_index("doc")
    s = lax.axis_index("seq")
    z, y = s // 2, s % 2
    yh, x, core = d // 8, (d // 2) % 4, d % 2
    s_pair = z * 2 + (1 - y)
    d_core = yh * 8 + x * 2 + (1 - core)
    d_far = (1 - yh) * 8 + x * 2 + core

    def at_x(offset):
        return yh * 8 + ((x + offset + 4) % 4) * 2 + core

    def at_z(offset):
        return ((z + offset + Z) % Z) * 2 + y

    def pair_of(step):
        return (x + 3 - step) % 4

    def cols(column, step):
        return pl.ds(pl.multiple_of((column * 4 + pair_of(step)) * LANES, LANES), LANES)

    pair_dev = (d, s_pair)
    core_dev = (d_core, s)
    far_dev = (d_far, s_pair)

    def own_kv(i):
        mine = cols(y, i)
        return [
            pltpu.make_async_copy(k_in.at[:, mine], kv.at[i, 4 + y, 0], l_sem.at[i, 0]),
            pltpu.make_async_copy(v_in.at[:, mine], kv.at[i, 4 + y, 1], l_sem.at[i, 1]),
        ]

    def own_q(i):
        return pltpu.make_async_copy(q_in.at[:, cols(y, i)], qbuf.at[i, y], l_sem.at[i, 2])

    own_ct = pltpu.make_async_copy(ct_in, ctb.at[y], l_sem.at[0, 3])
    own_w = pltpu.make_async_copy(w_in, wbuf.at[d], l_sem.at[1, 3])
    for i in range(STEPS):
        for copy in own_kv(i):
            copy.start()
    own_w.start()
    for i in range(STEPS):
        own_q(i).start()
    own_ct.start()

    barrier = pltpu.get_barrier_semaphore()
    partners = [pair_dev, core_dev, far_dev, (d_far, s)] + [(at_x(o), s) for o in (1, 2, 3)]
    for device in partners:
        pl.semaphore_signal(barrier, inc=1, device_id=device, device_id_type=MESH)

    def greet(o, carry):
        pl.semaphore_signal(barrier, inc=1, device_id=(d, at_z(o)), device_id_type=MESH)
        return carry

    lax.fori_loop(1, Z, greet, 0)
    pl.semaphore_wait(barrier, len(partners) + Z - 1)

    def pair_kv(i):
        theirs = cols(1 - y, i)
        return [
            remote(k_in.at[:, theirs], kv.at[i, 4 + y, 0], y_send.at[i, 0], y_recv.at[i, 0], pair_dev),
            remote(v_in.at[:, theirs], kv.at[i, 4 + y, 1], y_send.at[i, 1], y_recv.at[i, 1], pair_dev),
        ]

    def pair_q(i):
        return remote(
            q_in.at[:, cols(1 - y, i)], qbuf.at[i, y], y_send.at[i, 2], y_recv.at[i, 2], pair_dev
        )

    def take_kv(i):
        views = [kv.at[i, 5 - y, n] for n in range(2)]
        return [remote(views[n], views[n], y_send.at[i, n], y_recv.at[i, n], pair_dev) for n in range(2)]

    def take_q(i):
        here = qbuf.at[i, 1 - y]
        return remote(here, here, y_send.at[i, 2], y_recv.at[i, 2], pair_dev)

    def near_copy(i, n, part, arrival=False):
        o = SIDES[n]
        block = 4 + y if part == 0 else 5 - y
        to = block - 2 * o
        here = to if arrival else block
        return remote(
            kv.at[i, here], kv.at[i, to], z_send.at[i, n, part], z_recv.at[i, n, part], (d, at_z(o))
        )

    def halo(i, n, arrival=False):
        o = SIDES[n]
        to = 4 - 4 * o
        here = to if arrival else 4 - 2 * o
        return remote(
            kv.at[i, pl.ds(here, 2)], kv.at[i, pl.ds(to, 2)], zf_send.at[i, n], zf_recv.at[i, n], (d, at_z(o))
        )

    send_ct = remote(ct_in, ctb.at[y], ct_send, ct_recv, pair_dev)
    take_ct = remote(ctb.at[1 - y], ctb.at[1 - y], ct_send, ct_recv, pair_dev)

    def start_kv(i):
        for copy in pair_kv(i):
            copy.start()

    def start_q(i):
        pair_q(i).start()

    def own_near(i):
        for copy in own_kv(i):
            copy.wait()
        for n in range(2):
            near_copy(i, n, 0).start()

    def start_near(i):
        for copy in take_kv(i):
            copy.wait_recv()
        for n in range(2):
            near_copy(i, n, 1).start()

    def forward(i):
        for n in range(2):
            for part in range(2):
                near_copy(i, n, part, True).wait_recv()
            halo(i, n).start()

    start_kv(0)
    start_kv(1)
    start_q(0)
    for o in (1, 2, 3):
        remote(w_in, wbuf.at[d], wx_send.at[o - 1], wx_recv.at[o - 1], (at_x(o), s)).start()
    own_near(0)
    own_near(1)
    start_near(0)
    start_kv(2)
    start_q(1)
    start_near(1)
    start_kv(3)
    start_q(2)
    start_q(3)
    send_ct.start()

    bounds = []
    total = jnp.int32(0)
    for j in range(DOCS):
        total = total + lengths[0, j] * BLOCK
        bounds.append(total)

    def doc_of(position):
        ids = jnp.zeros_like(position)
        for bound in bounds:
            ids = ids + (position >= bound).astype(jnp.int32)
        return ids

    for yp in range(2):
        base = (z * 2 + yp) * ROWS

        def fill(j, carry, yp=yp, base=base):
            rows = lax.broadcasted_iota(jnp.int32, (ROWS, ROWS), 0)
            lanes = lax.broadcasted_iota(jnp.int32, (ROWS, ROWS), 1)
            key = base - WINDOW + j * ROWS + rows
            query = base + lanes
            near = jnp.abs(query - key) <= WINDOW
            inside = (key >= 0) & (key < Z * 2 * ROWS)
            ok = near & inside & (doc_of(key) == doc_of(query))
            bias[yp, j] = jnp.where(ok, 0.0, -jnp.inf).astype(F32)
            return carry

        lax.fori_loop(0, SPAN, fill, 0)

    def w_block(high, o):
        return wbuf.at[high * 8 + ((x - o + 4) % 4) * 2 + core]

    own_w.wait()
    for o in range(4):
        block = w_block(yh, o)
        if o:
            remote(block, block, wx_send.at[o - 1], wx_recv.at[o - 1], (at_x(-o), s)).wait_recv()
        remote(block, block, wy_send.at[o], wy_recv.at[o], far_dev).start()
        remote(block, block, wc_send.at[o], wc_recv.at[o], core_dev).start()

    forward(0)
    own_near(2)
    start_near(2)

    def grad_out_rows():
        own_ct.wait()
        take_ct.wait_recv()
        for yp in range(2):
            position = (z * 2 + yp) * ROWS + lax.broadcasted_iota(jnp.int32, (ROWS, LANES), 0)
            ids = doc_of(position)
            weight = jnp.zeros((ROWS, LANES), jnp.int32)
            for j in range(DOCS):
                weight = weight + jnp.where(ids == j, upweight[0, j], 0)
            weight = weight.astype(F32)
            for j in range(WIDTH // LANES):
                piece = slice(j * LANES, (j + 1) * LANES)
                gout[yp, :, piece] = (weight * ctb[yp, :, piece].astype(F32)).astype(BF16)

    def projection_rows():
        for o in range(4):
            block = w_block(1 - yh, o)
            remote(block, block, wy_send.at[o], wy_recv.at[o], far_dev).wait_recv()
            remote(block, block, wc_send.at[4 + o], wc_recv.at[4 + o], core_dev).start()
        for o in range(4):
            for h, high in ((0, yh), (1, 1 - yh)):
                block = wbuf.at[high * 8 + ((x - o + 4) % 4) * 2 + (1 - core)]
                remote(block, block, wc_send.at[4 * h + o], wc_recv.at[4 * h + o], core_dev).wait_recv()

    lane = lax.broadcasted_iota(jnp.int32, (ROWS, LANES), 1)

    def stacked(block):
        block = block.astype(F32)
        low = jnp.where(lane < HEAD_DIM, block, 0.0).astype(BF16)
        high = jnp.where(lane >= HEAD_DIM, block, 0.0).astype(BF16)
        return jnp.concatenate([low, high], axis=0)

    def unstacked(block):
        return jnp.concatenate([block[:HEAD_DIM, :ROWS], block[HEAD_DIM:, ROWS:]], axis=0)

    def key_block(j):
        return slice(j * ROWS, (j + 1) * ROWS)

    def ahead(i, yp):
        query2 = stacked(qbuf[i, yp])
        peak = jnp.full((8, 2 * ROWS), -jnp.inf, F32)
        for j in range(SPAN):
            mask = bias[yp, j]
            score = dot(kv[i, yp + j, 0], query2, NT) + jnp.concatenate([mask, mask], axis=1)
            s_scr[yp, key_block(j)] = score
            peak = jnp.maximum(peak, jnp.max(score.reshape(ROWS // 8, 8, 2 * ROWS), axis=0))
        peak = jnp.max(peak, axis=0, keepdims=True)
        norm = jnp.zeros((8, 2 * ROWS), F32)
        for j in range(SPAN):
            power = jnp.exp((s_scr[yp, key_block(j)] - peak) * (HEAD_DIM ** -0.5))
            s_scr[yp, key_block(j)] = power
            norm = norm + jnp.sum(power.reshape(ROWS // 8, 8, 2 * ROWS), axis=0)
        share = 1.0 / jnp.sum(norm, axis=0, keepdims=True)
        for j in range(SPAN):
            prob = s_scr[yp, key_block(j)] * share
            s_scr[yp, key_block(j)] = prob
            p_scr[yp, key_block(j)] = prob.astype(BF16)
        values = kv[i, yp:yp + SPAN, 1].reshape(SPAN * ROWS, LANES)
        mixed = unstacked(dot(values, p_scr[yp], TN))
        attpair[i, yp] = mixed.T.astype(BF16)
        return mixed.astype(BF16)

    def back(i, yp, w_pair):
        query2 = stacked(qbuf[i, yp])
        grad2 = stacked(dot(gout[yp], w_pair, NT).astype(BF16))
        centre = jnp.zeros((8, 2 * ROWS), F32)
        for j in range(SPAN):
            slope = dot(kv[i, yp + j, 1], grad2, NT)
            dp_scr[key_block(j)] = slope
            weighted = s_scr[yp, key_block(j)] * slope
            centre = centre + jnp.sum(weighted.reshape(ROWS // 8, 8, 2 * ROWS), axis=0)
        centre = jnp.sum(centre, axis=0, keepdims=True)
        for j in range(SPAN):
            prob = s_scr[yp, key_block(j)]
            grad_score = (prob * (dp_scr[key_block(j)] - centre) * (HEAD_DIM ** -0.5)).astype(BF16)
            ds_scr[key_block(j)] = grad_score
            key_part = dot(grad_score, query2)
            value_part = dot(p_scr[yp, key_block(j)], grad2)
            if yp == 0:
                acc[j, 0] = key_part
                acc[j, 1] = value_part
            elif j + 1 < SPAN:
                acc[j + 1, 0] += key_part
                acc[j + 1, 1] += value_part
            else:
                acc[j + 1, 0] = key_part
                acc[j + 1, 1] = value_part
        keys = kv[i, yp:yp + SPAN, 0].reshape(SPAN * ROWS, LANES)
        dqb[i, yp] = unstacked(dot(keys, ds_scr[...], TN)).T.astype(BF16)

    def att_send(i):
        return remote(
            attpair.at[i, 1 - y], attbuf.at[y * 4 + pair_of(i)], a_send.at[i], a_recv.at[i], pair_dev
        )

    def att_take(i):
        here = attbuf.at[(1 - y) * 4 + pair_of(i)]
        return remote(here, here, a_send.at[i], a_recv.at[i], pair_dev)

    def dq_own(i):
        return pltpu.make_async_copy(dqb.at[i, y], dq_out.at[:, cols(y, i)], o_sem.at[i, 0])

    def dq_pair(i):
        return remote(dqb.at[i, 1 - y], dq_out.at[:, cols(y, i)], dq_send.at[i], dq_recv.at[i], pair_dev)

    def dq_take(i):
        here = dq_out.at[:, cols(1 - y, i)]
        return remote(here, here, dq_send.at[i], dq_recv.at[i], pair_dev)

    def far_copy(i, n):
        return remote(fout.at[i, n], fhere.at[i, n], rf_send.at[i, n], rf_recv.at[i, n], (d, at_z(SIDES[n])))

    def ret_copy(i, n):
        return remote(rout.at[i, n], rin.at[i, n], r_send.at[i, n], r_recv.at[i, n], (d, at_z(SIDES[n])))

    def ret_start(i):
        for n in range(2):
            far_copy(i, n).wait_recv()
            rout[i, n] = (near[i, n] + fhere[i, n].astype(F32)).astype(BF16)
            ret_copy(i, n).start()

    def g1_copy(i):
        return remote(g1send.at[i], g1recv.at[i], g1_send.at[i], g1_rsem.at[i], core_dev)

    def g2_copy(i):
        return remote(g2send.at[i], g2recv.at[i], g2_send.at[i], g2_rsem.at[i], (at_x(-1 - i), s))

    def g2_start(i):
        g1_copy(i).wait_recv()
        g2send[i] = (gkeep[i, core] + g1recv[i].astype(F32)).astype(BF16)
        g2_copy(i).start()

    def fin_own(i):
        return [
            pltpu.make_async_copy(fin.at[i, y, n], out.at[:, cols(y, i)], o_sem.at[i, 1 + n])
            for n, out in ((0, dk_out), (1, dv_out))
        ]

    def fin_pair(i):
        return [
            remote(fin.at[i, 1 - y, n], out.at[:, cols(y, i)], f_send.at[i, n], f_recv.at[i, n], pair_dev)
            for n, out in ((0, dk_out), (1, dv_out))
        ]

    def fin_take(i):
        views = [out.at[:, cols(1 - y, i)] for out in (dk_out, dv_out)]
        return [remote(views[n], views[n], f_send.at[i, n], f_recv.at[i, n], pair_dev) for n in range(2)]

    def finish(i):
        total = own[i]
        for n in range(2):
            ret_copy(i, n).wait_recv()
            total = total + rin[i, n].astype(F32)
        fin[i] = total.astype(BF16)
        for copy in fin_pair(i) + fin_own(i):
            copy.start()

    def g4_copy(o):
        return remote(g4send.at[(z + o) % Z], g4recv.at[o], g4_send.at[o], g4_rsem.at[o], (d, at_z(o)))

    def head_sum():
        g1_copy(3).wait_recv()
        head = gkeep[3, core] + g1recv[3].astype(F32)
        for i in range(3):
            remote(g2recv.at[i], g2recv.at[i], g2_send.at[i], g2_rsem.at[i], (at_x(1 + i), s)).wait_recv()
            head = head + g2recv[i].astype(F32)
        for j in range(8):
            g2sum[j] = head[:, j * LANES:(j + 1) * LANES]
        g3send[...] = g2sum[pl.ds((1 - yh) * 4, 4)].astype(BF16)
        g3.start()

    g3 = remote(g3send, g3recv, g3_send, g3_rsem, (d_far, s))

    def z_pieces():
        g3.wait_recv()
        half_sum = g2sum[pl.ds(yh * 4, 4)] + g3recv[...].astype(F32)
        g4f[...] = half_sum.reshape(Z, 16, LANES)
        g4send[...] = g4f[...].astype(BF16)

        def g4_start(o, carry):
            g4_copy(o).start()
            return carry

        lax.fori_loop(1, Z, g4_start, 0)

    def step(i, carry):
        @pl.when(i < 3)
        def _():
            forward(i + 1)

        @pl.when(i == 0)
        def _():
            own_near(3)
            start_near(3)

        @pl.when(i > 0)
        def _():
            g2_start(i - 1)

        own_q(i).wait()
        take_q(i).wait_recv()
        for n in range(2):
            halo(i, n, True).wait_recv()
        mixed = [ahead(i, yp) for yp in range(2)]
        att_send(i).start()
        attbuf[y * 4 + pair_of(i)] = attpair[i, y]

        @pl.when(i == 0)
        def _():
            grad_out_rows()

        weight_part = dot(mixed[0], gout[0]) + dot(mixed[1], gout[1])
        gkeep[i, 0] = weight_part[:HEAD_DIM]
        gkeep[i, 1] = weight_part[HEAD_DIM:]
        g1send[i] = gkeep[i, 1 - core].astype(BF16)
        g1_copy(i).start()

        @pl.when(i == 0)
        def _():
            projection_rows()

        doc_row = y * 8 + pair_of(i) * 2
        w_pair = wbuf[pl.ds(doc_row, 2)].reshape(2 * HEAD_DIM, WIDTH)
        back(i, 0, w_pair)

        @pl.when(i == 3)
        def _():
            head_sum()

        back(i, 1, w_pair)
        for n in range(2):
            first = 8 * n
            fout[i, n] = acc[first:first + 2].astype(BF16)
            far_copy(i, n).start()
            near[i, n] = acc[2 + 4 * n:4 + 4 * n]
        own[i] = acc[4:6]
        dq_own(i).start()
        dq_pair(i).start()

        @pl.when(i == 3)
        def _():
            z_pieces()

        @pl.when(i > 0)
        def _():
            ret_start(i - 1)

        @pl.when(i > 1)
        def _():
            finish(i - 2)

        return carry

    lax.fori_loop(0, STEPS, step, 0)
    ret_start(3)
    finish(2)

    for i in range(STEPS):
        att_take(i).wait_recv()
    rows = jnp.concatenate([attbuf[j] for j in range(8)], axis=1)
    for j in range(4):
        piece = slice(j * 256, (j + 1) * 256)
        lob[:, piece] = dot(rows, wbuf[:, :, piece].reshape(WIDTH, 256)).astype(BF16)
    lo_copy = pltpu.make_async_copy(lob, lo_out, o_sem.at[0, 3])
    lo_copy.start()

    def g4_wait(o, total):
        g4_copy(o).wait_recv()
        return total + g4recv[o].astype(F32)

    piece_sum = lax.fori_loop(1, Z, g4_wait, g4f[z])
    zag[z] = (piece_sum * (1.0 / math.sqrt(Z * 2 * ROWS * 16))).astype(BF16)

    def g5_copy(o):
        return remote(zag.at[z], zag.at[z], g5_send.at[o], g5_rsem.at[o], (d, at_z(o)))

    def g5_take(o):
        here = zag.at[(z - o + Z) % Z]
        return remote(here, here, g5_send.at[o], g5_rsem.at[o], (d, at_z(o)))

    def g5_start(o, carry):
        g5_copy(o).start()
        return carry

    lax.fori_loop(1, Z, g5_start, 0)
    finish(3)

    def g5_wait(o, carry):
        g5_take(o).wait_recv()
        return carry

    lax.fori_loop(1, Z, g5_wait, 0)
    def g6_copy(n, device):
        return remote(zag, gwh.at[yh], g6_send.at[n], g6_rsem.at[yh], device)

    def g6_take(part):
        return remote(gwh.at[part], gwh.at[part], g6_send.at[0], g6_rsem.at[part], pair_dev)

    @pl.when(yh == y)
    def _():
        g6_copy(0, pair_dev).start()
        gwh[yh] = zag[...]
        g6_take(1 - yh).wait_recv()
        g6_copy(0, pair_dev).wait_send()

    @pl.when(yh != y)
    def _():
        g6_copy(0, far_dev).start()
        g6_copy(1, (d_far, s)).start()
        g6_take(0).wait_recv()
        g6_take(1).wait_recv()
        g6_copy(0, far_dev).wait_send()
        g6_copy(1, (d_far, s)).wait_send()

    for part in range(2):
        for j in range(4):
            lanes = slice((part * 4 + j) * LANES, (part * 4 + j + 1) * LANES)
            gwo[:, lanes] = gwh[part, 4 * j:4 * j + 4].reshape(HEAD_DIM, LANES).astype(F32)
    gw_copy = pltpu.make_async_copy(gwo, gw_out, o_sem.at[1, 3])
    gw_copy.start()

    def drain(i, carry):
        for copy in pair_kv(i):
            copy.wait_send()
        pair_q(i).wait_send()
        for n in range(2):
            near_copy(i, n, 0).wait_send()
            near_copy(i, n, 1).wait_send()
            halo(i, n).wait_send()
            far_copy(i, n).wait_send()
            ret_copy(i, n).wait_send()
        att_send(i).wait_send()
        dq_own(i).wait()
        dq_pair(i).wait_send()
        dq_take(i).wait_recv()
        g1_copy(i).wait_send()
        for copy in fin_own(i):
            copy.wait()
        for copy in fin_pair(i):
            copy.wait_send()
        for copy in fin_take(i):
            copy.wait_recv()
        return carry

    lax.fori_loop(0, STEPS, drain, 0)
    send_ct.wait_send()
    for o in (1, 2, 3):
        remote(w_in, wbuf.at[d], wx_send.at[o - 1], wx_recv.at[o - 1], (at_x(o), s)).wait_send()
        g2_copy(o - 1).wait_send()
    for o in range(4):
        block = w_block(yh, o)
        remote(block, block, wy_send.at[o], wy_recv.at[o], far_dev).wait_send()
        remote(block, block, wc_send.at[o], wc_recv.at[o], core_dev).wait_send()
        block = w_block(1 - yh, o)
        remote(block, block, wc_send.at[4 + o], wc_recv.at[4 + o], core_dev).wait_send()

    g3.wait_send()

    def drain_pieces(o, carry):
        g4_copy(o).wait_send()
        g5_copy(o).wait_send()
        return carry

    lax.fori_loop(1, Z, drain_pieces, 0)
    lo_copy.wait()
    gw_copy.wait()


def copy_kernel(*refs):
    sources, targets, rooms, sems = refs[:5], refs[5:10], refs[10:15], refs[15]
    loads = [pltpu.make_async_copy(sources[n], rooms[n], sems.at[n]) for n in range(5)]
    stores = [pltpu.make_async_copy(rooms[n], targets[n], sems.at[5 + n]) for n in range(5)]
    for load in loads:
        load.start()
    for load, store in zip(loads, stores):
        load.wait()
        store.start()
    for store in stores:
        store.wait()


def body(queries, key_rows, value_rows, cotangent, out_weight, lengths, upweight):
    vm = pltpu.VMEM
    dma = pltpu.SemaphoreType.DMA
    block = (ROWS, LANES)
    any_space = pl.BlockSpec(memory_space=pl.ANY)
    scalar = pl.BlockSpec(memory_space=pltpu.SMEM)
    rows_shape = jax.ShapeDtypeStruct((ROWS, WIDTH), BF16)
    outs = pl.pallas_call(
        layer_kernel,
        out_shape=(rows_shape,) * 4 + (jax.ShapeDtypeStruct((HEAD_DIM, WIDTH), F32),),
        in_specs=[scalar, scalar] + [any_space] * 5,
        out_specs=(any_space,) * 5,
        scratch_shapes=[
            vm((STEPS, 2) + block, BF16),
            vm((STEPS, SLOTS, 2) + block, BF16),
            vm((2, ROWS, WIDTH), BF16),
            vm((2, ROWS, WIDTH), BF16),
            vm((16, HEAD_DIM, WIDTH), BF16),
            vm((2, SPAN) + block, F32),
            vm((8,) + block, BF16),
            vm((STEPS, 2) + block, BF16),
            vm((STEPS, 2) + block, BF16),
            vm((SLOTS, 2) + block, F32),
            vm((STEPS, 2, 2) + block, F32),
            vm((STEPS, 2, 2, 2) + block, BF16),
            vm((STEPS, 2, 2, 2) + block, BF16),
            vm((STEPS, 2, 2, 2) + block, BF16),
            vm((STEPS, 2, 2, 2) + block, BF16),
            vm((STEPS, 2, 2) + block, BF16),
            vm((STEPS, 2, 2, 2) + block, F32),
            vm((STEPS, 2, HEAD_DIM, WIDTH), F32),
            vm((STEPS, HEAD_DIM, WIDTH), BF16),
            vm((STEPS, HEAD_DIM, WIDTH), BF16),
            vm((3, HEAD_DIM, WIDTH), BF16),
            vm((3, HEAD_DIM, WIDTH), BF16),
            vm((8, HEAD_DIM, LANES), F32),
            vm((4, HEAD_DIM, LANES), BF16),
            vm((4, HEAD_DIM, LANES), BF16),
            vm((Z, 16, LANES), F32),
            vm((Z, 16, LANES), BF16),
            vm((Z, 16, LANES), BF16),
            vm((Z, 16, LANES), BF16),
            vm((2, Z, 16, LANES), BF16),
            vm((HEAD_DIM, WIDTH), F32),
            vm((ROWS, WIDTH), BF16),
            vm((2, SPAN * ROWS, 2 * ROWS), F32),
            vm((SPAN * ROWS, 2 * ROWS), F32),
            vm((2, SPAN * ROWS, 2 * ROWS), BF16),
            vm((SPAN * ROWS, 2 * ROWS), BF16),
            dma((STEPS, 4)),
            dma((STEPS, 3)), dma((STEPS, 3)),
            dma, dma,
            dma((STEPS, 2, 2)), dma((STEPS, 2, 2)),
            dma((STEPS, 2)), dma((STEPS, 2)),
            dma((3,)), dma((3,)),
            dma((8,)), dma((8,)),
            dma((4,)), dma((4,)),
            dma((STEPS, 2)), dma((STEPS, 2)),
            dma((STEPS, 2)), dma((STEPS, 2)),
            dma((STEPS,)), dma((STEPS,)),
            dma((STEPS,)), dma((STEPS,)),
            dma((STEPS, 2)), dma((STEPS, 2)),
            dma((STEPS, 4)),
            dma((STEPS,)), dma((STEPS,)),
            dma((3,)), dma((3,)),
            dma, dma,
            dma((Z,)), dma((Z,)),
            dma((Z,)), dma((Z,)),
            dma((2,)), dma((2,)),
        ],
        compiler_params=pltpu.CompilerParams(
            collective_id=0, has_side_effects=True, vmem_limit_bytes=56 * 2**20
        ),
        name="layer",
    )(lengths, upweight, queries[0], key_rows[0], value_rows[0], cotangent[0], out_weight)
    outs = pl.pallas_call(
        copy_kernel,
        out_shape=tuple(jax.ShapeDtypeStruct(a.shape, a.dtype) for a in outs),
        in_specs=[any_space] * 5,
        out_specs=(any_space,) * 5,
        scratch_shapes=[vm(a.shape, a.dtype) for a in outs] + [dma((10,))],
        name="outputs",
    )(*outs)
    layer_out, grad_query, grad_key, grad_value, grad_weight = outs
    return (layer_out[None], grad_query[None], grad_key[None], grad_value[None], grad_weight)


def solution(mesh):
    rows = P("doc", "seq", None)
    flat = P("doc", None)
    return jax.shard_map(
        body,
        mesh=mesh,
        in_specs=(rows, rows, rows, rows, flat, flat, flat),
        out_specs=(rows, rows, rows, rows, flat),
        check_vma=False,
    )
```

```python
import math

import jax
import jax.numpy as jnp
from jax import lax
from jax.experimental import pallas as pl
from jax.experimental.pallas import tpu as pltpu
from jax.sharding import PartitionSpec as P

HEAD_DIM = 64
WINDOW = 512
BLOCK = 64
DOCS = 4
ROWS = 128
LANES = 128
SPAN = 9
SLOTS = 10
STEPS = 4
WIDTH = 1024
Z = 16
SIDES = (-1, 1)
MESH = pl.DeviceIdType.MESH
BF16 = jnp.bfloat16
F32 = jnp.float32

NT = (((1,), (1,)), ((), ()))
TN = (((0,), (0,)), ((), ()))


def dot(a, b, dims=(((1,), (0,)), ((), ()))):
    return lax.dot_general(a, b, dims, preferred_element_type=F32)


def remote(src, dst, send, recv, device):
    return pltpu.make_async_remote_copy(
        src_ref=src, dst_ref=dst, send_sem=send, recv_sem=recv, device_id=device, device_id_type=MESH
    )


def layer_kernel(
    lengths, upweight, q_in, k_in, v_in, ct_in, w_in,
    lo_out, dq_out, dk_out, dv_out, gw_out,
    qbuf, kv, ctb, gout, wbuf, bias, attbuf, attpair, dqb, acc, own, fout, fhere, rout, rin, fin,
    near, gkeep, g1send, g1recv, g2send, g2recv, g2sum, g3send, g3recv, g4f, g4send, g4recv, zag, gwh, gwo, lob,
    s_scr, dp_scr, p_scr, ds_scr,
    l_sem, y_send, y_recv, ct_send, ct_recv, z_send, z_recv, zf_send, zf_recv, wx_send, wx_recv,
    wc_send, wc_recv, wy_send, wy_recv, r_send, r_recv, rf_send, rf_recv, a_send, a_recv,
    dq_send, dq_recv, f_send, f_recv, o_sem, g1_send, g1_rsem, g2_send, g2_rsem,
    g3_send, g3_rsem, g4_send, g4_rsem, g5_send, g5_rsem, g6_send, g6_rsem,
):
    d = lax.axis_index("doc")
    s = lax.axis_index("seq")
    z, y = s // 2, s % 2
    yh, x, core = d // 8, (d // 2) % 4, d % 2
    s_pair = z * 2 + (1 - y)
    d_core = yh * 8 + x * 2 + (1 - core)
    d_far = (1 - yh) * 8 + x * 2 + core

    def at_x(offset):
        return yh * 8 + ((x + offset + 4) % 4) * 2 + core

    def at_z(offset):
        return ((z + offset + Z) % Z) * 2 + y

    def pair_of(step):
        return (x + 3 - step) % 4

    def cols(column, step):
        return pl.ds(pl.multiple_of((column * 4 + pair_of(step)) * LANES, LANES), LANES)

    pair_dev = (d, s_pair)
    core_dev = (d_core, s)
    far_dev = (d_far, s_pair)

    def own_kv(i):
        mine = cols(y, i)
        return [
            pltpu.make_async_copy(k_in.at[:, mine], kv.at[i, 4 + y, 0], l_sem.at[i, 0]),
            pltpu.make_async_copy(v_in.at[:, mine], kv.at[i, 4 + y, 1], l_sem.at[i, 1]),
        ]

    def own_q(i):
        return pltpu.make_async_copy(q_in.at[:, cols(y, i)], qbuf.at[i, y], l_sem.at[i, 2])

    own_ct = pltpu.make_async_copy(ct_in, ctb.at[y], l_sem.at[0, 3])
    own_w = pltpu.make_async_copy(w_in, wbuf.at[d], l_sem.at[1, 3])
    for i in range(STEPS):
        for copy in own_kv(i):
            copy.start()
    own_w.start()
    for i in range(STEPS):
        own_q(i).start()
    own_ct.start()

    barrier = pltpu.get_barrier_semaphore()
    partners = [pair_dev, core_dev, far_dev, (d_far, s)] + [(at_x(o), s) for o in (1, 2, 3)]
    for device in partners:
        pl.semaphore_signal(barrier, inc=1, device_id=device, device_id_type=MESH)

    def greet(o, carry):
        pl.semaphore_signal(barrier, inc=1, device_id=(d, at_z(o)), device_id_type=MESH)
        return carry

    lax.fori_loop(1, Z, greet, 0)
    pl.semaphore_wait(barrier, len(partners) + Z - 1)

    def pair_kv(i):
        theirs = cols(1 - y, i)
        return [
            remote(k_in.at[:, theirs], kv.at[i, 4 + y, 0], y_send.at[i, 0], y_recv.at[i, 0], pair_dev),
            remote(v_in.at[:, theirs], kv.at[i, 4 + y, 1], y_send.at[i, 1], y_recv.at[i, 1], pair_dev),
        ]

    def pair_q(i):
        return remote(
            q_in.at[:, cols(1 - y, i)], qbuf.at[i, y], y_send.at[i, 2], y_recv.at[i, 2], pair_dev
        )

    def take_kv(i):
        views = [kv.at[i, 5 - y, n] for n in range(2)]
        return [remote(views[n], views[n], y_send.at[i, n], y_recv.at[i, n], pair_dev) for n in range(2)]

    def take_q(i):
        here = qbuf.at[i, 1 - y]
        return remote(here, here, y_send.at[i, 2], y_recv.at[i, 2], pair_dev)

    def near_copy(i, n, part, arrival=False):
        o = SIDES[n]
        block = 4 + y if part == 0 else 5 - y
        to = block - 2 * o
        here = to if arrival else block
        return remote(
            kv.at[i, here], kv.at[i, to], z_send.at[i, n, part], z_recv.at[i, n, part], (d, at_z(o))
        )

    def halo(i, n, arrival=False):
        o = SIDES[n]
        to = 4 - 4 * o
        here = to if arrival else 4 - 2 * o
        return remote(
            kv.at[i, pl.ds(here, 2)], kv.at[i, pl.ds(to, 2)], zf_send.at[i, n], zf_recv.at[i, n], (d, at_z(o))
        )

    send_ct = remote(ct_in, ctb.at[y], ct_send, ct_recv, pair_dev)
    take_ct = remote(ctb.at[1 - y], ctb.at[1 - y], ct_send, ct_recv, pair_dev)

    def start_kv(i):
        for copy in pair_kv(i):
            copy.start()

    def start_q(i):
        pair_q(i).start()

    def own_near(i):
        for copy in own_kv(i):
            copy.wait()
        for n in range(2):
            near_copy(i, n, 0).start()

    def start_near(i):
        for copy in take_kv(i):
            copy.wait_recv()
        for n in range(2):
            near_copy(i, n, 1).start()

    def forward(i):
        for n in range(2):
            for part in range(2):
                near_copy(i, n, part, True).wait_recv()
            halo(i, n).start()

    start_kv(0)
    start_kv(1)
    start_q(0)
    for o in (1, 2, 3):
        remote(w_in, wbuf.at[d], wx_send.at[o - 1], wx_recv.at[o - 1], (at_x(o), s)).start()
    own_near(0)
    own_near(1)
    start_near(0)
    start_kv(2)
    start_q(1)
    start_near(1)
    start_kv(3)
    start_q(2)
    start_q(3)
    send_ct.start()

    bounds = []
    total = jnp.int32(0)
    for j in range(DOCS):
        total = total + lengths[0, j] * BLOCK
        bounds.append(total)

    def doc_of(position):
        ids = jnp.zeros_like(position)
        for bound in bounds:
            ids = ids + (position >= bound).astype(jnp.int32)
        return ids

    for yp in range(2):
        base = (z * 2 + yp) * ROWS

        def fill(j, carry, yp=yp, base=base):
            rows = lax.broadcasted_iota(jnp.int32, (ROWS, ROWS), 0)
            lanes = lax.broadcasted_iota(jnp.int32, (ROWS, ROWS), 1)
            key = base - WINDOW + j * ROWS + rows
            query = base + lanes
            near = jnp.abs(query - key) <= WINDOW
            inside = (key >= 0) & (key < Z * 2 * ROWS)
            ok = near & inside & (doc_of(key) == doc_of(query))
            bias[yp, j] = jnp.where(ok, 0.0, -jnp.inf).astype(F32)
            return carry

        lax.fori_loop(0, SPAN, fill, 0)

    def w_block(high, o):
        return wbuf.at[high * 8 + ((x - o + 4) % 4) * 2 + core]

    own_w.wait()
    for o in range(4):
        block = w_block(yh, o)
        if o:
            remote(block, block, wx_send.at[o - 1], wx_recv.at[o - 1], (at_x(-o), s)).wait_recv()
        remote(block, block, wy_send.at[o], wy_recv.at[o], far_dev).start()
        remote(block, block, wc_send.at[o], wc_recv.at[o], core_dev).start()

    forward(0)
    own_near(2)
    start_near(2)

    def grad_out_rows():
        own_ct.wait()
        take_ct.wait_recv()
        for yp in range(2):
            position = (z * 2 + yp) * ROWS + lax.broadcasted_iota(jnp.int32, (ROWS, LANES), 0)
            ids = doc_of(position)
            weight = jnp.zeros((ROWS, LANES), jnp.int32)
            for j in range(DOCS):
                weight = weight + jnp.where(ids == j, upweight[0, j], 0)
            weight = weight.astype(F32)
            for j in range(WIDTH // LANES):
                piece = slice(j * LANES, (j + 1) * LANES)
                gout[yp, :, piece] = (weight * ctb[yp, :, piece].astype(F32)).astype(BF16)

    def projection_rows():
        for o in range(4):
            block = w_block(1 - yh, o)
            remote(block, block, wy_send.at[o], wy_recv.at[o], far_dev).wait_recv()
            remote(block, block, wc_send.at[4 + o], wc_recv.at[4 + o], core_dev).start()
        for o in range(4):
            for h, high in ((0, yh), (1, 1 - yh)):
                block = wbuf.at[high * 8 + ((x - o + 4) % 4) * 2 + (1 - core)]
                remote(block, block, wc_send.at[4 * h + o], wc_recv.at[4 * h + o], core_dev).wait_recv()

    lane = lax.broadcasted_iota(jnp.int32, (ROWS, LANES), 1)

    def stacked(block):
        block = block.astype(F32)
        low = jnp.where(lane < HEAD_DIM, block, 0.0).astype(BF16)
        high = jnp.where(lane >= HEAD_DIM, block, 0.0).astype(BF16)
        return jnp.concatenate([low, high], axis=0)

    def unstacked(block):
        return jnp.concatenate([block[:HEAD_DIM, :ROWS], block[HEAD_DIM:, ROWS:]], axis=0)

    def key_block(j):
        return slice(j * ROWS, (j + 1) * ROWS)

    def ahead(i, yp):
        query2 = stacked(qbuf[i, yp])
        peak = jnp.full((8, 2 * ROWS), -jnp.inf, F32)
        for j in range(SPAN):
            mask = bias[yp, j]
            score = dot(kv[i, yp + j, 0], query2, NT) + jnp.concatenate([mask, mask], axis=1)
            s_scr[yp, key_block(j)] = score
            peak = jnp.maximum(peak, jnp.max(score.reshape(ROWS // 8, 8, 2 * ROWS), axis=0))
        peak = jnp.max(peak, axis=0, keepdims=True)
        norm = jnp.zeros((8, 2 * ROWS), F32)
        for j in range(SPAN):
            power = jnp.exp((s_scr[yp, key_block(j)] - peak) * (HEAD_DIM ** -0.5))
            s_scr[yp, key_block(j)] = power
            norm = norm + jnp.sum(power.reshape(ROWS // 8, 8, 2 * ROWS), axis=0)
        share = 1.0 / jnp.sum(norm, axis=0, keepdims=True)
        for j in range(SPAN):
            prob = s_scr[yp, key_block(j)] * share
            s_scr[yp, key_block(j)] = prob
            p_scr[yp, key_block(j)] = prob.astype(BF16)
        values = kv[i, yp:yp + SPAN, 1].reshape(SPAN * ROWS, LANES)
        mixed = unstacked(dot(values, p_scr[yp], TN))
        attpair[i, yp] = mixed.T.astype(BF16)
        return mixed.astype(BF16)

    def back(i, yp, w_pair):
        query2 = stacked(qbuf[i, yp])
        grad2 = stacked(dot(gout[yp], w_pair, NT).astype(BF16))
        centre = jnp.zeros((8, 2 * ROWS), F32)
        for j in range(SPAN):
            slope = dot(kv[i, yp + j, 1], grad2, NT)
            dp_scr[key_block(j)] = slope
            weighted = s_scr[yp, key_block(j)] * slope
            centre = centre + jnp.sum(weighted.reshape(ROWS // 8, 8, 2 * ROWS), axis=0)
        centre = jnp.sum(centre, axis=0, keepdims=True)
        for j in range(SPAN):
            prob = s_scr[yp, key_block(j)]
            grad_score = (prob * (dp_scr[key_block(j)] - centre) * (HEAD_DIM ** -0.5)).astype(BF16)
            ds_scr[key_block(j)] = grad_score
            key_part = dot(grad_score, query2)
            value_part = dot(p_scr[yp, key_block(j)], grad2)
            if yp == 0:
                acc[j, 0] = key_part
                acc[j, 1] = value_part
            elif j + 1 < SPAN:
                acc[j + 1, 0] += key_part
                acc[j + 1, 1] += value_part
            else:
                acc[j + 1, 0] = key_part
                acc[j + 1, 1] = value_part
        keys = kv[i, yp:yp + SPAN, 0].reshape(SPAN * ROWS, LANES)
        dqb[i, yp] = unstacked(dot(keys, ds_scr[...], TN)).T.astype(BF16)

    def att_send(i):
        return remote(
            attpair.at[i, 1 - y], attbuf.at[y * 4 + pair_of(i)], a_send.at[i], a_recv.at[i], pair_dev
        )

    def att_take(i):
        here = attbuf.at[(1 - y) * 4 + pair_of(i)]
        return remote(here, here, a_send.at[i], a_recv.at[i], pair_dev)

    def dq_own(i):
        return pltpu.make_async_copy(dqb.at[i, y], dq_out.at[:, cols(y, i)], o_sem.at[i, 0])

    def dq_pair(i):
        return remote(dqb.at[i, 1 - y], dq_out.at[:, cols(y, i)], dq_send.at[i], dq_recv.at[i], pair_dev)

    def dq_take(i):
        here = dq_out.at[:, cols(1 - y, i)]
        return remote(here, here, dq_send.at[i], dq_recv.at[i], pair_dev)

    def far_copy(i, n):
        return remote(fout.at[i, n], fhere.at[i, n], rf_send.at[i, n], rf_recv.at[i, n], (d, at_z(SIDES[n])))

    def ret_copy(i, n):
        return remote(rout.at[i, n], rin.at[i, n], r_send.at[i, n], r_recv.at[i, n], (d, at_z(SIDES[n])))

    def ret_start(i):
        for n in range(2):
            far_copy(i, n).wait_recv()
            rout[i, n] = (near[i, n] + fhere[i, n].astype(F32)).astype(BF16)
            ret_copy(i, n).start()

    def g1_copy(i):
        return remote(g1send.at[i], g1recv.at[i], g1_send.at[i], g1_rsem.at[i], core_dev)

    def g2_copy(i):
        return remote(g2send.at[i], g2recv.at[i], g2_send.at[i], g2_rsem.at[i], (at_x(-1 - i), s))

    def g2_start(i):
        g1_copy(i).wait_recv()
        g2send[i] = (gkeep[i, core] + g1recv[i].astype(F32)).astype(BF16)
        g2_copy(i).start()

    def fin_own(i):
        return [
            pltpu.make_async_copy(fin.at[i, y, n], out.at[:, cols(y, i)], o_sem.at[i, 1 + n])
            for n, out in ((0, dk_out), (1, dv_out))
        ]

    def fin_pair(i):
        return [
            remote(fin.at[i, 1 - y, n], out.at[:, cols(y, i)], f_send.at[i, n], f_recv.at[i, n], pair_dev)
            for n, out in ((0, dk_out), (1, dv_out))
        ]

    def fin_take(i):
        views = [out.at[:, cols(1 - y, i)] for out in (dk_out, dv_out)]
        return [remote(views[n], views[n], f_send.at[i, n], f_recv.at[i, n], pair_dev) for n in range(2)]

    def finish(i):
        total = own[i]
        for n in range(2):
            ret_copy(i, n).wait_recv()
            total = total + rin[i, n].astype(F32)
        fin[i] = total.astype(BF16)
        for copy in fin_pair(i) + fin_own(i):
            copy.start()

    def g4_copy(o):
        return remote(g4send.at[(z + o) % Z], g4recv.at[o], g4_send.at[o], g4_rsem.at[o], (d, at_z(o)))

    def head_sum():
        g1_copy(3).wait_recv()
        head = gkeep[3, core] + g1recv[3].astype(F32)
        for i in range(3):
            remote(g2recv.at[i], g2recv.at[i], g2_send.at[i], g2_rsem.at[i], (at_x(1 + i), s)).wait_recv()
            head = head + g2recv[i].astype(F32)
        for j in range(8):
            g2sum[j] = head[:, j * LANES:(j + 1) * LANES]
        g3send[...] = g2sum[pl.ds((1 - yh) * 4, 4)].astype(BF16)
        g3.start()

    g3 = remote(g3send, g3recv, g3_send, g3_rsem, (d_far, s))

    def z_pieces():
        g3.wait_recv()
        half_sum = g2sum[pl.ds(yh * 4, 4)] + g3recv[...].astype(F32)
        g4f[...] = half_sum.reshape(Z, 16, LANES)
        g4send[...] = g4f[...].astype(BF16)

        def g4_start(o, carry):
            g4_copy(o).start()
            return carry

        lax.fori_loop(1, Z, g4_start, 0)

    def step(i, carry):
        @pl.when(i < 3)
        def _():
            forward(i + 1)

        @pl.when(i == 0)
        def _():
            own_near(3)
            start_near(3)

        @pl.when(i > 0)
        def _():
            g2_start(i - 1)

        own_q(i).wait()
        take_q(i).wait_recv()
        for n in range(2):
            halo(i, n, True).wait_recv()
        mixed = [ahead(i, yp) for yp in range(2)]
        att_send(i).start()
        attbuf[y * 4 + pair_of(i)] = attpair[i, y]

        @pl.when(i == 0)
        def _():
            grad_out_rows()

        weight_part = dot(mixed[0], gout[0]) + dot(mixed[1], gout[1])
        gkeep[i, 0] = weight_part[:HEAD_DIM]
        gkeep[i, 1] = weight_part[HEAD_DIM:]
        g1send[i] = gkeep[i, 1 - core].astype(BF16)
        g1_copy(i).start()

        @pl.when(i == 0)
        def _():
            projection_rows()

        doc_row = y * 8 + pair_of(i) * 2
        w_pair = wbuf[pl.ds(doc_row, 2)].reshape(2 * HEAD_DIM, WIDTH)
        back(i, 0, w_pair)

        @pl.when(i == 3)
        def _():
            head_sum()

        back(i, 1, w_pair)
        for n in range(2):
            first = 8 * n
            fout[i, n] = acc[first:first + 2].astype(BF16)
            far_copy(i, n).start()
            near[i, n] = acc[2 + 4 * n:4 + 4 * n]
        own[i] = acc[4:6]
        dq_own(i).start()
        dq_pair(i).start()

        @pl.when(i == 3)
        def _():
            z_pieces()

        @pl.when(i > 0)
        def _():
            ret_start(i - 1)

        @pl.when(i > 1)
        def _():
            finish(i - 2)

        return carry

    lax.fori_loop(0, STEPS, step, 0)

    for i in range(STEPS):
        att_take(i).wait_recv()
    rows = jnp.concatenate([attbuf[j] for j in range(8)], axis=1)
    for j in range(4):
        piece = slice(j * 256, (j + 1) * 256)
        lob[:, piece] = dot(rows, wbuf[:, :, piece].reshape(WIDTH, 256)).astype(BF16)
    lo_copy = pltpu.make_async_copy(lob, lo_out, o_sem.at[0, 3])
    lo_copy.start()
    ret_start(3)
    finish(2)

    def g4_wait(o, total):
        g4_copy(o).wait_recv()
        return total + g4recv[o].astype(F32)

    piece_sum = lax.fori_loop(1, Z, g4_wait, g4f[z])
    zag[z] = (piece_sum * (1.0 / math.sqrt(Z * 2 * ROWS * 16))).astype(BF16)

    def g5_copy(o):
        return remote(zag.at[z], zag.at[z], g5_send.at[o], g5_rsem.at[o], (d, at_z(o)))

    def g5_take(o):
        here = zag.at[(z - o + Z) % Z]
        return remote(here, here, g5_send.at[o], g5_rsem.at[o], (d, at_z(o)))

    def g5_start(o, carry):
        g5_copy(o).start()
        return carry

    lax.fori_loop(1, Z, g5_start, 0)
    finish(3)

    def g5_wait(o, carry):
        g5_take(o).wait_recv()
        return carry

    lax.fori_loop(1, Z, g5_wait, 0)
    def g6_copy(n, device):
        return remote(zag, gwh.at[yh], g6_send.at[n], g6_rsem.at[yh], device)

    def g6_take(part):
        return remote(gwh.at[part], gwh.at[part], g6_send.at[0], g6_rsem.at[part], pair_dev)

    @pl.when(yh == y)
    def _():
        g6_copy(0, pair_dev).start()
        gwh[yh] = zag[...]
        g6_take(1 - yh).wait_recv()
        g6_copy(0, pair_dev).wait_send()

    @pl.when(yh != y)
    def _():
        g6_copy(0, far_dev).start()
        g6_copy(1, (d_far, s)).start()
        g6_take(0).wait_recv()
        g6_take(1).wait_recv()
        g6_copy(0, far_dev).wait_send()
        g6_copy(1, (d_far, s)).wait_send()

    for part in range(2):
        for j in range(4):
            lanes = slice((part * 4 + j) * LANES, (part * 4 + j + 1) * LANES)
            gwo[:, lanes] = gwh[part, 4 * j:4 * j + 4].reshape(HEAD_DIM, LANES).astype(F32)
    gw_copy = pltpu.make_async_copy(gwo, gw_out, o_sem.at[1, 3])
    gw_copy.start()

    def drain(i, carry):
        for copy in pair_kv(i):
            copy.wait_send()
        pair_q(i).wait_send()
        for n in range(2):
            near_copy(i, n, 0).wait_send()
            near_copy(i, n, 1).wait_send()
            halo(i, n).wait_send()
            far_copy(i, n).wait_send()
            ret_copy(i, n).wait_send()
        att_send(i).wait_send()
        dq_own(i).wait()
        dq_pair(i).wait_send()
        dq_take(i).wait_recv()
        g1_copy(i).wait_send()
        for copy in fin_own(i):
            copy.wait()
        for copy in fin_pair(i):
            copy.wait_send()
        for copy in fin_take(i):
            copy.wait_recv()
        return carry

    lax.fori_loop(0, STEPS, drain, 0)
    send_ct.wait_send()
    for o in (1, 2, 3):
        remote(w_in, wbuf.at[d], wx_send.at[o - 1], wx_recv.at[o - 1], (at_x(o), s)).wait_send()
        g2_copy(o - 1).wait_send()
    for o in range(4):
        block = w_block(yh, o)
        remote(block, block, wy_send.at[o], wy_recv.at[o], far_dev).wait_send()
        remote(block, block, wc_send.at[o], wc_recv.at[o], core_dev).wait_send()
        block = w_block(1 - yh, o)
        remote(block, block, wc_send.at[4 + o], wc_recv.at[4 + o], core_dev).wait_send()

    g3.wait_send()

    def drain_pieces(o, carry):
        g4_copy(o).wait_send()
        g5_copy(o).wait_send()
        return carry

    lax.fori_loop(1, Z, drain_pieces, 0)
    lo_copy.wait()
    gw_copy.wait()


def copy_kernel(*refs):
    sources, targets, rooms, sems = refs[:5], refs[5:10], refs[10:15], refs[15]
    loads = [pltpu.make_async_copy(sources[n], rooms[n], sems.at[n]) for n in range(5)]
    stores = [pltpu.make_async_copy(rooms[n], targets[n], sems.at[5 + n]) for n in range(5)]
    for load in loads:
        load.start()
    for load, store in zip(loads, stores):
        load.wait()
        store.start()
    for store in stores:
        store.wait()


def body(queries, key_rows, value_rows, cotangent, out_weight, lengths, upweight):
    vm = pltpu.VMEM
    dma = pltpu.SemaphoreType.DMA
    block = (ROWS, LANES)
    any_space = pl.BlockSpec(memory_space=pl.ANY)
    scalar = pl.BlockSpec(memory_space=pltpu.SMEM)
    rows_shape = jax.ShapeDtypeStruct((ROWS, WIDTH), BF16)
    outs = pl.pallas_call(
        layer_kernel,
        out_shape=(rows_shape,) * 4 + (jax.ShapeDtypeStruct((HEAD_DIM, WIDTH), F32),),
        in_specs=[scalar, scalar] + [any_space] * 5,
        out_specs=(any_space,) * 5,
        scratch_shapes=[
            vm((STEPS, 2) + block, BF16),
            vm((STEPS, SLOTS, 2) + block, BF16),
            vm((2, ROWS, WIDTH), BF16),
            vm((2, ROWS, WIDTH), BF16),
            vm((16, HEAD_DIM, WIDTH), BF16),
            vm((2, SPAN) + block, F32),
            vm((8,) + block, BF16),
            vm((STEPS, 2) + block, BF16),
            vm((STEPS, 2) + block, BF16),
            vm((SLOTS, 2) + block, F32),
            vm((STEPS, 2, 2) + block, F32),
            vm((STEPS, 2, 2, 2) + block, BF16),
            vm((STEPS, 2, 2, 2) + block, BF16),
            vm((STEPS, 2, 2, 2) + block, BF16),
            vm((STEPS, 2, 2, 2) + block, BF16),
            vm((STEPS, 2, 2) + block, BF16),
            vm((STEPS, 2, 2, 2) + block, F32),
            vm((STEPS, 2, HEAD_DIM, WIDTH), F32),
            vm((STEPS, HEAD_DIM, WIDTH), BF16),
            vm((STEPS, HEAD_DIM, WIDTH), BF16),
            vm((3, HEAD_DIM, WIDTH), BF16),
            vm((3, HEAD_DIM, WIDTH), BF16),
            vm((8, HEAD_DIM, LANES), F32),
            vm((4, HEAD_DIM, LANES), BF16),
            vm((4, HEAD_DIM, LANES), BF16),
            vm((Z, 16, LANES), F32),
            vm((Z, 16, LANES), BF16),
            vm((Z, 16, LANES), BF16),
            vm((Z, 16, LANES), BF16),
            vm((2, Z, 16, LANES), BF16),
            vm((HEAD_DIM, WIDTH), F32),
            vm((ROWS, WIDTH), BF16),
            vm((2, SPAN * ROWS, 2 * ROWS), F32),
            vm((SPAN * ROWS, 2 * ROWS), F32),
            vm((2, SPAN * ROWS, 2 * ROWS), BF16),
            vm((SPAN * ROWS, 2 * ROWS), BF16),
            dma((STEPS, 4)),
            dma((STEPS, 3)), dma((STEPS, 3)),
            dma, dma,
            dma((STEPS, 2, 2)), dma((STEPS, 2, 2)),
            dma((STEPS, 2)), dma((STEPS, 2)),
            dma((3,)), dma((3,)),
            dma((8,)), dma((8,)),
            dma((4,)), dma((4,)),
            dma((STEPS, 2)), dma((STEPS, 2)),
            dma((STEPS, 2)), dma((STEPS, 2)),
            dma((STEPS,)), dma((STEPS,)),
            dma((STEPS,)), dma((STEPS,)),
            dma((STEPS, 2)), dma((STEPS, 2)),
            dma((STEPS, 4)),
            dma((STEPS,)), dma((STEPS,)),
            dma((3,)), dma((3,)),
            dma, dma,
            dma((Z,)), dma((Z,)),
            dma((Z,)), dma((Z,)),
            dma((2,)), dma((2,)),
        ],
        compiler_params=pltpu.CompilerParams(
            collective_id=0, has_side_effects=True, vmem_limit_bytes=56 * 2**20
        ),
        name="layer",
    )(lengths, upweight, queries[0], key_rows[0], value_rows[0], cotangent[0], out_weight)
    outs = pl.pallas_call(
        copy_kernel,
        out_shape=tuple(jax.ShapeDtypeStruct(a.shape, a.dtype) for a in outs),
        in_specs=[any_space] * 5,
        out_specs=(any_space,) * 5,
        scratch_shapes=[vm(a.shape, a.dtype) for a in outs] + [dma((10,))],
        name="outputs",
    )(*outs)
    layer_out, grad_query, grad_key, grad_value, grad_weight = outs
    return (layer_out[None], grad_query[None], grad_key[None], grad_value[None], grad_weight)


def solution(mesh):
    rows = P("doc", "seq", None)
    flat = P("doc", None)
    return jax.shard_map(
        body,
        mesh=mesh,
        in_specs=(rows, rows, rows, rows, flat, flat, flat),
        out_specs=(rows, rows, rows, rows, flat),
        check_vma=False,
    )
```
